32 devices in a mesh: dp: 16 (over z, x, core), tensor: 2 (over y).
Axes of the slice: x: 2, y: 2, z: 4, core: 2. Of those that a mesh axis runs over, the one named last changes fastest.
Arguments:
- inputs: bfloat16 [16384, 768], P(('dp', 'tensor')), may hold values from -6 to 6
- grad_out: bfloat16 [16384, 768], P(('dp', 'tensor')), may hold values from -6 to 6
- page_lengths: int32 [16, 6], P('dp'), may hold values from 0 to 1024, as said below
- gain_one: bfloat16 [768], replicated, may hold values from 0.5 to 1.5
- gain_two: bfloat16 [768], replicated, may hold values from 0.5 to 1.5
- w_query: bfloat16 [768, 768], P(None, 'tensor'), may hold values from -0.21875 to 0.21875
- w_key: bfloat16 [768, 768], P(None, 'tensor'), may hold values from -0.21875 to 0.21875
- w_value: bfloat16 [768, 768], P(None, 'tensor'), may hold values from -0.21875 to 0.21875
- w_out: bfloat16 [768, 768], P('tensor'), may hold values from -3.5 to 3.5
- w_up: bfloat16 [768, 3072], P(None, 'tensor'), may hold values from -0.21875 to 0.21875
- w_down: bfloat16 [3072, 768], P('tensor'), may hold values from -0.109375 to 0.109375
- rel_table: bfloat16 [12, 16], P('tensor'), may hold values from -4 to 4
Outputs:
- out: bfloat16 [16384, 768], P(('dp', 'tensor'))
- input_grad: bfloat16 [16384, 768], P(('dp', 'tensor'))
- gain_one_grad: float32 [768], replicated
- gain_two_grad: float32 [768], replicated
- query_grad: float32 [768, 768], P(None, 'tensor')
- key_grad: float32 [768, 768], P(None, 'tensor')
- value_grad: float32 [768, 768], P(None, 'tensor')
- out_proj_grad: float32 [768, 768], P('tensor')
- up_grad: float32 [768, 3072], P(None, 'tensor')
- down_grad: float32 [3072, 768], P('tensor')
- table_grad: float32 [12, 16], P('tensor')
The draws below stay inside these ranges and needn't reach their ends.
Inputs may be any that keep to these rules, and one draw needn't show every extreme that they name: `page_lengths`: each row of a group lists pages of one resolution, all of 196, all of 576 or all of 1024 patches, as many as fit in 1024, then one slot with the remaining patches (possibly 0), then zeros; each row sums to 1024, and some group holds pages of 1024.
All inputs are finite; a program needn't handle non-finite values.
Results may differ from the reference program's by a relative error of at most 0.017.
Values may be sent and summed in bfloat16 or wider, within the bound.
No kernel may reach another device: no remote copies, remote signals or barrier semaphores. Data moves between devices by JAX's collectives and lax.ppermute only.
A program may use at most 192 MiB of HBM per device.

```python
import jax
import jax.numpy as jnp
from jax import lax

D = 768
HEADS = 12
HEAD_DIM = 64
FF = 3072
TOK_DEV = 1024
SMALL_PAGE = 196
MID_PAGE = 576
MAXPAGE = 1024
BLOCK = 512
BUCKETS = 16
PAGES = 6
GROUPS = 16
TOKENS = 16384


def draw_page_lengths(key, part):
    class_key = jax.random.fold_in(key, 11)
    pick_key = jax.random.fold_in(key, 23)
    classes = jax.random.randint(class_key, (GROUPS,), 0, 3)
    chosen = jax.random.randint(pick_key, (), 0, GROUPS)
    classes = jnp.where(jnp.arange(GROUPS) == chosen, 2, classes)
    page_size = jnp.where(classes == 0, SMALL_PAGE, jnp.where(classes == 1, MID_PAGE, MAXPAGE)).astype(jnp.int32)
    page_count = TOK_DEV // page_size
    remainder = TOK_DEV - page_count * page_size
    slots = jnp.arange(PAGES, dtype=jnp.int32)[None, :]
    filled = jnp.where(slots < page_count[:, None], page_size[:, None], jnp.where(slots == page_count[:, None], remainder[:, None], 0))
    return filled.astype(jnp.int32)


def block_levels(own_key, extent, pieces, smallest, largest):
    loudness = 1.0
    for dim, blocks in pieces:
        draws = jax.random.uniform(jax.random.fold_in(jax.random.fold_in(own_key, 6), dim), (blocks,), jnp.float32, smallest / len(pieces), largest / len(pieces))
        loudness = loudness * jnp.repeat(jnp.exp(draws), extent[dim] // blocks).reshape((-1,) + (1,) * (len(extent) - 1 - dim))
    return loudness


def bell_draw(key, shape, deviation, most, pieces=(), kind=jnp.bfloat16):
    entries = jax.random.normal(key, shape, jnp.float32) * deviation
    if len(pieces) > 0:
        entries = block_levels(key, shape, pieces, -0.22, 0.18) * entries
    return jnp.clip(entries, min=-most, max=most).astype(kind)


def setup_inputs(seed: int = 0) -> dict:
    key_of = jax.random.split(jax.random.key(seed), 13)
    inputs = bell_draw(key_of[0], (TOKENS, D), 1.0, 6.0, ((0, 32),))
    grad_out = bell_draw(key_of[1], (TOKENS, D), 1.0, 6.0, ((0, 32),))
    page_lengths = draw_page_lengths(jax.random.fold_in(key_of[12], 71), 0)
    gain_one = jnp.clip(1.0 + 0.1 * jax.random.normal(key_of[3], (D,), jnp.float32), 0.5, 1.5).astype(jnp.bfloat16)
    gain_two = jnp.clip(1.0 + 0.1 * jax.random.normal(key_of[4], (D,), jnp.float32), 0.5, 1.5).astype(jnp.bfloat16)
    w_query = bell_draw(key_of[5], (D, D), D ** -0.5, 0.21875, ((1, 2),))
    w_key = bell_draw(key_of[6], (D, D), D ** -0.5, 0.21875, ((1, 2),))
    w_value = bell_draw(key_of[7], (D, D), D ** -0.5, 0.21875, ((1, 2),))
    w_out = bell_draw(key_of[8], (D, D), (max(1, D // 256)) ** -0.5, 3.5, ((0, 2),))
    w_up = bell_draw(key_of[9], (D, FF), D ** -0.5, 0.21875, ((1, 2),))
    w_down = bell_draw(key_of[10], (FF, D), FF ** -0.5, 0.109375, ((0, 2),))
    rel_table = bell_draw(key_of[11], (HEADS, BUCKETS), 1.0, 4.0, ((0, 2),))
    return {"inputs": inputs, "grad_out": grad_out, "page_lengths": page_lengths, "gain_one": gain_one, "gain_two": gain_two, "w_query": w_query, "w_key": w_key, "w_value": w_value, "w_out": w_out, "w_up": w_up, "w_down": w_down, "rel_table": rel_table}


@jax.custom_vjp
def low(v):
    return lax.optimization_barrier(v.astype(jnp.bfloat16)).astype(jnp.float32)

@jax.custom_vjp
def low_back(v):
    return v

def low_keep(v):
    return (low(v), None)

def low_pass(kept, grad):
    return (grad,)

def back_keep(v):
    return (v, None)

def back_low(kept, grad):
    return (low(grad),)
low.defvjp(low_keep, low_pass)
low_back.defvjp(back_keep, back_low)

def layer_norm(values, gain):
    centred = values - lax.optimization_barrier(jnp.mean(values, axis=-1, keepdims=True))
    variance = lax.optimization_barrier(jnp.mean(centred * centred, axis=-1, keepdims=True))
    return centred * lax.rsqrt(variance + 1e-05) * gain

def product(left_side, right_side):
    return jnp.dot(left_side, right_side, precision=lax.Precision.HIGHEST, preferred_element_type=jnp.float32)

def bucket_of(offsets):
    half_count = BUCKETS // 2
    distance = jnp.abs(offsets) + 1
    levels = jnp.zeros_like(offsets)
    for exponent in range(1, half_count):
        levels = levels + (distance >= 2 ** exponent).astype(jnp.int32)
    return levels + half_count * (offsets < 0).astype(jnp.int32)

def pack_forward(tokens, lengths, weights):
    gain_one, gain_two, w_query, w_key, w_value, w_out, w_up, w_down, rel_table = weights
    row_total = tokens.shape[0]
    page_ends = jnp.cumsum(lengths).astype(jnp.int32)
    positions = jnp.arange(row_total, dtype=jnp.int32)
    page_of = lax.optimization_barrier(jnp.sum((positions[:, None] >= page_ends[None, :]).astype(jnp.int32), axis=1))
    normed = low(layer_norm(tokens, gain_one))
    heads_view = (row_total, HEADS, HEAD_DIM)
    query_heads = low(low_back(product(normed, w_query))).reshape(heads_view)
    key_heads = low(low_back(product(normed, w_key))).reshape(heads_view)
    value_heads = low(low_back(product(normed, w_value))).reshape(heads_view)
    score_scale = HEAD_DIM ** (-0.5)

    def attend(first_row):
        query_block = lax.dynamic_slice_in_dim(query_heads, first_row, BLOCK, 0)
        raw_scores = jnp.einsum('qhd,khd->hqk', query_block, key_heads, precision=lax.Precision.HIGHEST) * score_scale
        row_pos = first_row + jnp.arange(BLOCK, dtype=jnp.int32)
        buckets = bucket_of(row_pos[:, None] - positions[None, :])
        scores = low_back(raw_scores) + rel_table[:, buckets]
        same_page = lax.dynamic_slice_in_dim(page_of, first_row, BLOCK, 0)[:, None] == page_of[None, :]
        scores = jnp.where(same_page[None], scores, -1e+30)
        log_total = jax.nn.logsumexp(scores, axis=-1, keepdims=True)
        weight = low(jnp.exp(scores - log_total))
        return jnp.einsum('hqk,khd->qhd', weight, value_heads, precision=lax.Precision.HIGHEST)
    starts = jnp.arange(row_total // BLOCK, dtype=jnp.int32) * BLOCK
    attended = lax.map(jax.checkpoint(attend), starts).reshape(row_total, D)
    attended = low(low_back(attended))
    middle = tokens + low_back(product(attended, w_out))
    normed_two = low(layer_norm(middle, gain_two))
    pre_act = low_back(product(normed_two, w_up))
    hidden = low(jax.nn.gelu(pre_act, approximate=True))
    return middle + low_back(product(hidden, w_down))

def forward(inputs, lengths_all, weights):
    packs = inputs.reshape(GROUPS, TOK_DEV, D)

    def one_pack(pack_pair):
        return pack_forward(pack_pair[0], pack_pair[1], weights)
    return lax.map(jax.checkpoint(one_pack), (packs, lengths_all)).reshape(TOKENS, D)

def reference(inputs, grad_out, page_lengths, gain_one, gain_two, w_query, w_key, w_value, w_out, w_up, w_down, rel_table):
    floats = [array_in.astype(jnp.float32) for array_in in (inputs, gain_one, gain_two, w_query, w_key, w_value, w_out, w_up, w_down, rel_table)]

    def whole_layer(inputs_float, *weights):
        return forward(inputs_float, page_lengths, weights)
    result, pullback = jax.vjp(whole_layer, *floats)
    gradients = pullback(grad_out.astype(jnp.float32))
    return (result.astype(jnp.bfloat16), gradients[0].astype(jnp.bfloat16), gradients[1], gradients[2], gradients[3], gradients[4], gradients[5], gradients[6], gradients[7], gradients[8], gradients[9])
```

```python
import functools
import jax
import jax.numpy as jnp
from jax import lax
from jax.experimental import pallas as pl
from jax.experimental.pallas import tpu as pltpu
from jax.sharding import PartitionSpec as P

HEAD_DIM = 64
BUCKETS = 16
LOG2E = 1.4426950408889634
TILE = 128
QB = 256
MB = 1 << 20


def nt(left, right):
    return lax.dot_general(left, right, (((1,), (1,)), ((), ())), preferred_element_type=jnp.float32)


def nn(left, right):
    return jnp.dot(left, right, preferred_element_type=jnp.float32)


def half_of(block, side):
    lanes = lax.broadcasted_iota(jnp.int32, block.shape, 1)
    keep = (lanes < HEAD_DIM) if side == 0 else (lanes >= HEAD_DIM)
    return jnp.where(keep, block, jnp.zeros_like(block))


def tile_pos(local_tile, tensor_index, tiles):
    return lax.rem(local_tile + (tiles // 2) * tensor_index, tiles)


def bias_rows(strip_ref, side, key_tile, query_tile, tensor_index, tiles):
    pieces = []
    key_pos = tile_pos(key_tile, tensor_index, tiles)
    for step in range(QB // TILE):
        diff = tile_pos(query_tile + step, tensor_index, tiles) - key_pos
        pieces.append(strip_ref[side, jnp.clip(diff, -2, 2) + 2])
    return jnp.concatenate(pieces, axis=1)


def forward_kernel(info_ref, q_ref, k_ref, v_ref, kf_ref, qf_ref, strip_ref, o_ref, lse_ref):
    tensor_index = info_ref[0]
    query_tile = (info_ref[1] + pl.program_id(1)) * (QB // TILE)
    rows = k_ref.shape[0]
    tiles = rows // TILE
    keys = jnp.concatenate([k_ref[...], kf_ref[...]], axis=1)
    value_t = v_ref[...].T
    outs = []
    for side in range(2):
        query = jnp.concatenate([half_of(q_ref[...], side), qf_ref[...]], axis=1)
        raw = nt(keys, query)
        parts = []
        top = None
        for j in range(tiles):
            part = raw[j * TILE : (j + 1) * TILE] * (LOG2E * HEAD_DIM**-0.5) + bias_rows(
                strip_ref, side, j, query_tile, tensor_index, tiles
            )
            parts.append(part)
            top = part if top is None else jnp.maximum(top, part)
        peak = jnp.max(top, axis=0, keepdims=True)
        total = None
        weights = []
        for part in parts:
            weight = jnp.exp2(part - peak)
            total = weight if total is None else total + weight
            weights.append(weight.astype(jnp.bfloat16))
        total = jnp.sum(total, axis=0, keepdims=True)
        out_t = nn(value_t[side * HEAD_DIM : (side + 1) * HEAD_DIM], jnp.concatenate(weights, axis=0))
        outs.append(out_t * (1.0 / total))
        lse_ref[0, side : side + 1, :] = peak + jnp.log2(total)
    o_ref[...] = jnp.concatenate(outs, axis=0).T.astype(jnp.bfloat16)


def attention_forward(info, query, key, value, key_marks, query_marks, strip, blocks):
    rows, width = key.shape
    pairs = width // 128
    grid_spec = pltpu.PrefetchScalarGridSpec(
        num_scalar_prefetch=1,
        grid=(pairs, blocks),
        in_specs=[
            pl.BlockSpec((QB, 128), lambda p, i, s: (s[1] + i, p)),
            pl.BlockSpec((rows, 128), lambda p, i, s: (0, p)),
            pl.BlockSpec((rows, 128), lambda p, i, s: (0, p)),
            pl.BlockSpec((rows, 128), lambda p, i, s: (0, 0)),
            pl.BlockSpec((QB, 128), lambda p, i, s: (s[1] + i, 0)),
            pl.BlockSpec((2, 5, TILE, TILE), lambda p, i, s: (p, 0, 0, 0)),
        ],
        out_specs=[
            pl.BlockSpec((QB, 128), lambda p, i, s: (i, p)),
            pl.BlockSpec((1, 2, QB), lambda p, i, s: (p, 0, i)),
        ],
    )
    return pl.pallas_call(
        forward_kernel,
        grid_spec=grid_spec,
        out_shape=[
            jax.ShapeDtypeStruct((blocks * QB, width), jnp.bfloat16),
            jax.ShapeDtypeStruct((pairs, 2, blocks * QB), jnp.float32),
        ],
        compiler_params=pltpu.CompilerParams(vmem_limit_bytes=40 * MB),
        cost_estimate=pl.CostEstimate(
            flops=4 * 2 * pairs * blocks * QB * rows * 256,
            transcendentals=2 * pairs * blocks * QB * rows,
            bytes_accessed=8 * rows * width,
        ),
        name="attend",
    )(info, query, key, value, key_marks, query_marks, strip)


def band_levels(diff):
    delta = diff * TILE + (
        lax.broadcasted_iota(jnp.int32, (TILE, TILE), 1) - lax.broadcasted_iota(jnp.int32, (TILE, TILE), 0)
    )
    distance = jnp.abs(delta) + 1
    level = jnp.zeros_like(delta)
    for exponent in range(1, BUCKETS // 2):
        level = level + (distance >= 2**exponent).astype(jnp.int32)
    return level + (BUCKETS // 2) * (delta < 0).astype(jnp.int32)


def backward_kernel(
    seeded, info_ref, q_ref, do_ref, o_ref, lse_ref, k_ref, v_ref, kf_ref, qf_ref, strip_ref, *rest
):
    if seeded:
        dk_seed, dv_seed, *rest = rest
    dq_ref, dk_ref, dv_ref, table_ref, grads_ref, near_ref, far_ref = rest
    step = pl.program_id(1)
    tensor_index = info_ref[0]
    query_tile = (info_ref[1] + step) * (QB // TILE)
    rows = k_ref.shape[0]
    tiles = rows // TILE
    scale = HEAD_DIM**-0.5

    @pl.when(step == 0)
    def _():
        near_ref[...] = jnp.zeros_like(near_ref)
        far_ref[...] = jnp.zeros_like(far_ref)

    key_pair = k_ref[...]
    keys = jnp.concatenate([key_pair, kf_ref[...]], axis=1)
    key_t = key_pair.T
    values = v_ref[...]
    inner = (do_ref[...].astype(jnp.float32) * o_ref[...].astype(jnp.float32)).T
    marks = (
        lax.broadcasted_iota(jnp.int32, (16, rows), 1) // TILE
        == lax.broadcasted_iota(jnp.int32, (16, rows), 0)
    ).astype(jnp.bfloat16)
    probs, grads, grad_qs, query_halves, do_halves = [], [], [], [], []
    for side in range(2):
        query_half = half_of(q_ref[...], side)
        do_half = half_of(do_ref[...], side)
        query_halves.append(query_half)
        do_halves.append(do_half)
        raw = nt(keys, jnp.concatenate([query_half, qf_ref[...]], axis=1))
        grad_prob = nt(values, do_half)
        lse = lse_ref[0, side : side + 1, :]
        delta = jnp.sum(inner[side * HEAD_DIM : (side + 1) * HEAD_DIM], axis=0, keepdims=True)
        prob_parts, grad_parts = [], []
        for j in range(tiles):
            span = slice(j * TILE, (j + 1) * TILE)
            bias = bias_rows(strip_ref, side, j, query_tile, tensor_index, tiles)
            prob = jnp.exp2(raw[span] * (LOG2E * scale) + (bias - lse))
            grad = (prob * (grad_prob[span] - delta)).astype(jnp.bfloat16)
            grads_ref[side, span, :] = grad
            prob_parts.append(prob.astype(jnp.bfloat16))
            grad_parts.append(grad)
        probs.append(jnp.concatenate(prob_parts, axis=0))
        grad_all = jnp.concatenate(grad_parts, axis=0)
        grads.append(grad_all)
        left = jnp.concatenate([key_t[side * HEAD_DIM : (side + 1) * HEAD_DIM], marks], axis=0)
        grad_q = nn(left, grad_all)
        grad_qs.append(grad_q[:HEAD_DIM])
        sums = grad_q[HEAD_DIM : HEAD_DIM + 8]
        key_pos = tile_pos(lax.broadcasted_iota(jnp.int32, (8, TILE), 0), tensor_index, tiles)
        for part in range(QB // TILE):
            cols = slice(part * TILE, (part + 1) * TILE)
            query_pos = tile_pos(query_tile + part, tensor_index, tiles)
            piece = sums[:, cols]
            far_ref[side, 0] += jnp.where(key_pos <= query_pos - 2, piece, 0.0)
            far_ref[side, 1] += jnp.where(key_pos >= query_pos + 2, piece, 0.0)
            for diff in (-1, 0, 1):
                wanted = query_pos - diff
                valid = jnp.logical_and(wanted >= 0, wanted < tiles)
                local = tile_pos(jnp.clip(wanted, 0, tiles - 1), tensor_index, tiles)
                block = grads_ref[side, pl.ds(pl.multiple_of(local * TILE, TILE), TILE), cols]
                near_ref[side, diff + 1] += jnp.where(valid, block.astype(jnp.float32), 0.0)
    dv = nn(jnp.concatenate(probs, axis=1), jnp.concatenate(do_halves, axis=0))
    dk = nn(jnp.concatenate(grads, axis=1), jnp.concatenate(query_halves, axis=0)) * scale
    dq_ref[...] = (jnp.concatenate(grad_qs, axis=0).T * scale).astype(jnp.bfloat16)

    @pl.when(step == 0)
    def _():
        dk_ref[...] = dk_seed[...] + dk if seeded else dk
        dv_ref[...] = dv_seed[...] + dv if seeded else dv

    @pl.when(step > 0)
    def _():
        dk_ref[...] += dk
        dv_ref[...] += dv

    @pl.when(step == pl.num_programs(1) - 1)
    def _():
        sums = [[jnp.zeros((1, TILE), jnp.float32) for _ in range(BUCKETS)] for _ in range(2)]
        for side in range(2):
            sums[side][BUCKETS // 2 - 1] += jnp.sum(far_ref[side, 0], axis=0, keepdims=True)
            sums[side][BUCKETS - 1] += jnp.sum(far_ref[side, 1], axis=0, keepdims=True)
        for diff, present in ((0, [*range(8), *range(9, 16)]), (1, range(1, 8)), (-1, range(9, 16))):
            level = band_levels(diff)
            for bucket in present:
                hit = level == bucket
                for side in range(2):
                    sums[side][bucket] += jnp.sum(
                        jnp.where(hit, near_ref[side, diff + 1], 0.0), axis=0, keepdims=True
                    )
        for side in range(2):
            table_ref[0, side] = jnp.concatenate(sums[side], axis=0)


def attention_backward(info, query, grad_out, out, lse, key, value, key_marks, query_marks, strip, seeds, blocks):
    rows, width = key.shape
    pairs = width // 128
    seeded = seeds is not None
    wide = pl.BlockSpec((rows, 128), lambda p, i, s: (0, p))
    shifted = pl.BlockSpec((QB, 128), lambda p, i, s: (s[1] + i, p))
    local = pl.BlockSpec((QB, 128), lambda p, i, s: (i, p))
    grid_spec = pltpu.PrefetchScalarGridSpec(
        num_scalar_prefetch=1,
        grid=(pairs, blocks),
        in_specs=[
            shifted,
            local,
            local,
            pl.BlockSpec((1, 2, QB), lambda p, i, s: (p, 0, i)),
            wide,
            wide,
            pl.BlockSpec((rows, 128), lambda p, i, s: (0, 0)),
            pl.BlockSpec((QB, 128), lambda p, i, s: (s[1] + i, 0)),
            pl.BlockSpec((2, 5, TILE, TILE), lambda p, i, s: (p, 0, 0, 0)),
        ]
        + ([wide, wide] if seeded else []),
        out_specs=[
            local,
            wide,
            wide,
            pl.BlockSpec((1, 2, BUCKETS, TILE), lambda p, i, s: (p, 0, 0, 0)),
        ],
        scratch_shapes=[
            pltpu.VMEM((2, rows, QB), jnp.bfloat16),
            pltpu.VMEM((2, 3, TILE, TILE), jnp.float32),
            pltpu.VMEM((2, 2, 8, TILE), jnp.float32),
        ],
    )
    return pl.pallas_call(
        functools.partial(backward_kernel, seeded),
        grid_spec=grid_spec,
        out_shape=[
            jax.ShapeDtypeStruct((blocks * QB, width), jnp.bfloat16),
            jax.ShapeDtypeStruct((rows, width), jnp.float32),
            jax.ShapeDtypeStruct((rows, width), jnp.float32),
            jax.ShapeDtypeStruct((pairs, 2, BUCKETS, TILE), jnp.float32),
        ],
        compiler_params=pltpu.CompilerParams(vmem_limit_bytes=48 * MB),
        cost_estimate=pl.CostEstimate(
            flops=10 * 2 * pairs * blocks * QB * rows * 256,
            transcendentals=2 * pairs * blocks * QB * rows,
            bytes_accessed=20 * rows * width,
        ),
        name="attend_back",
    )(info, query, grad_out, out, lse, key, value, key_marks, query_marks, strip, *(seeds or ()))


def bias_strip(rel_table):
    table = rel_table.astype(jnp.float32) * LOG2E
    delta = (
        (jnp.arange(5, dtype=jnp.int32) - 2)[:, None, None] * TILE
        + jnp.arange(TILE, dtype=jnp.int32)[None, None, :]
        - jnp.arange(TILE, dtype=jnp.int32)[None, :, None]
    )
    distance = jnp.abs(delta) + 1
    level = jnp.zeros_like(delta)
    for exponent in range(1, BUCKETS // 2):
        level = level + (distance >= 2**exponent).astype(jnp.int32)
    bucket = level + (BUCKETS // 2) * (delta < 0).astype(jnp.int32)
    strip = jnp.zeros((table.shape[0],) + bucket.shape, jnp.float32)
    for b in range(BUCKETS):
        strip = jnp.where(bucket[None] == b, table[:, b][:, None, None, None], strip)
    return strip


def page_marks(lengths, positions):
    ends = jnp.cumsum(lengths)
    page = jnp.sum((positions[:, None] >= ends[None, :]).astype(jnp.int32), axis=1)
    lanes = jnp.arange(128, dtype=jnp.int32)[None, :]
    hit = page[:, None] == lanes
    slots = lanes < lengths.shape[0]
    key_marks = hit.astype(jnp.bfloat16)
    query_marks = jnp.where(jnp.logical_and(slots, jnp.logical_not(hit)), -1e30, 0.0).astype(jnp.bfloat16)
    return key_marks, query_marks


def plain_times(left, right):
    return jnp.dot(left, right, preferred_element_type=jnp.float32)


def transposed_times(left, right):
    return lax.dot_general(left, right, (((0,), (0,)), ((), ())), preferred_element_type=jnp.float32)


def standardize(values):
    centred = values - jnp.mean(values, axis=-1, keepdims=True)
    variance = jnp.mean(centred * centred, axis=-1, keepdims=True)
    inverse = lax.rsqrt(variance + 1e-05)
    return centred * inverse, inverse


def norm_back(grad, standard, inverse, gain):
    scaled = grad * gain
    mean = jnp.mean(scaled, axis=-1, keepdims=True)
    slope = jnp.mean(scaled * standard, axis=-1, keepdims=True)
    return inverse * (scaled - mean - standard * slope), jnp.sum(grad * standard, axis=0)


def swap(values):
    return lax.ppermute(values, "tensor", [(0, 1), (1, 0)])


def dp_swap(values, bit, count):
    return lax.ppermute(values, "dp", [(i, i ^ bit) for i in range(count)])


def reduce_over_dp(part, bits, count):
    index = lax.axis_index("dp")
    place = jnp.int32(0)
    for bit in bits:
        mine = lax.rem(index // bit, 2)
        half = part.shape[0] // 2
        sent = lax.dynamic_slice_in_dim(part, (1 - mine) * half, half, 0)
        kept = lax.dynamic_slice_in_dim(part, mine * half, half, 0)
        part = (kept.astype(jnp.float32) + dp_swap(sent, bit, count).astype(jnp.float32)).astype(jnp.bfloat16)
        place = place * 2 + mine
    done = 1
    for bit in bits:
        done *= 2
    if done < count:
        groups = [[j * done + i for j in range(count // done)] for i in range(done)]
        part = lax.psum(part, "dp", axis_index_groups=groups)
    for bit in reversed(bits):
        part = jnp.concatenate([part, dp_swap(part, bit, count)], axis=0)
    return part, place


def place_blocks(part, place, blocks, outs, maps, picks):
    rows, width = part.shape
    size = rows // blocks

    def kernel(place_ref, part_ref, *out_refs):
        step = pl.program_id(0)
        for out_ref, (low, high) in zip(out_refs, picks):

            @pl.when(jnp.logical_and(step >= low, step < high))
            def _():
                out_ref[...] = part_ref[...].astype(jnp.float32)

    return pl.pallas_call(
        kernel,
        grid_spec=pltpu.PrefetchScalarGridSpec(
            num_scalar_prefetch=1,
            grid=(blocks,),
            in_specs=[pl.BlockSpec((size, width), lambda b, s: (jnp.bitwise_xor(b, s[0]), 0))],
            out_specs=[pl.BlockSpec((size, width), m) for m in maps],
        ),
        out_shape=[jax.ShapeDtypeStruct(o, jnp.float32) for o in outs],
        name="place",
    )(place.reshape(1), part)


def body(
    inputs, grad_out, page_lengths, gain_one, gain_two, w_query, w_key, w_value, w_out, w_up, w_down, rel_table
):
    count = lax.axis_size("dp")
    tensor_index = lax.axis_index("tensor")
    own_rows = inputs.shape[0]
    rows = 2 * own_rows
    width = w_query.shape[1]
    blocks = own_rows // QB
    gain_first = gain_one.astype(jnp.float32)
    gain_second = gain_two.astype(jnp.float32)
    tokens = inputs.astype(jnp.float32)
    standard_one, inverse_one = standardize(tokens)
    normed_own = (standard_one * gain_first).astype(jnp.bfloat16)
    normed = jnp.concatenate([normed_own, swap(normed_own)], axis=0)
    grad_rows = jnp.concatenate([grad_out, swap(grad_out)], axis=0)
    query = plain_times(normed, w_query).astype(jnp.bfloat16)
    key = plain_times(normed, w_key).astype(jnp.bfloat16)
    value = plain_times(normed, w_value).astype(jnp.bfloat16)
    positions = lax.rem(jnp.arange(rows, dtype=jnp.int32) + own_rows * tensor_index, rows)
    key_marks, query_marks = page_marks(page_lengths[0], positions)
    strip = bias_strip(rel_table)
    own_info = jnp.stack([tensor_index, jnp.int32(0)])
    peer_info = jnp.stack([tensor_index, jnp.int32(blocks)])
    shared = (query, key, value, key_marks, query_marks, strip)
    peer_out, peer_lse = attention_forward(peer_info, *shared, blocks)
    peer_branch = swap(plain_times(peer_out, w_out).astype(jnp.bfloat16))
    own_out, own_lse = attention_forward(own_info, *shared, blocks)
    middle = tokens + plain_times(own_out, w_out) + peer_branch.astype(jnp.float32)
    standard_two, inverse_two = standardize(middle)
    normed_two_own = (standard_two * gain_second).astype(jnp.bfloat16)
    normed_two_peer = swap(normed_two_own)

    def feed(normed_rows, grads):
        pre_act = plain_times(normed_rows, w_up)
        inner = 0.7978845608 * (pre_act + 0.044715 * pre_act * pre_act * pre_act)
        bent = jnp.tanh(inner)
        hidden = (0.5 * pre_act * (1.0 + bent)).astype(jnp.bfloat16)
        slope = 0.5 * (1.0 + bent) + 0.5 * pre_act * (1.0 - bent * bent) * 0.7978845608 * (
            1.0 + 3 * 0.044715 * pre_act * pre_act
        )
        grad_pre = (nt(grads, w_down) * slope).astype(jnp.bfloat16)
        return hidden, grad_pre

    own_hidden, own_pre = feed(normed_two_own, grad_out)
    peer_hidden, peer_pre = feed(normed_two_peer, grad_rows[own_rows:])
    grad_two_peer = swap(nt(peer_pre, w_up).astype(jnp.bfloat16))
    grad_two = nt(own_pre, w_up) + grad_two_peer.astype(jnp.float32)
    hidden = jnp.concatenate([own_hidden, peer_hidden], axis=0)
    grad_pre = jnp.concatenate([own_pre, peer_pre], axis=0)
    normed_two = jnp.concatenate([normed_two_own, normed_two_peer], axis=0)
    down_part = transposed_times(hidden, grad_rows).astype(jnp.bfloat16)
    up_part = transposed_times(normed_two, grad_pre).astype(jnp.bfloat16)
    model = up_part.shape[0]
    up_part = jnp.concatenate([up_part[:, :model], up_part[:, model:]], axis=0)
    bits_one = [b for b in (1, 2, 4, 8) if b < count]
    bits_two = [b for b in (1, 4, 8, 2) if b < count]
    down_sum, down_place = reduce_over_dp(down_part, bits_one, count)
    up_sum, up_place = reduce_over_dp(up_part, bits_two, count)
    pieces = 2 ** len(bits_one)
    branch_peer = swap(plain_times(peer_hidden, w_down).astype(jnp.bfloat16))
    out = (middle + plain_times(own_hidden, w_down) + branch_peer.astype(jnp.float32)).astype(jnp.bfloat16)

    grad_middle, gain_two_part = norm_back(grad_two, standard_two, inverse_two, gain_second)
    grad_middle = grad_out.astype(jnp.float32) + grad_middle
    branch_own = grad_middle.astype(jnp.bfloat16)
    branch_peer_grad = swap(branch_own)
    own_grad = nt(branch_own, w_out).astype(jnp.bfloat16)
    grad_q_own, key_sum, value_sum, table_own = attention_backward(
        own_info, query, own_grad, own_out, own_lse, key, value, key_marks, query_marks, strip, None, blocks
    )
    peer_grad = nt(branch_peer_grad, w_out).astype(jnp.bfloat16)
    grad_q_peer, key_sum, value_sum, table_peer = attention_backward(
        peer_info,
        query,
        peer_grad,
        peer_out,
        peer_lse,
        key,
        value,
        key_marks,
        query_marks,
        strip,
        (key_sum, value_sum),
        blocks,
    )
    out_part = transposed_times(own_out, branch_own) + transposed_times(peer_out, branch_peer_grad)
    grad_key = key_sum.astype(jnp.bfloat16)
    grad_value = value_sum.astype(jnp.bfloat16)
    grad_one_peer = (
        nt(grad_q_peer, w_query) + nt(grad_key[own_rows:], w_key) + nt(grad_value[own_rows:], w_value)
    ).astype(jnp.bfloat16)
    grad_one_peer = swap(grad_one_peer)
    grad_one = nt(grad_q_own, w_query) + nt(grad_key[:own_rows], w_key) + nt(grad_value[:own_rows], w_value)
    grad_one = grad_one + grad_one_peer.astype(jnp.float32)
    query_part = transposed_times(normed, jnp.concatenate([grad_q_own, grad_q_peer], axis=0))
    key_part = transposed_times(normed, grad_key)
    value_part = transposed_times(normed, grad_value)
    last = jnp.concatenate(
        [query_part, key_part, value_part, out_part[:, :width], out_part[:, width:]], axis=0
    ).astype(jnp.bfloat16)
    half = last.shape[0] // 2
    first_sum, first_place = reduce_over_dp(last[:half], bits_one, count)
    second_sum, second_place = reduce_over_dp(last[half:], bits_two, count)
    grad_tokens, gain_one_part = norm_back(grad_one, standard_one, inverse_one, gain_first)
    input_grad = (grad_middle + grad_tokens).astype(jnp.bfloat16)

    gains = jnp.stack([gain_one_part, gain_two_part])
    gains = gains + swap(gains)
    table_part = jnp.sum(table_own + table_peer, axis=-1).reshape(rel_table.shape)
    small = jnp.concatenate([gains.reshape(-1), table_part.reshape(-1)])
    for bit in bits_one:
        small = small + dp_swap(small, bit, count)
    if pieces < count:
        groups = [[j * pieces + i for j in range(count // pieces)] for i in range(pieces)]
        small = lax.psum(small, "dp", axis_index_groups=groups)
    gains = small[: 2 * model].reshape(2, model)
    table_total = small[2 * model :].reshape(rel_table.shape)

    ff = w_up.shape[1]
    (down_total,) = place_blocks(
        down_sum, down_place, pieces, [(ff, model)], [lambda b, s: (b, 0)], [(0, pieces)]
    )
    (up_total,) = place_blocks(
        up_sum,
        up_place,
        pieces,
        [(model, ff)],
        [lambda b, s: (lax.rem(b, pieces // 2), b // (pieces // 2))],
        [(0, pieces)],
    )
    fine = pieces // 2
    query_total, key_total = place_blocks(
        first_sum,
        first_place,
        pieces,
        [(model, width), (model, width)],
        [lambda b, s: (jnp.minimum(b, fine - 1), 0), lambda b, s: (jnp.maximum(b - fine, 0), 0)],
        [(0, fine), (fine, pieces)],
    )
    value_total, out_total = place_blocks(
        second_sum,
        second_place,
        pieces,
        [(model, width), (width, model)],
        [
            lambda b, s: (jnp.minimum(b, fine - 1), 0),
            lambda b, s: (lax.rem(jnp.maximum(b - fine, 0), fine // 2), jnp.maximum(b - fine, 0) // (fine // 2)),
        ],
        [(0, fine), (fine, pieces)],
    )
    return (
        out,
        input_grad,
        gains[0],
        gains[1],
        query_total,
        key_total,
        value_total,
        out_total,
        up_total,
        down_total,
        table_total,
    )


def solution(mesh):
    in_specs = (
        P(("dp", "tensor"), None),
        P(("dp", "tensor"), None),
        P("dp", None),
        P(),
        P(),
        P(None, "tensor"),
        P(None, "tensor"),
        P(None, "tensor"),
        P("tensor", None),
        P(None, "tensor"),
        P("tensor", None),
        P("tensor", None),
    )
    out_specs = (
        P(("dp", "tensor"), None),
        P(("dp", "tensor"), None),
        P(),
        P(),
        P(None, "tensor"),
        P(None, "tensor"),
        P(None, "tensor"),
        P("tensor", None),
        P(None, "tensor"),
        P("tensor", None),
        P("tensor", None),
    )
    return jax.shard_map(body, mesh=mesh, in_specs=in_specs, out_specs=out_specs, check_vma=False)
```

```python
import functools
import jax
import jax.numpy as jnp
from jax import lax
from jax.experimental import pallas as pl
from jax.experimental.pallas import tpu as pltpu
from jax.sharding import PartitionSpec as P

HEAD_DIM = 64
BUCKETS = 16
LOG2E = 1.4426950408889634
TILE = 128
QB = 256
MB = 1 << 20


def cost(flops, traffic):
    return pl.CostEstimate(flops=int(flops), transcendentals=0, bytes_accessed=int(traffic))


def nt(left, right):
    return lax.dot_general(left, right, (((1,), (1,)), ((), ())), preferred_element_type=jnp.float32)


def nn(left, right):
    return jnp.dot(left, right, preferred_element_type=jnp.float32)


def half_of(block, side):
    lanes = lax.broadcasted_iota(jnp.int32, block.shape, 1)
    keep = (lanes < HEAD_DIM) if side == 0 else (lanes >= HEAD_DIM)
    return jnp.where(keep, block, jnp.zeros_like(block))


def tile_pos(local_tile, tensor_index, tiles):
    return lax.rem(local_tile + (tiles // 2) * tensor_index, tiles)


def bias_rows(strip_ref, head, key_tile, query_tile, query_tiles, tensor_index, tiles):
    pieces = []
    key_pos = tile_pos(key_tile, tensor_index, tiles)
    for step in range(query_tiles):
        diff = tile_pos(query_tile + step, tensor_index, tiles) - key_pos
        pieces.append(strip_ref[head, jnp.clip(diff, -2, 2) + 2])
    return jnp.concatenate(pieces, axis=1)


def ones_rows(rows):
    return (lax.broadcasted_iota(jnp.int32, (16, rows), 0) == 0).astype(jnp.bfloat16)


def vmem():
    return pl.BlockSpec(memory_space=pltpu.VMEM)


def smem():
    return pl.BlockSpec(memory_space=pltpu.SMEM)


def rows_of(refs):
    return jnp.concatenate([ref[...] for ref in refs], axis=0) if len(refs) > 1 else refs[0][...]


def attention_forward(info, start, count, peer, query, keys, values, key_marks, query_marks, strip, w_out, part_type):
    own_rows, width = query.shape
    rows = key_marks.shape[0]
    model = w_out.shape[1]
    pairs = width // 128
    tiles = rows // TILE
    query_tiles = count // TILE
    base = (own_rows if peer else 0) + start
    first = base // TILE

    def kernel(info_ref, q_ref, ko_ref, kp_ref, vo_ref, vp_ref, kf_ref, qf_ref, strip_ref, w_ref, o_ref, lse_ref, part_ref):
        tensor_index = info_ref[0]
        marks = qf_ref[base : base + count, :]
        for pair in range(pairs):
            lanes = slice(pair * 128, (pair + 1) * 128)
            keys = jnp.concatenate(
                [jnp.concatenate([ko_ref[:, lanes], kp_ref[:, lanes]], axis=0), kf_ref[...]], axis=1
            )
            value_t = jnp.concatenate([vo_ref[:, lanes].T, vp_ref[:, lanes].T], axis=1)
            outs = []
            for side in range(2):
                query_half = half_of(q_ref[start : start + count, lanes], side)
                raw = nt(keys, jnp.concatenate([query_half, marks], axis=1))
                parts = []
                top = None
                for j in range(tiles):
                    part = raw[j * TILE : (j + 1) * TILE] * (LOG2E * HEAD_DIM**-0.5) + bias_rows(
                        strip_ref, 2 * pair + side, j, first, query_tiles, tensor_index, tiles
                    )
                    parts.append(part)
                    top = part if top is None else jnp.maximum(top, part)
                peak = jnp.max(top, axis=0, keepdims=True)
                weights = jnp.concatenate([jnp.exp2(part - peak).astype(jnp.bfloat16) for part in parts], axis=0)
                left = jnp.concatenate([value_t[side * HEAD_DIM : (side + 1) * HEAD_DIM], ones_rows(rows)], axis=0)
                out_t = nn(left, weights)
                total = out_t[HEAD_DIM : HEAD_DIM + 1]
                outs.append(out_t[:HEAD_DIM] * (1.0 / total))
                lse_ref[pair, side : side + 1, :] = peak + jnp.log2(total)
            o_ref[:, lanes] = jnp.concatenate(outs, axis=0).T.astype(jnp.bfloat16)
        part_ref[...] = nn(o_ref[...], w_ref[...]).astype(part_type)

    return pl.pallas_call(
        kernel,
        in_specs=[smem()] + [vmem()] * 9,
        out_specs=[vmem()] * 3,
        out_shape=[
            jax.ShapeDtypeStruct((count, width), jnp.bfloat16),
            jax.ShapeDtypeStruct((pairs, 2, count), jnp.float32),
            jax.ShapeDtypeStruct((count, model), part_type),
        ],
        compiler_params=pltpu.CompilerParams(vmem_limit_bytes=8 * MB),
        cost_estimate=cost(9 * 10**9 * count // own_rows, 8 * rows * width),
        name="attend",
    )(info, query, *keys, *values, key_marks, query_marks, strip, w_out)


def attention_backward(
    info, start, peer, query, grad_out, out, lse, keys, values, key_marks, query_marks, strip, seeds, sum_type
):
    own_rows, width = query.shape
    count = grad_out.shape[0]
    rows = key_marks.shape[0]
    pairs = width // 128
    tiles = rows // TILE
    query_tiles = count // TILE
    base = (own_rows if peer else 0) + start
    first = base // TILE
    shift = start if out.shape[0] > count else 0
    seeded = seeds is not None
    scale = HEAD_DIM**-0.5

    def kernel(info_ref, q_ref, do_ref, o_ref, lse_ref, ko_ref, kp_ref, vo_ref, vp_ref, kf_ref, qf_ref, strip_ref, *rest):
        if seeded:
            dk_seed, dv_seed, *rest = rest
        dq_ref, dk_ref, dv_ref, near_ref, far_ref, grads_ref = rest
        tensor_index = info_ref[0]
        query_marks = qf_ref[base : base + count, :]
        marks = (
            lax.broadcasted_iota(jnp.int32, (16, rows), 1) // TILE
            == lax.broadcasted_iota(jnp.int32, (16, rows), 0)
        ).astype(jnp.bfloat16)
        key_pos = tile_pos(lax.broadcasted_iota(jnp.int32, (8, TILE), 0), tensor_index, tiles)
        for pair in range(pairs):
            lanes = slice(pair * 128, (pair + 1) * 128)
            key_pair = jnp.concatenate([ko_ref[:, lanes], kp_ref[:, lanes]], axis=0)
            keys = jnp.concatenate([key_pair, kf_ref[...]], axis=1)
            key_t = key_pair.T
            values = jnp.concatenate([vo_ref[:, lanes], vp_ref[:, lanes]], axis=0)
            inner = do_ref[:, lanes].astype(jnp.float32) * o_ref[shift : shift + count, lanes].astype(jnp.float32)
            inner = inner.T
            probs, grads, grad_qs, query_halves, do_halves = [], [], [], [], []
            for side in range(2):
                head = 2 * pair + side
                query_half = half_of(q_ref[start : start + count, lanes], side)
                do_half = half_of(do_ref[:, lanes], side)
                query_halves.append(query_half)
                do_halves.append(do_half)
                raw = nt(keys, jnp.concatenate([query_half, query_marks], axis=1))
                grad_prob = nt(values, do_half)
                lse = lse_ref[pair, side : side + 1, shift : shift + count]
                delta = jnp.sum(inner[side * HEAD_DIM : (side + 1) * HEAD_DIM], axis=0, keepdims=True)
                prob_parts, grad_parts = [], []
                for j in range(tiles):
                    span = slice(j * TILE, (j + 1) * TILE)
                    bias = bias_rows(strip_ref, head, j, first, query_tiles, tensor_index, tiles)
                    prob = jnp.exp2(raw[span] * (LOG2E * scale) + (bias - lse))
                    grad = (prob * (grad_prob[span] - delta)).astype(jnp.bfloat16)
                    grads_ref[side, span, :] = grad
                    prob_parts.append(prob.astype(jnp.bfloat16))
                    grad_parts.append(grad)
                probs.append(jnp.concatenate(prob_parts, axis=0))
                grad_all = jnp.concatenate(grad_parts, axis=0)
                grads.append(grad_all)
                left = jnp.concatenate([key_t[side * HEAD_DIM : (side + 1) * HEAD_DIM], marks], axis=0)
                grad_q = nn(left, grad_all)
                grad_qs.append(grad_q[:HEAD_DIM])
                sums = grad_q[HEAD_DIM : HEAD_DIM + 8]
                before, after = jnp.zeros((8, TILE), jnp.float32), jnp.zeros((8, TILE), jnp.float32)
                for part in range(query_tiles):
                    query_pos = tile_pos(first + part, tensor_index, tiles)
                    piece = sums[:, part * TILE : (part + 1) * TILE]
                    before = before + jnp.where(key_pos <= query_pos - 2, piece, 0.0)
                    after = after + jnp.where(key_pos >= query_pos + 2, piece, 0.0)
                far_ref[head, 0] = before
                far_ref[head, 1] = after
                for diff in (-1, 0, 1):
                    near = None
                    for part in range(query_tiles):
                        wanted = tile_pos(first + part, tensor_index, tiles) - diff
                        valid = jnp.logical_and(wanted >= 0, wanted < tiles)
                        local = tile_pos(jnp.clip(wanted, 0, tiles - 1), tensor_index, tiles)
                        block = grads_ref[
                            side,
                            pl.ds(pl.multiple_of(local * TILE, TILE), TILE),
                            part * TILE : (part + 1) * TILE,
                        ].astype(jnp.float32)
                        block = block if diff == 0 else jnp.where(valid, block, 0.0)
                        near = block if near is None else near + block
                    near_ref[head, diff + 1] = near
            dv = nn(jnp.concatenate(probs, axis=1), jnp.concatenate(do_halves, axis=0))
            dk = nn(jnp.concatenate(grads, axis=1), jnp.concatenate(query_halves, axis=0)) * scale
            if seeded:
                dv = dv + dv_seed[:, lanes]
                dk = dk + dk_seed[:, lanes]
            dv_ref[:, lanes] = dv.astype(sum_type)
            dk_ref[:, lanes] = dk.astype(sum_type)
            dq_ref[:, lanes] = (jnp.concatenate(grad_qs, axis=0).T * scale).astype(jnp.bfloat16)

    return pl.pallas_call(
        kernel,
        in_specs=[smem()] + [vmem()] * (13 if seeded else 11),
        out_specs=[vmem()] * 5,
        out_shape=[
            jax.ShapeDtypeStruct((count, width), jnp.bfloat16),
            jax.ShapeDtypeStruct((rows, width), sum_type),
            jax.ShapeDtypeStruct((rows, width), sum_type),
            jax.ShapeDtypeStruct((2 * pairs, 3, TILE, TILE), jnp.float32),
            jax.ShapeDtypeStruct((2 * pairs, 2, 8, TILE), jnp.float32),
        ],
        scratch_shapes=[pltpu.VMEM((2, rows, count), jnp.bfloat16)],
        compiler_params=pltpu.CompilerParams(vmem_limit_bytes=14 * MB),
        cost_estimate=cost(18 * 10**9 * count // own_rows, 20 * rows * width),
        name="attend_back",
    )(info, query, grad_out, out, lse, *keys, *values, key_marks, query_marks, strip, *(seeds or ()))


def band_levels(diff):
    delta = diff * TILE + (
        lax.broadcasted_iota(jnp.int32, (TILE, TILE), 1) - lax.broadcasted_iota(jnp.int32, (TILE, TILE), 0)
    )
    distance = jnp.abs(delta) + 1
    level = jnp.zeros_like(delta)
    for exponent in range(1, BUCKETS // 2):
        level = level + (distance >= 2**exponent).astype(jnp.int32)
    return level + (BUCKETS // 2) * (delta < 0).astype(jnp.int32)


def band_sums(nears, fars):
    heads = nears[0].shape[0]
    calls = len(nears)

    def kernel(*refs):
        near_refs, far_refs, o_ref = refs[:calls], refs[calls : 2 * calls], refs[-1]
        rows = [[jnp.zeros((1, TILE), jnp.float32) for _ in range(BUCKETS)] for _ in range(heads)]
        for head in range(heads):
            far = sum(ref[head] for ref in far_refs)
            rows[head][BUCKETS // 2 - 1] += jnp.sum(far[0], axis=0, keepdims=True)
            rows[head][BUCKETS - 1] += jnp.sum(far[1], axis=0, keepdims=True)
        for diff, present in ((0, [*range(8), *range(9, 16)]), (1, range(1, 8)), (-1, range(9, 16))):
            level = band_levels(diff)
            for head in range(heads):
                near = sum(ref[head, diff + 1] for ref in near_refs)
                for bucket in present:
                    rows[head][bucket] += jnp.sum(jnp.where(level == bucket, near, 0.0), axis=0, keepdims=True)
        at = lax.broadcasted_iota(jnp.int32, (BUCKETS, TILE), 0) == lax.broadcasted_iota(
            jnp.int32, (BUCKETS, TILE), 1
        )
        o_ref[...] = jnp.zeros_like(o_ref)
        for head in range(heads):
            sums = jnp.sum(jnp.concatenate(rows[head], axis=0), axis=1, keepdims=True)
            o_ref[head : head + 1, :] = jnp.sum(jnp.where(at, sums, 0.0), axis=0, keepdims=True)

    return pl.pallas_call(
        kernel,
        in_specs=[vmem()] * (2 * calls),
        out_specs=vmem(),
        out_shape=jax.ShapeDtypeStruct((8, TILE), jnp.float32),
        compiler_params=pltpu.CompilerParams(vmem_limit_bytes=8 * MB),
        cost_estimate=cost(heads * 3 * 16 * TILE * TILE, heads * 8 * TILE * TILE),
        name="band_sums",
    )(*nears, *fars)


def pack_small(gain_one_part, gain_two_parts, table, heads):
    model = gain_one_part.shape[1]
    calls = len(gain_two_parts)

    def kernel(*refs):
        one_ref, table_ref, o_ref = refs[0], refs[calls + 1], refs[calls + 2]
        o_ref[...] = jnp.zeros_like(o_ref)
        o_ref[0:1, :] = jnp.sum(one_ref[...], axis=0, keepdims=True)
        two = sum(ref[...] for ref in refs[1 : calls + 1])
        o_ref[1:2, :] = jnp.sum(two, axis=0, keepdims=True)
        o_ref[2 : 2 + heads, :TILE] = table_ref[:heads, :]

    return pl.pallas_call(
        kernel,
        in_specs=[vmem()] * (calls + 2),
        out_specs=vmem(),
        out_shape=jax.ShapeDtypeStruct((8, model), jnp.float32),
        compiler_params=pltpu.CompilerParams(vmem_limit_bytes=2 * MB),
        cost_estimate=cost(1000, 1000),
        name="pack_small",
    )(gain_one_part, *gain_two_parts, table)


def add_small(mine, theirs, rows):
    def kernel(a_ref, b_ref, o_ref):
        line = lax.broadcasted_iota(jnp.int32, a_ref.shape, 0)
        o_ref[...] = a_ref[...] + jnp.where(line < rows, b_ref[...], 0.0)

    return pl.pallas_call(
        kernel,
        in_specs=[vmem()] * 2,
        out_specs=vmem(),
        out_shape=jax.ShapeDtypeStruct(mine.shape, jnp.float32),
        compiler_params=pltpu.CompilerParams(vmem_limit_bytes=2 * MB),
        cost_estimate=cost(1000, 1000),
        name="add_small",
    )(mine, theirs)


def bias_strip(rel_table):
    heads = rel_table.shape[0]

    def kernel(t_ref, o_ref):
        table = t_ref[...].astype(jnp.float32) * LOG2E
        levels = [band_levels(diff) for diff in (-1, 0, 1)]
        masks = [[level == bucket for bucket in range(BUCKETS)] for level in levels]
        for head in range(heads):
            entries = [table[head : head + 1, bucket : bucket + 1] for bucket in range(BUCKETS)]
            for slot, present in enumerate((range(9, 16), [*range(8), *range(9, 16)], range(1, 8))):
                tile = jnp.zeros((TILE, TILE), jnp.float32)
                for bucket in present:
                    tile = jnp.where(masks[slot][bucket], entries[bucket], tile)
                o_ref[head, slot + 1] = tile
            o_ref[head, 0] = jnp.broadcast_to(entries[15], (TILE, TILE))
            o_ref[head, 4] = jnp.broadcast_to(entries[7], (TILE, TILE))

    return pl.pallas_call(
        kernel,
        in_specs=[vmem()],
        out_specs=vmem(),
        out_shape=jax.ShapeDtypeStruct((heads, 5, TILE, TILE), jnp.float32),
        compiler_params=pltpu.CompilerParams(vmem_limit_bytes=8 * MB),
        cost_estimate=cost(heads * 3 * 16 * TILE * TILE, heads * 20 * TILE * TILE),
        name="bias_strip",
    )(rel_table)


def page_marks(lengths, rows, tensor_index):
    slots = lengths.shape[0]

    def kernel(len_ref, t_ref, k_ref, q_ref):
        place = lax.broadcasted_iota(jnp.int32, (rows, 128), 0) + (rows // 2) * t_ref[0]
        place = jnp.where(place >= rows, place - rows, place)
        lanes = lax.broadcasted_iota(jnp.int32, (rows, 128), 1)
        end = jnp.int32(0)
        page = jnp.zeros((rows, 128), jnp.int32)
        for slot in range(slots):
            end = end + len_ref[slot]
            page = page + (place >= end).astype(jnp.int32)
        k_ref[...] = jnp.where(page == lanes, 1.0, 0.0).astype(jnp.bfloat16)
        other = jnp.logical_and(page != lanes, lanes < slots)
        q_ref[...] = jnp.where(other, -1e30, 0.0).astype(jnp.bfloat16)

    return pl.pallas_call(
        kernel,
        in_specs=[smem(), smem()],
        out_specs=[vmem()] * 2,
        out_shape=[jax.ShapeDtypeStruct((rows, 128), jnp.bfloat16)] * 2,
        compiler_params=pltpu.CompilerParams(vmem_limit_bytes=8 * MB),
        cost_estimate=cost(rows * 128 * 16, rows * 512),
        name="page_marks",
    )(lengths, tensor_index)


def tn(left, right):
    return lax.dot_general(left, right, (((0,), (0,)), ((), ())), preferred_element_type=jnp.float32)


def standardize(values):
    centred = values - jnp.mean(values, axis=-1, keepdims=True)
    variance = jnp.mean(centred * centred, axis=-1, keepdims=True)
    inverse = lax.rsqrt(variance + 1e-05)
    return centred * inverse, inverse


def norm_back(grad, standard, inverse, gain):
    scaled = grad * gain
    mean = jnp.mean(scaled, axis=-1, keepdims=True)
    slope = jnp.mean(scaled * standard, axis=-1, keepdims=True)
    return inverse * (scaled - mean - standard * slope)


def fold_rows(values):
    return jnp.sum(values.reshape(-1, 8, values.shape[-1]), axis=0)


def first_norm(inputs, gain):
    rows, model = inputs.shape

    def kernel(x_ref, g_ref, o_ref):
        gain = g_ref[...].astype(jnp.float32)
        for start in range(0, rows, 128):
            standard, _ = standardize(x_ref[start : start + 128, :].astype(jnp.float32))
            o_ref[start : start + 128, :] = (standard * gain).astype(jnp.bfloat16)

    return pl.pallas_call(
        kernel,
        in_specs=[vmem()] * 2,
        out_specs=vmem(),
        out_shape=jax.ShapeDtypeStruct((rows, model), jnp.bfloat16),
        compiler_params=pltpu.CompilerParams(vmem_limit_bytes=6 * MB),
        cost_estimate=cost(rows * model * 8, 4 * rows * model),
        name="first_norm",
    )(inputs, gain)


def project(normed, weights):
    rows, model = normed.shape
    width = weights[0].shape[1]

    def kernel(x_ref, *refs):
        for w_ref, o_ref in zip(refs[:3], refs[3:]):
            o_ref[...] = nn(x_ref[...], w_ref[...]).astype(jnp.bfloat16)

    return pl.pallas_call(
        kernel,
        in_specs=[vmem()] * 4,
        out_specs=[vmem()] * 3,
        out_shape=[jax.ShapeDtypeStruct((rows, width), jnp.bfloat16)] * 3,
        compiler_params=pltpu.CompilerParams(vmem_limit_bytes=4 * MB),
        cost_estimate=cost(6 * rows * model * width, 2 * 3 * model * width + 4 * rows * model),
        name="project",
    )(normed, *weights)


def second_norm(start, inputs, own_part, peer_part, gain):
    rows, model = peer_part.shape

    def kernel(x_ref, a_ref, b_ref, g_ref, m_ref, o_ref):
        gain = g_ref[...].astype(jnp.float32)
        for offset in range(0, rows, 128):
            span = slice(offset, offset + 128)
            wide = slice(start + offset, start + offset + 128)
            middle = x_ref[wide, :].astype(jnp.float32) + a_ref[wide, :] + b_ref[span, :].astype(jnp.float32)
            m_ref[span, :] = middle
            standard, _ = standardize(middle)
            o_ref[span, :] = (standard * gain).astype(jnp.bfloat16)

    return pl.pallas_call(
        kernel,
        in_specs=[vmem()] * 4,
        out_specs=[vmem()] * 2,
        out_shape=[
            jax.ShapeDtypeStruct((rows, model), jnp.float32),
            jax.ShapeDtypeStruct((rows, model), jnp.bfloat16),
        ],
        compiler_params=pltpu.CompilerParams(vmem_limit_bytes=8 * MB),
        cost_estimate=cost(rows * model * 8, 14 * rows * model),
        name="second_norm",
    )(inputs, own_part, peer_part, gain)


FF_CHUNK = 512


def feed(normeds, start, grads, w_up, w_down, sum_type):
    rows = sum(n.shape[0] for n in normeds)
    model, ff = w_up.shape
    calls = len(normeds)

    def kernel(*refs):
        g_ref, u_ref, d_ref, h_ref, p_ref, gn_ref, bt_ref = refs[calls:]
        normed = rows_of(refs[:calls])
        for begin in range(0, ff, FF_CHUNK):
            span = slice(begin, begin + FF_CHUNK)
            pre = nn(normed, u_ref[:, span])
            grad_hidden = nt(g_ref[start : start + rows, :], d_ref[span, :])
            square = pre * pre
            bent = jnp.tanh(pre * (0.7978845608 + (0.7978845608 * 0.044715) * square))
            gate = 0.5 + 0.5 * bent
            h_ref[:, span] = (pre * gate).astype(jnp.bfloat16)
            slope = gate + pre * (0.5 - 0.5 * bent * bent) * (
                0.7978845608 + (3 * 0.7978845608 * 0.044715) * square
            )
            p_ref[:, span] = (grad_hidden * slope).astype(jnp.bfloat16)
        gn_ref[...] = nt(p_ref[...], u_ref[...]).astype(sum_type)
        bt_ref[...] = nn(h_ref[...], d_ref[...]).astype(sum_type)

    return pl.pallas_call(
        kernel,
        in_specs=[vmem()] * (calls + 3),
        out_specs=[vmem()] * 4,
        out_shape=[jax.ShapeDtypeStruct((rows, ff), jnp.bfloat16)] * 2
        + [jax.ShapeDtypeStruct((rows, model), sum_type)] * 2,
        compiler_params=pltpu.CompilerParams(vmem_limit_bytes=8 * MB),
        cost_estimate=cost(8 * rows * model * ff, 4 * model * ff + 8 * rows * ff),
        name="feed",
    )(*normeds, grads, w_up, w_down)


def grouped_call(kernel, groups, **options):
    sizes = [len(g) for g in groups]

    def body(place_ref, *refs):
        lists, at = [], 0
        for size in sizes:
            lists.append(refs[at : at + size])
            at += size
        kernel(place_ref, *lists, *refs[at:])

    return pl.pallas_call(body, in_specs=[smem()] + [vmem()] * sum(sizes), **options)


def turned(refs, span=slice(None)):
    return jnp.concatenate([ref[:, span].T for ref in refs], axis=1)


def feed_grads(places, pieces, hiddens, grad_pres, normeds, grads):
    rows = sum(h.shape[0] for h in hiddens)
    ff = hiddens[0].shape[1]
    model = normeds[0].shape[1]
    size = ff // pieces
    fine = model // size

    def kernel(place_ref, h_refs, p_refs, n_refs, g_refs, down_ref, up_ref):
        grad = rows_of(g_refs)
        normed_t = turned(n_refs)
        for part in range(ff // model):
            span = slice(part * model, (part + 1) * model)
            down = nn(turned(h_refs, span), grad).astype(jnp.bfloat16)
            for k in range(fine):
                store_piece(down_ref, place_ref[0], pieces, part * fine + k, size, down[k * size : (k + 1) * size])
        for part in range(ff // model):
            span = slice(part * model, (part + 1) * model)
            pre = jnp.concatenate([ref[:, span] for ref in p_refs], axis=0)
            up = nn(normed_t, pre).astype(jnp.bfloat16)
            for k in range(fine):
                store_piece(up_ref, place_ref[1], pieces, part * fine + k, size, up[k * size : (k + 1) * size])

    groups = (hiddens, grad_pres, normeds, grads)
    return grouped_call(
        kernel,
        groups,
        out_specs=[vmem()] * 2,
        out_shape=[jax.ShapeDtypeStruct((2, ff // 2, model), jnp.bfloat16)] * 2,
        compiler_params=pltpu.CompilerParams(vmem_limit_bytes=11 * MB),
        cost_estimate=cost(4 * rows * model * ff, 4 * rows * ff + 4 * ff * model),
        name="feed_grads",
    )(places, *[a for g in groups for a in g])


def second_norm_back(start, own_part, peer_part, middle, grad_out, gain, w_out):
    rows, model = middle.shape
    width = w_out.shape[0]

    def kernel(a_ref, b_ref, m_ref, g_ref, gain_ref, w_ref, gm_ref, gb_ref, ga_ref, gain_out):
        gain = gain_ref[...].astype(jnp.float32)
        part = jnp.zeros((8, model), jnp.float32)
        for offset in range(0, rows, 128):
            span = slice(offset, offset + 128)
            wide = slice(start + offset, start + offset + 128)
            grad = a_ref[wide, :] + b_ref[span, :].astype(jnp.float32)
            standard, inverse = standardize(m_ref[span, :])
            result = g_ref[wide, :].astype(jnp.float32) + norm_back(grad, standard, inverse, gain)
            gm_ref[span, :] = result
            gb_ref[span, :] = result.astype(jnp.bfloat16)
            part = part + fold_rows(grad * standard)
        gain_out[...] = part
        ga_ref[...] = nt(gb_ref[...], w_ref[...]).astype(jnp.bfloat16)

    return pl.pallas_call(
        kernel,
        in_specs=[vmem()] * 6,
        out_specs=[vmem()] * 4,
        out_shape=[
            jax.ShapeDtypeStruct((rows, model), jnp.float32),
            jax.ShapeDtypeStruct((rows, model), jnp.bfloat16),
            jax.ShapeDtypeStruct((rows, width), jnp.bfloat16),
            jax.ShapeDtypeStruct((8, model), jnp.float32),
        ],
        compiler_params=pltpu.CompilerParams(vmem_limit_bytes=10 * MB),
        cost_estimate=cost(2 * rows * model * width, 18 * rows * model),
        name="second_norm_back",
    )(own_part, peer_part, middle, grad_out, gain, w_out)


def normed_grad(grad_qs, grad_k, grad_v, offset, weights):
    rows = sum(q.shape[0] for q in grad_qs)
    model, width = weights[0].shape
    calls = len(grad_qs)

    def kernel(*refs):
        k_ref, v_ref, wq_ref, wk_ref, wv_ref, o_ref = refs[calls:]
        span = slice(offset, offset + rows)
        total = nt(rows_of(refs[:calls]), wq_ref[...])
        total = total + nt(k_ref[span, :], wk_ref[...]) + nt(v_ref[span, :], wv_ref[...])
        o_ref[...] = total.astype(jnp.bfloat16)

    return pl.pallas_call(
        kernel,
        in_specs=[vmem()] * (calls + 5),
        out_specs=vmem(),
        out_shape=jax.ShapeDtypeStruct((rows, model), jnp.bfloat16),
        compiler_params=pltpu.CompilerParams(vmem_limit_bytes=6 * MB),
        cost_estimate=cost(6 * rows * model * width, 6 * rows * width + 6 * model * width),
        name="normed_grad",
    )(*grad_qs, grad_k, grad_v, *weights)


def first_norm_back(grad_qs, grad_k, grad_v, weights, peer_part, inputs, middles, gain):
    rows, model = inputs.shape
    width = weights[0].shape[1]
    calls = len(grad_qs)
    size = rows // calls

    def kernel(*refs):
        q_refs, m_refs = refs[:calls], refs[calls : 2 * calls]
        k_ref, v_ref, wq_ref, wk_ref, wv_ref, b_ref, x_ref, gain_ref, o_ref, gain_out = refs[2 * calls :]
        gain = gain_ref[...].astype(jnp.float32)
        part = jnp.zeros((8, model), jnp.float32)
        for call in range(calls):
            span = slice(call * size, (call + 1) * size)
            grad = nt(q_refs[call][...], wq_ref[...])
            grad = grad + nt(k_ref[span, :], wk_ref[...]) + nt(v_ref[span, :], wv_ref[...])
            grad = grad + b_ref[span, :].astype(jnp.float32)
            standard, inverse = standardize(x_ref[span, :].astype(jnp.float32))
            result = m_refs[call][...] + norm_back(grad, standard, inverse, gain)
            o_ref[span, :] = result.astype(jnp.bfloat16)
            part = part + fold_rows(grad * standard)
        gain_out[...] = part

    return pl.pallas_call(
        kernel,
        in_specs=[vmem()] * (2 * calls + 8),
        out_specs=[vmem()] * 2,
        out_shape=[
            jax.ShapeDtypeStruct((rows, model), jnp.bfloat16),
            jax.ShapeDtypeStruct((8, model), jnp.float32),
        ],
        compiler_params=pltpu.CompilerParams(vmem_limit_bytes=10 * MB),
        cost_estimate=cost(6 * rows * model * width, 12 * rows * model),
        name="first_norm_back",
    )(*grad_qs, *middles, grad_k, grad_v, *weights, peer_part, inputs, gain)


def store_piece(ref, place, pieces, block, size, values):
    half = pieces // 2
    spot = jnp.bitwise_xor(place, block)
    ref[spot // half, pl.ds(pl.multiple_of(lax.rem(spot, half) * size, size), size), :] = values


def attention_grads(places, pieces, normeds, grad_qs, grad_k, grad_v, outs, branches):
    rows, width = grad_k.shape
    model = normeds[0].shape[1]
    size = 2 * model // pieces
    fine = model // size

    def kernel(place_ref, n_refs, q_refs, k_refs, v_refs, o_refs, b_refs, first_ref, second_ref):
        normed_t = turned(n_refs)
        for ref, which, base, right in (
            (first_ref, 0, 0, rows_of(q_refs)),
            (first_ref, 0, fine, rows_of(k_refs)),
            (second_ref, 1, 0, rows_of(v_refs)),
        ):
            result = nn(normed_t, right).astype(jnp.bfloat16)
            for k in range(fine):
                store_piece(ref, place_ref[which], pieces, base + k, size, result[k * size : (k + 1) * size])
        result = nn(turned(o_refs), rows_of(b_refs)).astype(jnp.bfloat16)
        for side in range(2):
            for k in range(fine // 2):
                store_piece(
                    second_ref,
                    place_ref[1],
                    pieces,
                    fine + side * (fine // 2) + k,
                    size,
                    result[k * size : (k + 1) * size, side * width : (side + 1) * width],
                )

    groups = (normeds, grad_qs, (grad_k,), (grad_v,), outs, branches)
    return grouped_call(
        kernel,
        groups,
        out_specs=[vmem()] * 2,
        out_shape=[jax.ShapeDtypeStruct((2, model, width), jnp.bfloat16)] * 2,
        compiler_params=pltpu.CompilerParams(vmem_limit_bytes=9 * MB),
        cost_estimate=cost(8 * rows * model * width, 6 * rows * model),
        name="attention_grads",
    )(places, *[a for g in groups for a in g])


def swap(values):
    return lax.ppermute(values, "tensor", [(0, 1), (1, 0)])


def dp_swap(values, bit, count):
    return lax.ppermute(values, "dp", [(i, i ^ bit) for i in range(count)])


def place_of(bits):
    index = lax.axis_index("dp")
    place = jnp.int32(0)
    for bit in bits:
        place = place * 2 + lax.rem(index // bit, 2)
    return place


class Reduction:
    def __init__(self, halves, bits, count):
        self.keep, self.bits, self.count = halves[0], bits, count
        self.level = 0
        self.coming = dp_swap(halves[1], bits[0], count)
        self.part = None

    def after(self, token):
        if self.level < len(self.bits):
            self.keep, _ = tie(self.keep, token)
        else:
            self.part, _ = tie(self.part, token)

    def add(self):
        total = self.keep.astype(jnp.float32) + self.coming.astype(jnp.float32)
        self.part = total.astype(jnp.bfloat16)
        self.level += 1
        if self.level == len(self.bits):
            done = 2 ** len(self.bits)
            if done < self.count:
                groups = [[j * done + i for j in range(self.count // done)] for i in range(done)]
                self.part = lax.psum(self.part, "dp", axis_index_groups=groups)
        return self.part

    def send(self):
        if self.level < len(self.bits):
            half = self.part.shape[0] // 2
            self.keep = self.part[:half]
            self.coming = dp_swap(self.part[half:], self.bits[self.level], self.count)
        else:
            self.coming = dp_swap(self.part, self.bits[2 * len(self.bits) - 1 - self.level], self.count)

    def join(self):
        self.part = jnp.concatenate([self.part, self.coming], axis=0)
        self.level += 1
        return self.part


def tie(*values):
    return lax.optimization_barrier(values)


def place_feed(halves, place, pieces, shape, index_map):
    rows, width = halves[0].shape
    size = 2 * rows // pieces
    steps = 8
    per = pieces // steps

    def kernel(place_ref, a_ref, b_ref, out_ref):
        for k in range(per):
            spot = jnp.bitwise_xor(place_ref[0], pl.program_id(0) * per + k)
            span = pl.ds(pl.multiple_of(lax.rem(spot, pieces // 2) * size, size), size)
            values = jnp.where(spot < pieces // 2, a_ref[span, :], b_ref[span, :])
            out_ref[k * size : (k + 1) * size, :] = values.astype(jnp.float32)

    flat = pl.BlockSpec((rows, width), lambda b, s: (0, 0))
    return pl.pallas_call(
        kernel,
        grid_spec=pltpu.PrefetchScalarGridSpec(
            num_scalar_prefetch=1,
            grid=(steps,),
            in_specs=[flat, flat],
            out_specs=pl.BlockSpec((per * size, width), index_map),
        ),
        out_shape=jax.ShapeDtypeStruct(shape, jnp.float32),
        compiler_params=pltpu.CompilerParams(vmem_limit_bytes=12 * MB),
        cost_estimate=cost(rows * width, 12 * rows * width),
        name="place_feed",
    )(place.reshape(1), *halves)


def place_attention(first, second, places, pieces):
    model, width = first[0].shape
    size = 2 * model // pieces
    fine = model // size

    def kernel(place_ref, fa_ref, fb_ref, sa_ref, sb_ref, q_ref, k_ref, v_ref, o_ref):
        for out_ref, a_ref, b_ref, which, base in (
            (q_ref, fa_ref, fb_ref, 0, 0),
            (k_ref, fa_ref, fb_ref, 0, fine),
            (v_ref, sa_ref, sb_ref, 1, 0),
            (o_ref, sa_ref, sb_ref, 1, fine),
        ):
            for k in range(fine):
                spot = jnp.bitwise_xor(place_ref[which], base + k)
                rows = pl.ds(pl.multiple_of(lax.rem(spot, pieces // 2) * size, size), size)
                values = jnp.where(spot < pieces // 2, a_ref[rows, :], b_ref[rows, :]).astype(jnp.float32)
                if out_ref is o_ref:
                    side, row = k // (fine // 2), k % (fine // 2)
                    o_ref[row * size : (row + 1) * size, side * width : (side + 1) * width] = values
                else:
                    out_ref[k * size : (k + 1) * size, :] = values

    return pl.pallas_call(
        kernel,
        in_specs=[smem()] + [vmem()] * 4,
        out_specs=[vmem()] * 4,
        out_shape=[jax.ShapeDtypeStruct((model, width), jnp.float32)] * 3
        + [jax.ShapeDtypeStruct((width, model), jnp.float32)],
        compiler_params=pltpu.CompilerParams(vmem_limit_bytes=8 * MB),
        cost_estimate=cost(4 * model * width, 24 * model * width),
        name="place_attention",
    )(places, *first, *second)


def body(
    inputs, grad_out, page_lengths, gain_one, gain_two, w_query, w_key, w_value, w_out, w_up, w_down, rel_table
):
    count = lax.axis_size("dp")
    tensor_index = lax.axis_index("tensor")
    own_rows, model = inputs.shape
    rows = 2 * own_rows
    half = own_rows // 2
    ff = w_up.shape[1]
    weights = (w_query, w_key, w_value)
    bits_one = [b for b in (1, 2, 4, 8) if b < count]
    bits_two = [b for b in (1, 4, 8, 2) if b < count]
    pieces = 2 ** len(bits_one)
    places = jnp.stack([place_of(bits_one), place_of(bits_two)])

    info = tensor_index.reshape(1)
    gain_one, gain_two = gain_one.reshape(1, model), gain_two.reshape(1, model)
    inputs, places, info, gain_one, gain_two, rel_table = tie(
        inputs, places, info, gain_one, gain_two, rel_table
    )
    normed_own = first_norm(inputs, gain_one)
    normed_peer = swap(normed_own)
    query_own, key_own, value_own = project(normed_own, weights)
    key_marks, query_marks = page_marks(page_lengths[0], rows, info)
    strip = bias_strip(rel_table)
    sent_grad, normed_peer = tie(grad_out, normed_peer)
    grad_peer = swap(sent_grad)
    query_peer, key_peer, value_peer = project(normed_peer, weights)
    keys, values = (key_own, key_peer), (value_own, value_peer)
    marks = (key_marks, query_marks, strip)

    peer_outs, peer_lses, parts_from_peer = [], [], []
    query = query_peer
    for start in (0, half):
        out, lse, part = attention_forward(
            info, start, half, True, query, keys, values, *marks, w_out, jnp.bfloat16
        )
        peer_outs.append(out)
        peer_lses.append(lse)
        parts_from_peer.append(swap(part))
        query, _ = tie(query_peer, part)
    query, _, grad_peer = tie(query_own, part, grad_peer)
    own_out, own_lse, own_part = attention_forward(
        info, 0, own_rows, False, query, keys, values, *marks, w_out, jnp.float32
    )
    middles, normed_twos, normed_twos_peer = [], [], []
    for side, start in enumerate((0, half)):
        arrived = parts_from_peer[side]
        if side > 0:
            arrived, _ = tie(arrived, normed_two)
        middle, normed_two = second_norm(start, inputs, own_part, arrived, gain_two)
        middles.append(middle)
        normed_twos.append(normed_two)
        normed_twos_peer.append(swap(normed_two))
    own_hidden, own_pre, own_two, own_branch = feed(normed_twos, 0, grad_out, w_up, w_down, jnp.float32)
    last = own_two
    peer_hiddens, peer_pres, peer_branches, twos_from_peer = [], [], [], []
    for side, start in enumerate((0, half)):
        normed_two, _ = tie(normed_twos_peer[side], last)
        hidden, pre, two, branch = feed([normed_two], start, grad_peer, w_up, w_down, jnp.bfloat16)
        peer_hiddens.append(hidden)
        peer_pres.append(pre)
        peer_branches.append(branch)
        twos_from_peer.append(swap(two))
        last = two
    down_payload, up_payload = feed_grads(
        places,
        pieces,
        (own_hidden, *peer_hiddens),
        (own_pre, *peer_pres),
        (*normed_twos, *normed_twos_peer),
        (grad_out, grad_peer),
    )
    down = Reduction(down_payload, bits_one, count)
    up = Reduction(up_payload, bits_two, count)
    own_two, _ = tie(own_two, down_payload)
    back = second_norm_back(0, own_two, twos_from_peer[0], middles[0], grad_out, gain_two, w_out)
    backs = [back]
    branches_peer = [swap(back[1])]
    down.after(back[2])
    down.add()
    up.after(down.part)
    up.add()
    two, *_ = tie(twos_from_peer[1], down.part, up.part)
    down.send(), up.send()
    back = second_norm_back(half, own_two, two, middles[1], grad_out, gain_two, w_out)
    backs.append(back)
    branches_peer.append(swap(back[1]))
    seeds = None
    last = back[2]
    nears, fars, grad_qs_own, grad_qs_peer = [], [], [], []
    for side, start in enumerate((0, half)):
        grad, _ = tie(backs[side][2], last)
        grad_q, key_sum, value_sum, near, far = attention_backward(
            info, start, False, query_own, grad, own_out, own_lse, keys, values, *marks, seeds, jnp.float32
        )
        seeds = (key_sum, value_sum)
        nears.append(near)
        fars.append(far)
        grad_qs_own.append(grad_q)
        last = grad_q
    down.after(last)
    down.add()
    up.after(down.part)
    up.add()
    last = (down.part, up.part)
    down.send(), up.send()
    for side, start in enumerate((0, half)):
        branch, *_ = tie(branches_peer[side], *last)
        grad = nt(branch, w_out).astype(jnp.bfloat16)
        grad_q, key_sum, value_sum, near, far = attention_backward(
            info,
            start,
            True,
            query_peer,
            grad,
            peer_outs[side],
            peer_lses[side],
            keys,
            values,
            *marks,
            seeds,
            jnp.float32 if side == 0 else jnp.bfloat16,
        )
        seeds = (key_sum, value_sum)
        nears.append(near)
        fars.append(far)
        grad_qs_peer.append(grad_q)
        last = (grad_q,)
    grad_key, grad_value = seeds
    down.after(last[0])
    down.add()
    down.send()
    tied_q, _ = tie(grad_qs_peer[1], down.part)
    first_payload, second_payload = attention_grads(
        places,
        pieces,
        (normed_own, normed_peer),
        (*grad_qs_own, grad_qs_peer[0], tied_q),
        grad_key,
        grad_value,
        (own_out, *peer_outs),
        (backs[0][1], backs[1][1], *branches_peer),
    )
    first = Reduction(first_payload, bits_one, count)
    second = Reduction(second_payload, bits_two, count)
    tied_q, _ = tie(grad_qs_peer[1], first_payload)
    one_part = normed_grad((grad_qs_peer[0], tied_q), grad_key, grad_value, own_rows, weights)
    one_from_peer = swap(one_part)
    branches_sent = [tie(b, one_part)[0] for b in peer_branches]
    token = one_part

    def advance(chain):
        nonlocal token
        chain.after(token)
        if chain.level < len(bits_one):
            chain.add()
        else:
            chain.join()
        token = chain.part
        chain.send()

    for chain in (first, second, up, down, first, second, up, down, first, second, up):
        advance(chain)
    tied_peer, _ = tie(one_from_peer, token)
    input_grad, gain_one_part = first_norm_back(
        (*grad_qs_own,),
        grad_key,
        grad_value,
        weights,
        tied_peer,
        inputs,
        (backs[0][0], backs[1][0]),
        gain_one,
    )
    token = gain_one_part
    for chain in (first, second, down, first, second, up, down, first, second, up, first, second):
        advance(chain)

    branch_from_peer = swap(jnp.concatenate(branches_sent, axis=0))
    middle = jnp.concatenate(middles, axis=0)
    out = (middle + own_branch + branch_from_peer.astype(jnp.float32)).astype(jnp.bfloat16)
    heads = rel_table.shape[0]
    bands = band_sums(nears, fars)
    small = pack_small(gain_one_part, [backs[0][3], backs[1][3]], bands, heads)
    small = add_small(small, swap(small), 2)
    for bit in bits_one:
        small = add_small(small, dp_swap(small, bit, count), 8)
    if pieces < count:
        groups = [[j * pieces + i for j in range(count // pieces)] for i in range(pieces)]
        small = lax.psum(small, "dp", axis_index_groups=groups)
    table_total = small[2 : 2 + heads, : rel_table.shape[1]]
    down_total = place_feed((down.part, down.coming), places[0], pieces, (ff, model), lambda b, s: (b, 0))
    up_total = place_feed(
        (up.part, up.coming), places[1], pieces, (model, ff), lambda b, s: (lax.rem(b, 4), b // 4)
    )
    query_total, key_total, value_total, out_total = place_attention(
        (first.part, first.coming), (second.part, second.coming), places, pieces
    )
    return (
        out,
        input_grad,
        small[0],
        small[1],
        query_total,
        key_total,
        value_total,
        out_total,
        up_total,
        down_total,
        table_total,
    )


def solution(mesh):
    in_specs = (
        P(("dp", "tensor"), None),
        P(("dp", "tensor"), None),
        P("dp", None),
        P(),
        P(),
        P(None, "tensor"),
        P(None, "tensor"),
        P(None, "tensor"),
        P("tensor", None),
        P(None, "tensor"),
        P("tensor", None),
        P("tensor", None),
    )
    out_specs = (
        P(("dp", "tensor"), None),
        P(("dp", "tensor"), None),
        P(),
        P(),
        P(None, "tensor"),
        P(None, "tensor"),
        P(None, "tensor"),
        P("tensor", None),
        P(None, "tensor"),
        P("tensor", None),
        P("tensor", None),
    )
    return jax.shard_map(body, mesh=mesh, in_specs=in_specs, out_specs=out_specs, check_vma=False)
```

```python
import functools
import jax
import jax.numpy as jnp
from jax import lax
from jax.experimental import pallas as pl
from jax.experimental.pallas import tpu as pltpu
from jax.sharding import PartitionSpec as P

HEAD_DIM = 64
BUCKETS = 16
LOG2E = 1.4426950408889634
TILE = 128
QB = 256
MB = 1 << 20


def cost(flops, traffic, share=0.01):
    return pl.CostEstimate(flops=int(share * flops), transcendentals=0, bytes_accessed=int(share * traffic))


def nt(left, right):
    return lax.dot_general(left, right, (((1,), (1,)), ((), ())), preferred_element_type=jnp.float32)


def nn(left, right):
    return jnp.dot(left, right, preferred_element_type=jnp.float32)


def half_of(block, side):
    lanes = lax.broadcasted_iota(jnp.int32, block.shape, 1)
    keep = (lanes < HEAD_DIM) if side == 0 else (lanes >= HEAD_DIM)
    return jnp.where(keep, block, jnp.zeros_like(block))


def tile_pos(local_tile, tensor_index, tiles):
    return lax.rem(local_tile + (tiles // 2) * tensor_index, tiles)


def bias_rows(strip_ref, head, key_tile, query_tile, query_tiles, tensor_index, tiles):
    pieces = []
    key_pos = tile_pos(key_tile, tensor_index, tiles)
    for step in range(query_tiles):
        diff = tile_pos(query_tile + step, tensor_index, tiles) - key_pos
        pieces.append(strip_ref[head, jnp.clip(diff, -2, 2) + 2])
    return jnp.concatenate(pieces, axis=1)


def ones_rows(rows):
    return (lax.broadcasted_iota(jnp.int32, (16, rows), 0) == 0).astype(jnp.bfloat16)


def vmem():
    return pl.BlockSpec(memory_space=pltpu.VMEM)


def smem():
    return pl.BlockSpec(memory_space=pltpu.SMEM)


def rows_of(refs):
    return jnp.concatenate([ref[...] for ref in refs], axis=0) if len(refs) > 1 else refs[0][...]


def attention_forward(info, start, count, peer, query, keys, values, key_marks, query_marks, strip, w_out, part_type):
    own_rows, width = query.shape
    rows = key_marks.shape[0]
    model = w_out.shape[1]
    pairs = width // 128
    tiles = rows // TILE
    query_tiles = count // TILE
    base = (own_rows if peer else 0) + start
    first = base // TILE

    def kernel(info_ref, q_ref, ko_ref, kp_ref, vo_ref, vp_ref, kf_ref, qf_ref, strip_ref, w_ref, o_ref, lse_ref, part_ref):
        tensor_index = info_ref[0]
        marks = qf_ref[base : base + count, :]
        def one_pair(pair, carry):
            lanes = pl.ds(pl.multiple_of(pair * 128, 128), 128)
            keys = jnp.concatenate(
                [jnp.concatenate([ko_ref[:, lanes], kp_ref[:, lanes]], axis=0), kf_ref[...]], axis=1
            )
            value_t = jnp.concatenate([vo_ref[:, lanes].T, vp_ref[:, lanes].T], axis=1)
            outs = []
            for side in range(2):
                query_half = half_of(q_ref[start : start + count, lanes], side)
                raw = nt(keys, jnp.concatenate([query_half, marks], axis=1))
                parts = []
                top = None
                for j in range(tiles):
                    part = raw[j * TILE : (j + 1) * TILE] * (LOG2E * HEAD_DIM**-0.5) + bias_rows(
                        strip_ref, 2 * pair + side, j, first, query_tiles, tensor_index, tiles
                    )
                    parts.append(part)
                    top = part if top is None else jnp.maximum(top, part)
                peak = jnp.max(top, axis=0, keepdims=True)
                weights = jnp.concatenate([jnp.exp2(part - peak).astype(jnp.bfloat16) for part in parts], axis=0)
                left = jnp.concatenate([value_t[side * HEAD_DIM : (side + 1) * HEAD_DIM], ones_rows(rows)], axis=0)
                out_t = nn(left, weights)
                total = out_t[HEAD_DIM : HEAD_DIM + 1]
                outs.append(out_t[:HEAD_DIM] * (1.0 / total))
                lse_ref[pair, side : side + 1, :] = peak + jnp.log2(total)
            o_ref[:, lanes] = jnp.concatenate(outs, axis=0).T.astype(jnp.bfloat16)
            return carry

        lax.fori_loop(0, pairs, one_pair, 0)
        part_ref[...] = nn(o_ref[...], w_ref[...]).astype(part_type)

    return pl.pallas_call(
        kernel,
        in_specs=[smem()] + [vmem()] * 9,
        out_specs=[vmem()] * 3,
        out_shape=[
            jax.ShapeDtypeStruct((count, width), jnp.bfloat16),
            jax.ShapeDtypeStruct((pairs, 2, count), jnp.float32),
            jax.ShapeDtypeStruct((count, model), part_type),
        ],
        compiler_params=pltpu.CompilerParams(vmem_limit_bytes=8 * MB),
        cost_estimate=cost(9 * 10**9 * count // own_rows, 8 * rows * width),
        name="attend",
    )(info, query, *keys, *values, key_marks, query_marks, strip, w_out)


def attention_backward(
    info, start, peer, query, grad_out, out, lse, keys, values, key_marks, query_marks, strip, seeds, sum_type
):
    own_rows, width = query.shape
    count = grad_out.shape[0]
    rows = key_marks.shape[0]
    pairs = width // 128
    tiles = rows // TILE
    query_tiles = count // TILE
    base = (own_rows if peer else 0) + start
    first = base // TILE
    shift = start if out.shape[0] > count else 0
    seeded = seeds is not None
    scale = HEAD_DIM**-0.5

    def kernel(info_ref, q_ref, do_ref, o_ref, lse_ref, ko_ref, kp_ref, vo_ref, vp_ref, kf_ref, qf_ref, strip_ref, *rest):
        if seeded:
            dk_seed, dv_seed, *rest = rest
        dq_ref, dk_ref, dv_ref, near_ref, far_ref, grads_ref = rest
        tensor_index = info_ref[0]
        query_marks = qf_ref[base : base + count, :]
        marks = (
            lax.broadcasted_iota(jnp.int32, (16, rows), 1) // TILE
            == lax.broadcasted_iota(jnp.int32, (16, rows), 0)
        ).astype(jnp.bfloat16)
        key_pos = tile_pos(lax.broadcasted_iota(jnp.int32, (8, TILE), 0), tensor_index, tiles)
        def one_pair(pair, carry):
            lanes = pl.ds(pl.multiple_of(pair * 128, 128), 128)
            key_pair = jnp.concatenate([ko_ref[:, lanes], kp_ref[:, lanes]], axis=0)
            keys = jnp.concatenate([key_pair, kf_ref[...]], axis=1)
            key_t = key_pair.T
            values = jnp.concatenate([vo_ref[:, lanes], vp_ref[:, lanes]], axis=0)
            inner = do_ref[:, lanes].astype(jnp.float32) * o_ref[shift : shift + count, lanes].astype(jnp.float32)
            inner = inner.T
            probs, grads, grad_qs, query_halves, do_halves = [], [], [], [], []
            for side in range(2):
                head = 2 * pair + side
                query_half = half_of(q_ref[start : start + count, lanes], side)
                do_half = half_of(do_ref[:, lanes], side)
                query_halves.append(query_half)
                do_halves.append(do_half)
                raw = nt(keys, jnp.concatenate([query_half, query_marks], axis=1))
                grad_prob = nt(values, do_half)
                lse = lse_ref[pair, side : side + 1, shift : shift + count]
                delta = jnp.sum(inner[side * HEAD_DIM : (side + 1) * HEAD_DIM], axis=0, keepdims=True)
                prob_parts, grad_parts = [], []
                for j in range(tiles):
                    span = slice(j * TILE, (j + 1) * TILE)
                    bias = bias_rows(strip_ref, head, j, first, query_tiles, tensor_index, tiles)
                    prob = jnp.exp2(raw[span] * (LOG2E * scale) + (bias - lse))
                    grad = (prob * (grad_prob[span] - delta)).astype(jnp.bfloat16)
                    grads_ref[side, span, :] = grad
                    prob_parts.append(prob.astype(jnp.bfloat16))
                    grad_parts.append(grad)
                probs.append(jnp.concatenate(prob_parts, axis=0))
                grad_all = jnp.concatenate(grad_parts, axis=0)
                grads.append(grad_all)
                left = jnp.concatenate([key_t[side * HEAD_DIM : (side + 1) * HEAD_DIM], marks], axis=0)
                grad_q = nn(left, grad_all)
                grad_qs.append(grad_q[:HEAD_DIM])
                sums = grad_q[HEAD_DIM : HEAD_DIM + 8]
                before, after = jnp.zeros((8, TILE), jnp.float32), jnp.zeros((8, TILE), jnp.float32)
                for part in range(query_tiles):
                    query_pos = tile_pos(first + part, tensor_index, tiles)
                    piece = sums[:, part * TILE : (part + 1) * TILE]
                    before = before + jnp.where(key_pos <= query_pos - 2, piece, 0.0)
                    after = after + jnp.where(key_pos >= query_pos + 2, piece, 0.0)
                far_ref[head, 0] = before
                far_ref[head, 1] = after
                for diff in (-1, 0, 1):
                    near = None
                    for part in range(query_tiles):
                        wanted = tile_pos(first + part, tensor_index, tiles) - diff
                        valid = jnp.logical_and(wanted >= 0, wanted < tiles)
                        local = tile_pos(jnp.clip(wanted, 0, tiles - 1), tensor_index, tiles)
                        block = grads_ref[
                            side,
                            pl.ds(pl.multiple_of(local * TILE, TILE), TILE),
                            part * TILE : (part + 1) * TILE,
                        ].astype(jnp.float32)
                        block = block if diff == 0 else jnp.where(valid, block, 0.0)
                        near = block if near is None else near + block
                    near_ref[head, diff + 1] = near
            dv = nn(jnp.concatenate(probs, axis=1), jnp.concatenate(do_halves, axis=0))
            dk = nn(jnp.concatenate(grads, axis=1), jnp.concatenate(query_halves, axis=0)) * scale
            if seeded:
                dv = dv + dv_seed[:, lanes]
                dk = dk + dk_seed[:, lanes]
            dv_ref[:, lanes] = dv.astype(sum_type)
            dk_ref[:, lanes] = dk.astype(sum_type)
            dq_ref[:, lanes] = (jnp.concatenate(grad_qs, axis=0).T * scale).astype(jnp.bfloat16)
            return carry

        lax.fori_loop(0, pairs, one_pair, 0)

    return pl.pallas_call(
        kernel,
        in_specs=[smem()] + [vmem()] * (13 if seeded else 11),
        out_specs=[vmem()] * 5,
        out_shape=[
            jax.ShapeDtypeStruct((count, width), jnp.bfloat16),
            jax.ShapeDtypeStruct((rows, width), sum_type),
            jax.ShapeDtypeStruct((rows, width), sum_type),
            jax.ShapeDtypeStruct((2 * pairs, 3, TILE, TILE), jnp.float32),
            jax.ShapeDtypeStruct((2 * pairs, 2, 8, TILE), jnp.float32),
        ],
        scratch_shapes=[pltpu.VMEM((2, rows, count), jnp.bfloat16)],
        compiler_params=pltpu.CompilerParams(vmem_limit_bytes=14 * MB),
        cost_estimate=cost(18 * 10**9 * count // own_rows, 20 * rows * width),
        name="attend_back",
    )(info, query, grad_out, out, lse, *keys, *values, key_marks, query_marks, strip, *(seeds or ()))


def band_levels(diff):
    delta = diff * TILE + (
        lax.broadcasted_iota(jnp.int32, (TILE, TILE), 1) - lax.broadcasted_iota(jnp.int32, (TILE, TILE), 0)
    )
    distance = jnp.abs(delta) + 1
    level = jnp.zeros_like(delta)
    for exponent in range(1, BUCKETS // 2):
        level = level + (distance >= 2**exponent).astype(jnp.int32)
    return level + (BUCKETS // 2) * (delta < 0).astype(jnp.int32)


def band_sums(nears, fars):
    heads = nears[0].shape[0]
    calls = len(nears)

    def kernel(*refs):
        near_refs, far_refs, o_ref = refs[:calls], refs[calls : 2 * calls], refs[-1]
        rows = [[jnp.zeros((1, TILE), jnp.float32) for _ in range(BUCKETS)] for _ in range(heads)]
        for head in range(heads):
            far = sum(ref[head] for ref in far_refs)
            rows[head][BUCKETS // 2 - 1] += jnp.sum(far[0], axis=0, keepdims=True)
            rows[head][BUCKETS - 1] += jnp.sum(far[1], axis=0, keepdims=True)
        for diff, present in ((0, [*range(8), *range(9, 16)]), (1, range(1, 8)), (-1, range(9, 16))):
            level = band_levels(diff)
            for head in range(heads):
                near = sum(ref[head, diff + 1] for ref in near_refs)
                for bucket in present:
                    rows[head][bucket] += jnp.sum(jnp.where(level == bucket, near, 0.0), axis=0, keepdims=True)
        at = lax.broadcasted_iota(jnp.int32, (BUCKETS, TILE), 0) == lax.broadcasted_iota(
            jnp.int32, (BUCKETS, TILE), 1
        )
        o_ref[...] = jnp.zeros_like(o_ref)
        for head in range(heads):
            sums = jnp.sum(jnp.concatenate(rows[head], axis=0), axis=1, keepdims=True)
            o_ref[head : head + 1, :] = jnp.sum(jnp.where(at, sums, 0.0), axis=0, keepdims=True)

    return pl.pallas_call(
        kernel,
        in_specs=[vmem()] * (2 * calls),
        out_specs=vmem(),
        out_shape=jax.ShapeDtypeStruct((8, TILE), jnp.float32),
        compiler_params=pltpu.CompilerParams(vmem_limit_bytes=8 * MB),
        cost_estimate=cost(heads * 3 * 16 * TILE * TILE, heads * 8 * TILE * TILE),
        name="band_sums",
    )(*nears, *fars)


def pack_small(gain_one_part, gain_two_parts, table, heads):
    model = gain_one_part.shape[1]
    calls = len(gain_two_parts)

    def kernel(*refs):
        one_ref, table_ref, o_ref = refs[0], refs[calls + 1], refs[calls + 2]
        o_ref[...] = jnp.zeros_like(o_ref)
        o_ref[0:1, :] = jnp.sum(one_ref[...], axis=0, keepdims=True)
        two = sum(ref[...] for ref in refs[1 : calls + 1])
        o_ref[1:2, :] = jnp.sum(two, axis=0, keepdims=True)
        o_ref[2 : 2 + heads, :TILE] = table_ref[:heads, :]

    return pl.pallas_call(
        kernel,
        in_specs=[vmem()] * (calls + 2),
        out_specs=vmem(),
        out_shape=jax.ShapeDtypeStruct((8, model), jnp.float32),
        compiler_params=pltpu.CompilerParams(vmem_limit_bytes=2 * MB),
        cost_estimate=cost(1000, 1000),
        name="pack_small",
    )(gain_one_part, *gain_two_parts, table)


def add_small(mine, theirs, rows):
    def kernel(a_ref, b_ref, o_ref):
        line = lax.broadcasted_iota(jnp.int32, a_ref.shape, 0)
        o_ref[...] = a_ref[...] + jnp.where(line < rows, b_ref[...], 0.0)

    return pl.pallas_call(
        kernel,
        in_specs=[vmem()] * 2,
        out_specs=vmem(),
        out_shape=jax.ShapeDtypeStruct(mine.shape, jnp.float32),
        compiler_params=pltpu.CompilerParams(vmem_limit_bytes=2 * MB),
        cost_estimate=cost(1000, 1000),
        name="add_small",
    )(mine, theirs)


def bias_strip(rel_table):
    heads = rel_table.shape[0]

    def kernel(t_ref, o_ref):
        table = t_ref[...].astype(jnp.float32) * LOG2E
        levels = [band_levels(diff) for diff in (-1, 0, 1)]
        masks = [[level == bucket for bucket in range(BUCKETS)] for level in levels]
        for head in range(heads):
            entries = [table[head : head + 1, bucket : bucket + 1] for bucket in range(BUCKETS)]
            for slot, present in enumerate((range(9, 16), [*range(8), *range(9, 16)], range(1, 8))):
                tile = jnp.zeros((TILE, TILE), jnp.float32)
                for bucket in present:
                    tile = jnp.where(masks[slot][bucket], entries[bucket], tile)
                o_ref[head, slot + 1] = tile
            o_ref[head, 0] = jnp.broadcast_to(entries[15], (TILE, TILE))
            o_ref[head, 4] = jnp.broadcast_to(entries[7], (TILE, TILE))

    return pl.pallas_call(
        kernel,
        in_specs=[vmem()],
        out_specs=vmem(),
        out_shape=jax.ShapeDtypeStruct((heads, 5, TILE, TILE), jnp.float32),
        compiler_params=pltpu.CompilerParams(vmem_limit_bytes=8 * MB),
        cost_estimate=cost(10**9, 0, 1),
        name="bias_strip",
    )(rel_table)


def page_marks(lengths, rows, tensor_index):
    slots = lengths.shape[0]

    def kernel(len_ref, t_ref, k_ref, q_ref):
        place = lax.broadcasted_iota(jnp.int32, (rows, 128), 0) + (rows // 2) * t_ref[0]
        place = jnp.where(place >= rows, place - rows, place)
        lanes = lax.broadcasted_iota(jnp.int32, (rows, 128), 1)
        end = jnp.int32(0)
        page = jnp.zeros((rows, 128), jnp.int32)
        for slot in range(slots):
            end = end + len_ref[slot]
            page = page + (place >= end).astype(jnp.int32)
        k_ref[...] = jnp.where(page == lanes, 1.0, 0.0).astype(jnp.bfloat16)
        other = jnp.logical_and(page != lanes, lanes < slots)
        q_ref[...] = jnp.where(other, -1e30, 0.0).astype(jnp.bfloat16)

    return pl.pallas_call(
        kernel,
        in_specs=[smem(), smem()],
        out_specs=[vmem()] * 2,
        out_shape=[jax.ShapeDtypeStruct((rows, 128), jnp.bfloat16)] * 2,
        compiler_params=pltpu.CompilerParams(vmem_limit_bytes=8 * MB),
        cost_estimate=cost(10**9, 0, 1),
        name="page_marks",
    )(lengths, tensor_index)


def tn(left, right):
    return lax.dot_general(left, right, (((0,), (0,)), ((), ())), preferred_element_type=jnp.float32)


def standardize(values):
    centred = values - jnp.mean(values, axis=-1, keepdims=True)
    variance = jnp.mean(centred * centred, axis=-1, keepdims=True)
    inverse = lax.rsqrt(variance + 1e-05)
    return centred * inverse, inverse


def norm_back(grad, standard, inverse, gain):
    scaled = grad * gain
    mean = jnp.mean(scaled, axis=-1, keepdims=True)
    slope = jnp.mean(scaled * standard, axis=-1, keepdims=True)
    return inverse * (scaled - mean - standard * slope)


def fold_rows(values):
    return jnp.sum(values.reshape(-1, 8, values.shape[-1]), axis=0)


def first_norm(inputs, gain):
    rows, model = inputs.shape

    def kernel(x_ref, g_ref, o_ref):
        gain = g_ref[...].astype(jnp.float32)
        for start in range(0, rows, 128):
            standard, _ = standardize(x_ref[start : start + 128, :].astype(jnp.float32))
            o_ref[start : start + 128, :] = (standard * gain).astype(jnp.bfloat16)

    return pl.pallas_call(
        kernel,
        in_specs=[vmem()] * 2,
        out_specs=vmem(),
        out_shape=jax.ShapeDtypeStruct((rows, model), jnp.bfloat16),
        compiler_params=pltpu.CompilerParams(vmem_limit_bytes=6 * MB),
        cost_estimate=cost(rows * model * 8, 4 * rows * model),
        name="first_norm",
    )(inputs, gain)


def project(normed, weights):
    rows, model = normed.shape
    width = weights[0].shape[1]

    def kernel(x_ref, *refs):
        for w_ref, o_ref in zip(refs[:3], refs[3:]):
            o_ref[...] = nn(x_ref[...], w_ref[...]).astype(jnp.bfloat16)

    return pl.pallas_call(
        kernel,
        in_specs=[vmem()] * 4,
        out_specs=[vmem()] * 3,
        out_shape=[jax.ShapeDtypeStruct((rows, width), jnp.bfloat16)] * 3,
        compiler_params=pltpu.CompilerParams(vmem_limit_bytes=4 * MB),
        cost_estimate=cost(6 * rows * model * width, 0, 1),
        name="project",
    )(normed, *weights)


def second_norm(start, inputs, own_part, peer_part, gain):
    rows, model = peer_part.shape

    def kernel(x_ref, a_ref, b_ref, g_ref, m_ref, o_ref):
        gain = g_ref[...].astype(jnp.float32)
        for offset in range(0, rows, 128):
            span = slice(offset, offset + 128)
            wide = slice(start + offset, start + offset + 128)
            middle = x_ref[wide, :].astype(jnp.float32) + a_ref[wide, :] + b_ref[span, :].astype(jnp.float32)
            m_ref[span, :] = middle
            standard, _ = standardize(middle)
            o_ref[span, :] = (standard * gain).astype(jnp.bfloat16)

    return pl.pallas_call(
        kernel,
        in_specs=[vmem()] * 4,
        out_specs=[vmem()] * 2,
        out_shape=[
            jax.ShapeDtypeStruct((rows, model), jnp.float32),
            jax.ShapeDtypeStruct((rows, model), jnp.bfloat16),
        ],
        compiler_params=pltpu.CompilerParams(vmem_limit_bytes=8 * MB),
        cost_estimate=cost(rows * model * 8, 14 * rows * model),
        name="second_norm",
    )(inputs, own_part, peer_part, gain)


FF_CHUNK = 512


def feed(normeds, start, grads, w_up, w_down, sum_type):
    rows = sum(n.shape[0] for n in normeds)
    model, ff = w_up.shape
    calls = len(normeds)

    def kernel(*refs):
        g_ref, u_ref, d_ref, h_ref, p_ref, gn_ref, bt_ref = refs[calls:]
        normed = rows_of(refs[:calls])
        for begin in range(0, ff, FF_CHUNK):
            span = slice(begin, begin + FF_CHUNK)
            pre = nn(normed, u_ref[:, span])
            grad_hidden = nt(g_ref[start : start + rows, :], d_ref[span, :])
            square = pre * pre
            bent = jnp.tanh(pre * (0.7978845608 + (0.7978845608 * 0.044715) * square))
            gate = 0.5 + 0.5 * bent
            h_ref[:, span] = (pre * gate).astype(jnp.bfloat16)
            slope = gate + pre * (0.5 - 0.5 * bent * bent) * (
                0.7978845608 + (3 * 0.7978845608 * 0.044715) * square
            )
            p_ref[:, span] = (grad_hidden * slope).astype(jnp.bfloat16)
        gn_ref[...] = nt(p_ref[...], u_ref[...]).astype(sum_type)
        bt_ref[...] = nn(h_ref[...], d_ref[...]).astype(sum_type)

    return pl.pallas_call(
        kernel,
        in_specs=[vmem()] * (calls + 3),
        out_specs=[vmem()] * 4,
        out_shape=[jax.ShapeDtypeStruct((rows, ff), jnp.bfloat16)] * 2
        + [jax.ShapeDtypeStruct((rows, model), sum_type)] * 2,
        compiler_params=pltpu.CompilerParams(vmem_limit_bytes=8 * MB),
        cost_estimate=cost(8 * rows * model * ff, 4 * model * ff + 8 * rows * ff),
        name="feed",
    )(*normeds, grads, w_up, w_down)


def grouped_call(kernel, groups, **options):
    sizes = [len(g) for g in groups]

    def body(place_ref, *refs):
        lists, at = [], 0
        for size in sizes:
            lists.append(refs[at : at + size])
            at += size
        kernel(place_ref, *lists, *refs[at:])

    return pl.pallas_call(body, in_specs=[smem()] + [vmem()] * sum(sizes), **options)


def turned(refs, span=slice(None)):
    return jnp.concatenate([ref[:, span].T for ref in refs], axis=1)


def feed_grads(places, pieces, hiddens, grad_pres, normeds, grads):
    rows = sum(h.shape[0] for h in hiddens)
    ff = hiddens[0].shape[1]
    model = normeds[0].shape[1]
    size = ff // pieces
    fine = model // size

    def kernel(place_ref, h_refs, p_refs, n_refs, g_refs, *rest):
        down_ref, up_ref = rest[4:]
        grad = rows_of(g_refs)
        normed_t = turned(n_refs)
        for part in range(ff // model):
            span = slice(part * model, (part + 1) * model)
            down = nn(turned(h_refs, span), grad).astype(jnp.bfloat16)
            for k in range(fine):
                store_piece(down_ref, place_ref[0], pieces, part * fine + k, size, down[k * size : (k + 1) * size])
        for part in range(ff // model):
            span = slice(part * model, (part + 1) * model)
            pre = jnp.concatenate([ref[:, span] for ref in p_refs], axis=0)
            up = nn(normed_t, pre).astype(jnp.bfloat16)
            for k in range(fine):
                store_piece(up_ref, place_ref[1], pieces, part * fine + k, size, up[k * size : (k + 1) * size])
        for number, out_ref in enumerate(rest[:4]):
            out_ref[...] = (down_ref, up_ref)[number // 2][number % 2]

    groups = (hiddens, grad_pres, normeds, grads)
    return grouped_call(
        kernel,
        groups,
        out_specs=[vmem()] * 4,
        out_shape=[jax.ShapeDtypeStruct((ff // 2, model), jnp.bfloat16)] * 4,
        scratch_shapes=[pltpu.VMEM((2, ff // 2, model), jnp.bfloat16)] * 2,
        compiler_params=pltpu.CompilerParams(vmem_limit_bytes=16 * MB),
        cost_estimate=cost(4 * rows * model * ff, 4 * rows * ff + 4 * ff * model),
        name="feed_grads",
    )(places, *[a for g in groups for a in g])


def second_norm_back(start, own_part, peer_part, middle, grad_out, gain, w_out):
    rows, model = middle.shape
    width = w_out.shape[0]

    def kernel(a_ref, b_ref, m_ref, g_ref, gain_ref, w_ref, gm_ref, gb_ref, ga_ref, gain_out):
        gain = gain_ref[...].astype(jnp.float32)
        part = jnp.zeros((8, model), jnp.float32)
        for offset in range(0, rows, 128):
            span = slice(offset, offset + 128)
            wide = slice(start + offset, start + offset + 128)
            grad = a_ref[wide, :] + b_ref[span, :].astype(jnp.float32)
            standard, inverse = standardize(m_ref[span, :])
            result = g_ref[wide, :].astype(jnp.float32) + norm_back(grad, standard, inverse, gain)
            gm_ref[span, :] = result
            gb_ref[span, :] = result.astype(jnp.bfloat16)
            part = part + fold_rows(grad * standard)
        gain_out[...] = part
        ga_ref[...] = nt(gb_ref[...], w_ref[...]).astype(jnp.bfloat16)

    return pl.pallas_call(
        kernel,
        in_specs=[vmem()] * 6,
        out_specs=[vmem()] * 4,
        out_shape=[
            jax.ShapeDtypeStruct((rows, model), jnp.float32),
            jax.ShapeDtypeStruct((rows, model), jnp.bfloat16),
            jax.ShapeDtypeStruct((rows, width), jnp.bfloat16),
            jax.ShapeDtypeStruct((8, model), jnp.float32),
        ],
        compiler_params=pltpu.CompilerParams(vmem_limit_bytes=10 * MB),
        cost_estimate=cost(10**11, 0, 1 if start else 0.0),
        name="second_norm_back",
    )(own_part, peer_part, middle, grad_out, gain, w_out)


def normed_grad(grad_qs, grad_k, grad_v, offset, weights):
    rows = sum(q.shape[0] for q in grad_qs)
    model, width = weights[0].shape
    calls = len(grad_qs)

    def kernel(*refs):
        k_ref, v_ref, wq_ref, wk_ref, wv_ref, o_ref = refs[calls:]
        span = slice(offset, offset + rows)
        total = nt(rows_of(refs[:calls]), wq_ref[...])
        total = total + nt(k_ref[span, :], wk_ref[...]) + nt(v_ref[span, :], wv_ref[...])
        o_ref[...] = total.astype(jnp.bfloat16)

    return pl.pallas_call(
        kernel,
        in_specs=[vmem()] * (calls + 5),
        out_specs=vmem(),
        out_shape=jax.ShapeDtypeStruct((rows, model), jnp.bfloat16),
        compiler_params=pltpu.CompilerParams(vmem_limit_bytes=6 * MB),
        cost_estimate=cost(10**11, 0, 1),
        name="normed_grad",
    )(*grad_qs, grad_k, grad_v, *weights)


def first_norm_back(grad_qs, grad_k, grad_v, weights, peer_part, inputs, middles, gain):
    rows, model = inputs.shape
    width = weights[0].shape[1]
    calls = len(grad_qs)
    size = rows // calls

    def kernel(*refs):
        q_refs, m_refs = refs[:calls], refs[calls : 2 * calls]
        k_ref, v_ref, wq_ref, wk_ref, wv_ref, b_ref, x_ref, gain_ref, o_ref, gain_out = refs[2 * calls :]
        gain = gain_ref[...].astype(jnp.float32)
        part = jnp.zeros((8, model), jnp.float32)
        for call in range(calls):
            span = slice(call * size, (call + 1) * size)
            grad = nt(q_refs[call][...], wq_ref[...])
            grad = grad + nt(k_ref[span, :], wk_ref[...]) + nt(v_ref[span, :], wv_ref[...])
            grad = grad + b_ref[span, :].astype(jnp.float32)
            standard, inverse = standardize(x_ref[span, :].astype(jnp.float32))
            result = m_refs[call][...] + norm_back(grad, standard, inverse, gain)
            o_ref[span, :] = result.astype(jnp.bfloat16)
            part = part + fold_rows(grad * standard)
        gain_out[...] = part

    return pl.pallas_call(
        kernel,
        in_specs=[vmem()] * (2 * calls + 8),
        out_specs=[vmem()] * 2,
        out_shape=[
            jax.ShapeDtypeStruct((rows, model), jnp.bfloat16),
            jax.ShapeDtypeStruct((8, model), jnp.float32),
        ],
        compiler_params=pltpu.CompilerParams(vmem_limit_bytes=10 * MB),
        cost_estimate=cost(6 * rows * model * width, 12 * rows * model),
        name="first_norm_back",
    )(*grad_qs, *middles, grad_k, grad_v, *weights, peer_part, inputs, gain)


def store_piece(ref, place, pieces, block, size, values):
    half = pieces // 2
    spot = jnp.bitwise_xor(place, block)
    ref[spot // half, pl.ds(pl.multiple_of(lax.rem(spot, half) * size, size), size), :] = values


def attention_grads(places, pieces, normeds, grad_qs, grad_k, grad_v, outs, branches):
    rows, width = grad_k.shape
    model = normeds[0].shape[1]
    size = 2 * model // pieces
    fine = model // size

    def kernel(place_ref, n_refs, q_refs, k_refs, v_refs, o_refs, b_refs, *rest):
        first_ref, second_ref = rest[4:]
        normed_t = turned(n_refs)
        for ref, which, base, right in (
            (first_ref, 2, 0, rows_of(q_refs)),
            (first_ref, 2, fine, rows_of(k_refs)),
            (second_ref, 3, 0, rows_of(v_refs)),
        ):
            result = nn(normed_t, right).astype(jnp.bfloat16)
            for k in range(fine):
                store_piece(ref, place_ref[which], pieces, base + k, size, result[k * size : (k + 1) * size])
        result = nn(turned(o_refs), rows_of(b_refs)).astype(jnp.bfloat16)
        for side in range(2):
            for k in range(fine // 2):
                store_piece(
                    second_ref,
                    place_ref[3],
                    pieces,
                    fine + side * (fine // 2) + k,
                    size,
                    result[k * size : (k + 1) * size, side * width : (side + 1) * width],
                )
        for number, out_ref in enumerate(rest[:4]):
            out_ref[...] = (first_ref, second_ref)[number // 2][number % 2]

    groups = (normeds, grad_qs, (grad_k,), (grad_v,), outs, branches)
    return grouped_call(
        kernel,
        groups,
        out_specs=[vmem()] * 4,
        out_shape=[jax.ShapeDtypeStruct((model, width), jnp.bfloat16)] * 4,
        scratch_shapes=[pltpu.VMEM((2, model, width), jnp.bfloat16)] * 2,
        compiler_params=pltpu.CompilerParams(vmem_limit_bytes=12 * MB),
        cost_estimate=cost(8 * rows * model * width, 6 * rows * model),
        name="attention_grads",
    )(places, *[a for g in groups for a in g])


def swap(values):
    return lax.ppermute(values, "tensor", [(0, 1), (1, 0)])


def dp_swap(values, bit, count):
    return lax.ppermute(values, "dp", [(i, i ^ bit) for i in range(count)])


def place_of(bits):
    index = lax.axis_index("dp")
    place = jnp.int32(0)
    for bit in bits:
        place = place * 2 + lax.rem(index // bit, 2)
    return place


def owner_place(block, bits, gather):
    place = 0
    for bit in reversed(gather):
        place = place * 2 + (block // 2 ** (len(bits) - 1 - bits.index(bit))) % 2
    return place


def add_rows(mine, theirs, split, weight):
    rows, width = mine.shape
    size = rows // 2 if split else rows

    def kernel(a_ref, b_ref, *out_refs):
        for part, out_ref in enumerate(out_refs):
            span = slice(part * size, (part + 1) * size)
            total = a_ref[span, :].astype(jnp.float32) + b_ref[span, :].astype(jnp.float32)
            out_ref[...] = total.astype(jnp.bfloat16)

    count = 2 if split else 1
    return pl.pallas_call(
        kernel,
        in_specs=[vmem()] * 2,
        out_specs=[vmem()] * count,
        out_shape=[jax.ShapeDtypeStruct((size, width), jnp.bfloat16)] * count,
        compiler_params=pltpu.CompilerParams(vmem_limit_bytes=4 * MB),
        cost_estimate=cost(weight, 0, 1),
        name="add_rows",
    )(mine, theirs)


def join_rows(upper, lower, weight):
    rows, width = upper.shape

    def kernel(a_ref, b_ref, o_ref):
        o_ref[:rows, :] = a_ref[...]
        o_ref[rows:, :] = b_ref[...]

    return pl.pallas_call(
        kernel,
        in_specs=[vmem()] * 2,
        out_specs=vmem(),
        out_shape=jax.ShapeDtypeStruct((2 * rows, width), jnp.bfloat16),
        compiler_params=pltpu.CompilerParams(vmem_limit_bytes=2 * MB),
        cost_estimate=cost(weight, 0, 1),
        name="join_rows",
    )(upper, lower)


class Reduction:
    def __init__(self, halves, bits, last, gather, count):
        self.keep, self.bits, self.last, self.gather, self.count = halves[0], bits, last, gather, count
        self.level = 0
        self.coming = dp_swap(halves[1], bits[0], count)
        self.part = None

    @property
    def steps(self):
        return len(self.bits) + len(self.last) + len(self.gather) - 1

    def after(self, token):
        if self.level < len(self.bits) + len(self.last):
            self.keep, _ = tie(self.keep, token)
        else:
            self.part, _ = tie(self.part, token)

    def advance(self, weight):
        sums = len(self.bits) + len(self.last)
        if self.level < sums:
            split = self.level + 1 < len(self.bits)
            self.part, *sent = add_rows(self.keep, self.coming, split, weight)
        else:
            self.part = join_rows(self.part, self.coming, weight)
        self.level += 1
        if self.level == sums:
            done = 2**sums
            if done < self.count:
                groups = [[j * done + i for j in range(self.count // done)] for i in range(done)]
                self.part = lax.psum(self.part, "dp", axis_index_groups=groups)
        if self.level < len(self.bits):
            self.keep = self.part
            self.coming = dp_swap(sent[0], self.bits[self.level], self.count)
        elif self.level < sums:
            self.keep = self.part
            self.coming = dp_swap(self.part, self.last[0], self.count)
        else:
            self.coming = dp_swap(self.part, self.gather[self.level - sums], self.count)
        return self.part


def tie(*values):
    return lax.optimization_barrier(values)


def place_feed(halves, place, bits, gather, shape, index_map):
    pieces = 2 ** len(bits)
    rows, width = halves[0].shape
    size = 2 * rows // pieces
    steps = 8
    per = pieces // steps

    def kernel(place_ref, a_ref, b_ref, out_ref):
        for k in range(per):
            spot = jnp.bitwise_xor(place_ref[0], owner_place(pl.program_id(0) * per + k, bits, gather))
            span = pl.ds(pl.multiple_of(lax.rem(spot, pieces // 2) * size, size), size)
            values = jnp.where(spot < pieces // 2, a_ref[span, :], b_ref[span, :])
            out_ref[k * size : (k + 1) * size, :] = values.astype(jnp.float32)

    flat = pl.BlockSpec((rows, width), lambda b, s: (0, 0))
    return pl.pallas_call(
        kernel,
        grid_spec=pltpu.PrefetchScalarGridSpec(
            num_scalar_prefetch=1,
            grid=(steps,),
            in_specs=[flat, flat],
            out_specs=pl.BlockSpec((per * size, width), index_map),
        ),
        out_shape=jax.ShapeDtypeStruct(shape, jnp.float32),
        compiler_params=pltpu.CompilerParams(vmem_limit_bytes=12 * MB),
        cost_estimate=cost(rows * width, 12 * rows * width),
        name="place_feed",
    )(place.reshape(1), *halves)


def place_attention(first, second, places, orders):
    pieces = 2 ** len(orders[0][0])
    model, width = first[0].shape
    size = 2 * model // pieces
    fine = model // size

    def kernel(place_ref, fa_ref, fb_ref, sa_ref, sb_ref, q_ref, k_ref, v_ref, o_ref):
        for out_ref, a_ref, b_ref, which, base in (
            (q_ref, fa_ref, fb_ref, 0, 0),
            (k_ref, fa_ref, fb_ref, 0, fine),
            (v_ref, sa_ref, sb_ref, 1, 0),
            (o_ref, sa_ref, sb_ref, 1, fine),
        ):
            for k in range(fine):
                spot = jnp.bitwise_xor(place_ref[which], owner_place(base + k, orders[which][0], orders[which][2]))
                rows = pl.ds(pl.multiple_of(lax.rem(spot, pieces // 2) * size, size), size)
                values = jnp.where(spot < pieces // 2, a_ref[rows, :], b_ref[rows, :]).astype(jnp.float32)
                if out_ref is o_ref:
                    side, row = k // (fine // 2), k % (fine // 2)
                    o_ref[row * size : (row + 1) * size, side * width : (side + 1) * width] = values
                else:
                    out_ref[k * size : (k + 1) * size, :] = values

    return pl.pallas_call(
        kernel,
        in_specs=[smem()] + [vmem()] * 4,
        out_specs=[vmem()] * 4,
        out_shape=[jax.ShapeDtypeStruct((model, width), jnp.float32)] * 3
        + [jax.ShapeDtypeStruct((width, model), jnp.float32)],
        compiler_params=pltpu.CompilerParams(vmem_limit_bytes=8 * MB),
        cost_estimate=cost(4 * model * width, 24 * model * width),
        name="place_attention",
    )(places, *first, *second)


def finish(middles, own_branch, arrived):
    rows, model = own_branch.shape
    calls = len(middles)
    size = rows // calls

    def kernel(*refs):
        b_ref, own_ref, o_ref = refs[calls:]
        for call in range(calls):
            span = slice(call * size, (call + 1) * size)
            total = refs[call][...] + own_ref[span, :] + b_ref[span, :].astype(jnp.float32)
            o_ref[span, :] = total.astype(jnp.bfloat16)

    return pl.pallas_call(
        kernel,
        in_specs=[vmem()] * (calls + 2),
        out_specs=vmem(),
        out_shape=jax.ShapeDtypeStruct((rows, model), jnp.bfloat16),
        compiler_params=pltpu.CompilerParams(vmem_limit_bytes=4 * MB),
        cost_estimate=cost(3 * rows * model, 14 * rows * model),
        name="finish",
    )(*middles, arrived, own_branch)


ORDER = (
    "LNa", "FG", "D0", "LNb", "U0", "D1", "U1", "B1a", "B1b", "B2a", "D2", "B2b", "AG", "D3", "NG",
    "V0", "bands", "P0", "U2", "V1", "P1", "D4", "U3", "P2", "LN1", "E5", "D5", "V2", "P3", "U4",
    "V3", "P4", "D6", "U5", "out", "s0", "V4", "P5", "s1", "plD", "s2", "V5", "U6", "s3", "P6",
    "s4", "V6", "plU", "plP", "fin",
)
BITS = {
    "D": ((1, 4, 2), (8,), (4, 2, 1)),
    "U": ((1, 4, 2), (8,), (4, 2, 1)),
    "P": ((1, 4, 2), (8,), (2, 4, 1)),
    "V": ((1, 2, 4), (8,), (4, 2, 1)),
}


def body(
    inputs, grad_out, page_lengths, gain_one, gain_two, w_query, w_key, w_value, w_out, w_up, w_down, rel_table
):
    count = lax.axis_size("dp")
    tensor_index = lax.axis_index("tensor")
    own_rows, model = inputs.shape
    rows = 2 * own_rows
    half = own_rows // 2
    ff = w_up.shape[1]
    weights = (w_query, w_key, w_value)
    orders = {name: [[bit for bit in bits if bit < count] for bits in lists] for name, lists in BITS.items()}
    pieces = 2 ** len(orders["D"][0])
    pay_places = jnp.stack([place_of(orders[name][0]) for name in "DUPV"])
    got_places = jnp.stack([place_of(orders[name][2][::-1]) for name in "DUPV"])

    info = tensor_index.reshape(1)
    gain_one, gain_two = gain_one.reshape(1, model), gain_two.reshape(1, model)
    inputs, pay_places, got_places, info, gain_one, gain_two, rel_table = tie(
        inputs, pay_places, got_places, info, gain_one, gain_two, rel_table
    )
    normed_own = first_norm(inputs, gain_one)
    normed_peer = swap(normed_own)
    query_own, key_own, value_own = project(normed_own, weights)
    key_marks, query_marks = page_marks(page_lengths[0], rows, info)
    strip = bias_strip(rel_table)
    sent_grad, _ = tie(grad_out, query_own)
    grad_peer = swap(sent_grad)
    query_peer, key_peer, value_peer = project(normed_peer, weights)
    keys, values = (key_own, key_peer), (value_own, value_peer)
    marks = (key_marks, query_marks, strip)

    peer_outs, peer_lses, parts_from_peer = [], [], []
    query = query_peer
    for start in (0, half):
        out, lse, part = attention_forward(
            info, start, half, True, query, keys, values, *marks, w_out, jnp.bfloat16
        )
        peer_outs.append(out)
        peer_lses.append(lse)
        parts_from_peer.append(swap(part))
        query, _ = tie(query_peer, part)
    query, _, grad_peer = tie(query_own, part, grad_peer)
    own_out, own_lse, own_part = attention_forward(
        info, 0, own_rows, False, query, keys, values, *marks, w_out, jnp.float32
    )
    middles, normed_twos, normed_twos_peer = [], [], []
    for side, start in enumerate((0, half)):
        arrived = parts_from_peer[side]
        if side > 0:
            arrived, _ = tie(arrived, normed_two)
        middle, normed_two = second_norm(start, inputs, own_part, arrived, gain_two)
        middles.append(middle)
        normed_twos.append(normed_two)
        normed_twos_peer.append(swap(normed_two))
    own_hidden, own_pre, own_two, own_branch = feed(normed_twos, 0, grad_out, w_up, w_down, jnp.float32)
    last = own_two
    peer_hiddens, peer_pres, peer_branches, twos_from_peer = [], [], [], []
    for side, start in enumerate((0, half)):
        normed_two, _ = tie(normed_twos_peer[side], last)
        hidden, pre, two, branch = feed([normed_two], start, grad_peer, w_up, w_down, jnp.bfloat16)
        peer_hiddens.append(hidden)
        peer_pres.append(pre)
        peer_branches.append(branch)
        twos_from_peer.append(swap(two))
        last = two
    chains = {}
    token = peer_branches[1]
    seeds = None
    backs, branches_peer, grad_qs_own, grad_qs_peer, nears, fars = [], [], [], [], [], []
    heads = rel_table.shape[0]
    got = {}

    def late(value):
        return tie(value, token)[0]

    def halves(name):
        return chains[name].part, chains[name].coming

    for event in ORDER:
        side = 1 if event.endswith("b") else 0
        start = side * half
        if event in ("D0", "U0", "P0", "V0"):
            continue
        if event == "FG":
            payloads = feed_grads(
                pay_places,
                pieces,
                (own_hidden, *peer_hiddens),
                (own_pre, *peer_pres),
                (*normed_twos, *normed_twos_peer),
                (late(grad_out), grad_peer),
            )
            for number, name in enumerate("DU"):
                chains[name] = Reduction(payloads[2 * number : 2 * number + 2], *orders[name], count)
            token = payloads[0]
        elif event[0] in chains and event[1].isdigit():
            chain = chains[event[0]]
            if chain.level < chain.steps:
                chain.after(token)
                token = chain.advance(4600000000 if "P" in chains else 0)
        elif event in ("LNa", "LNb"):
            back = second_norm_back(
                start, own_two, late(twos_from_peer[side]), middles[side], grad_out, gain_two, w_out
            )
            backs.append(back)
            branches_peer.append(swap(back[1]))
            token = back[2]
        elif event in ("B1a", "B1b"):
            result = attention_backward(
                info,
                start,
                False,
                query_own,
                late(backs[side][2]),
                own_out,
                own_lse,
                keys,
                values,
                *marks,
                seeds,
                jnp.float32,
            )
            grad_qs_own.append(result[0])
        elif event in ("B2a", "B2b"):
            result = attention_backward(
                info,
                start,
                True,
                query_peer,
                nt(late(branches_peer[side]), w_out).astype(jnp.bfloat16),
                peer_outs[side],
                peer_lses[side],
                keys,
                values,
                *marks,
                seeds,
                jnp.bfloat16 if side else jnp.float32,
            )
            grad_qs_peer.append(result[0])
        elif event == "AG":
            payloads = attention_grads(
                pay_places,
                pieces,
                (normed_own, normed_peer),
                (*grad_qs_own, grad_qs_peer[0], late(grad_qs_peer[1])),
                *seeds,
                (own_out, *peer_outs),
                (backs[0][1], backs[1][1], *branches_peer),
            )
            for number, name in enumerate("PV"):
                chains[name] = Reduction(payloads[2 * number : 2 * number + 2], *orders[name], count)
            token = payloads[0]
        elif event == "NG":
            token = normed_grad((grad_qs_peer[0], late(grad_qs_peer[1])), *seeds, own_rows, weights)
            one_from_peer = swap(token)
        elif event == "E5":
            arrived = swap(jnp.concatenate([late(peer_branches[0]), peer_branches[1]], axis=0))
        elif event == "bands":
            token = bands = band_sums([late(nears[0]), *nears[1:]], fars)
        elif event == "LN1":
            input_grad, token = first_norm_back(
                grad_qs_own,
                *seeds,
                weights,
                late(one_from_peer),
                inputs,
                (backs[0][0], backs[1][0]),
                gain_one,
            )
            gain_one_part = token
        elif event == "s0":
            token = small = pack_small(late(gain_one_part), [backs[0][3], backs[1][3]], bands, heads)
            other, reach = swap(small), 2
        elif event in ("s1", "s2", "s3", "s4", "fin"):
            token = small = add_small(small, late(other), reach)
            reach = 8
            bit = {"s1": 1, "s2": 2, "s3": 4, "s4": 8, "fin": 0}[event]
            other = dp_swap(small, bit, count) if 0 < bit < count else jnp.zeros_like(small)
        elif event == "out":
            token = out = finish(middles, own_branch, late(arrived))
        elif event == "plD":
            part, coming = halves("D")
            token = down_total = place_feed(
                (part, late(coming)), got_places[0], orders["D"][0], orders["D"][2], (ff, model), lambda b, s: (b, 0)
            )
        elif event == "plU":
            part, coming = halves("U")
            token = up_total = place_feed(
                (part, late(coming)), got_places[1], orders["U"][0], orders["U"][2], (model, ff), lambda b, s: (lax.rem(b, 4), b // 4)
            )
        elif event == "plP":
            part, coming = halves("V")
            totals = place_attention(halves("P"), (part, late(coming)), got_places[2:], (orders["P"], orders["V"]))
            token = totals[0]
        if event[0] == "B" and event[1].isdigit():
            token, seeds = result[0], result[1:3]
            nears.append(result[3])
            fars.append(result[4])

    if count > 16:
        groups = [[j * 16 + i for j in range(count // 16)] for i in range(16)]
        small = lax.psum(small, "dp", axis_index_groups=groups)
    table_total = small[2 : 2 + heads, : rel_table.shape[1]]
    return (
        out,
        input_grad,
        small[0],
        small[1],
        *totals,
        up_total,
        down_total,
        table_total,
    )


def solution(mesh):
    in_specs = (
        P(("dp", "tensor"), None),
        P(("dp", "tensor"), None),
        P("dp", None),
        P(),
        P(),
        P(None, "tensor"),
        P(None, "tensor"),
        P(None, "tensor"),
        P("tensor", None),
        P(None, "tensor"),
        P("tensor", None),
        P("tensor", None),
    )
    out_specs = (
        P(("dp", "tensor"), None),
        P(("dp", "tensor"), None),
        P(),
        P(),
        P(None, "tensor"),
        P(None, "tensor"),
        P(None, "tensor"),
        P("tensor", None),
        P(None, "tensor"),
        P("tensor", None),
        P("tensor", None),
    )
    return jax.shard_map(body, mesh=mesh, in_specs=in_specs, out_specs=out_specs, check_vma=False)
```

```python
import functools
import jax
import jax.numpy as jnp
from jax import lax
from jax.experimental import pallas as pl
from jax.experimental.pallas import tpu as pltpu
from jax.sharding import PartitionSpec as P

HEAD_DIM = 64
BUCKETS = 16
LOG2E = 1.4426950408889634
TILE = 128
QB = 256
MB = 1 << 20


def cost(flops, traffic, share=0.01):
    return pl.CostEstimate(flops=int(share * flops), transcendentals=0, bytes_accessed=int(share * traffic))


def nt(left, right):
    return lax.dot_general(left, right, (((1,), (1,)), ((), ())), preferred_element_type=jnp.float32)


def nn(left, right):
    return jnp.dot(left, right, preferred_element_type=jnp.float32)


def half_of(block, side):
    lanes = lax.broadcasted_iota(jnp.int32, block.shape, 1)
    keep = (lanes < HEAD_DIM) if side == 0 else (lanes >= HEAD_DIM)
    return jnp.where(keep, block, jnp.zeros_like(block))


def tile_pos(local_tile, tensor_index, tiles):
    return lax.rem(local_tile + (tiles // 2) * tensor_index, tiles)


def bias_rows(strip_ref, head, key_tile, query_tile, query_tiles, tensor_index, tiles):
    pieces = []
    key_pos = tile_pos(key_tile, tensor_index, tiles)
    for step in range(query_tiles):
        diff = tile_pos(query_tile + step, tensor_index, tiles) - key_pos
        pieces.append(strip_ref[head, jnp.clip(diff, -2, 2) + 2])
    return jnp.concatenate(pieces, axis=1)


def ones_rows(rows):
    return (lax.broadcasted_iota(jnp.int32, (16, rows), 0) == 0).astype(jnp.bfloat16)


def vmem():
    return pl.BlockSpec(memory_space=pltpu.VMEM)


def smem():
    return pl.BlockSpec(memory_space=pltpu.SMEM)


def rows_of(refs):
    return jnp.concatenate([ref[...] for ref in refs], axis=0) if len(refs) > 1 else refs[0][...]


def attention_forward(info, start, count, peer, query, keys, values, key_marks, query_marks, strip, w_out, part_type):
    own_rows, width = query.shape
    rows = key_marks.shape[0]
    model = w_out.shape[1]
    pairs = width // 128
    tiles = rows // TILE
    query_tiles = count // TILE
    base = (own_rows if peer else 0) + start
    first = base // TILE

    def kernel(info_ref, q_ref, ko_ref, kp_ref, vo_ref, vp_ref, kf_ref, qf_ref, strip_ref, w_ref, o_ref, lse_ref, part_ref):
        tensor_index = info_ref[0]
        marks = qf_ref[base : base + count, :]
        def one_pair(pair, carry):
            lanes = pl.ds(pl.multiple_of(pair * 128, 128), 128)
            keys = jnp.concatenate(
                [jnp.concatenate([ko_ref[:, lanes], kp_ref[:, lanes]], axis=0), kf_ref[...]], axis=1
            )
            value_t = jnp.concatenate([vo_ref[:, lanes].T, vp_ref[:, lanes].T], axis=1)
            outs = []
            for side in range(2):
                query_half = half_of(q_ref[start : start + count, lanes], side)
                raw = nt(keys, jnp.concatenate([query_half, marks], axis=1))
                parts = []
                top = None
                for j in range(tiles):
                    part = raw[j * TILE : (j + 1) * TILE] * (LOG2E * HEAD_DIM**-0.5) + bias_rows(
                        strip_ref, 2 * pair + side, j, first, query_tiles, tensor_index, tiles
                    )
                    parts.append(part)
                    top = part if top is None else jnp.maximum(top, part)
                peak = jnp.max(top, axis=0, keepdims=True)
                weights = jnp.concatenate([jnp.exp2(part - peak).astype(jnp.bfloat16) for part in parts], axis=0)
                left = jnp.concatenate([value_t[side * HEAD_DIM : (side + 1) * HEAD_DIM], ones_rows(rows)], axis=0)
                out_t = nn(left, weights)
                total = out_t[HEAD_DIM : HEAD_DIM + 1]
                outs.append(out_t[:HEAD_DIM] * (1.0 / total))
                lse_ref[pair, side : side + 1, :] = peak + jnp.log2(total)
            o_ref[:, lanes] = jnp.concatenate(outs, axis=0).T.astype(jnp.bfloat16)
            return carry

        lax.fori_loop(0, pairs, one_pair, 0)
        part_ref[...] = nn(o_ref[...], w_ref[...]).astype(part_type)

    return pl.pallas_call(
        kernel,
        in_specs=[smem()] + [vmem()] * 9,
        out_specs=[vmem()] * 3,
        out_shape=[
            jax.ShapeDtypeStruct((count, width), jnp.bfloat16),
            jax.ShapeDtypeStruct((pairs, 2, count), jnp.float32),
            jax.ShapeDtypeStruct((count, model), part_type),
        ],
        compiler_params=pltpu.CompilerParams(vmem_limit_bytes=8 * MB),
        cost_estimate=cost(9 * 10**9 * count // own_rows, 8 * rows * width),
        name="attend",
    )(info, query, *keys, *values, key_marks, query_marks, strip, w_out)


def attention_backward(
    info, start, peer, query, grad_out, out, lse, keys, values, key_marks, query_marks, strip, seeds, sum_type
):
    own_rows, width = query.shape
    count = grad_out.shape[0]
    rows = key_marks.shape[0]
    pairs = width // 128
    tiles = rows // TILE
    query_tiles = count // TILE
    base = (own_rows if peer else 0) + start
    first = base // TILE
    shift = start if out.shape[0] > count else 0
    seeded = seeds is not None
    scale = HEAD_DIM**-0.5

    def kernel(info_ref, q_ref, do_ref, o_ref, lse_ref, ko_ref, kp_ref, vo_ref, vp_ref, kf_ref, qf_ref, strip_ref, *rest):
        if seeded:
            dk_seed, dv_seed, *rest = rest
        dq_ref, dk_ref, dv_ref, near_ref, far_ref, grads_ref = rest
        tensor_index = info_ref[0]
        query_marks = qf_ref[base : base + count, :]
        marks = (
            lax.broadcasted_iota(jnp.int32, (16, rows), 1) // TILE
            == lax.broadcasted_iota(jnp.int32, (16, rows), 0)
        ).astype(jnp.bfloat16)
        key_pos = tile_pos(lax.broadcasted_iota(jnp.int32, (8, TILE), 0), tensor_index, tiles)
        def one_pair(pair, carry):
            lanes = pl.ds(pl.multiple_of(pair * 128, 128), 128)
            key_pair = jnp.concatenate([ko_ref[:, lanes], kp_ref[:, lanes]], axis=0)
            keys = jnp.concatenate([key_pair, kf_ref[...]], axis=1)
            key_t = key_pair.T
            values = jnp.concatenate([vo_ref[:, lanes], vp_ref[:, lanes]], axis=0)
            inner = do_ref[:, lanes].astype(jnp.float32) * o_ref[shift : shift + count, lanes].astype(jnp.float32)
            inner = inner.T
            probs, grads, grad_qs, query_halves, do_halves = [], [], [], [], []
            for side in range(2):
                head = 2 * pair + side
                query_half = half_of(q_ref[start : start + count, lanes], side)
                do_half = half_of(do_ref[:, lanes], side)
                query_halves.append(query_half)
                do_halves.append(do_half)
                raw = nt(keys, jnp.concatenate([query_half, query_marks], axis=1))
                grad_prob = nt(values, do_half)
                lse = lse_ref[pair, side : side + 1, shift : shift + count]
                delta = jnp.sum(inner[side * HEAD_DIM : (side + 1) * HEAD_DIM], axis=0, keepdims=True)
                prob_parts, grad_parts = [], []
                for j in range(tiles):
                    span = slice(j * TILE, (j + 1) * TILE)
                    bias = bias_rows(strip_ref, head, j, first, query_tiles, tensor_index, tiles)
                    prob = jnp.exp2(raw[span] * (LOG2E * scale) + (bias - lse))
                    grad = (prob * (grad_prob[span] - delta)).astype(jnp.bfloat16)
                    grads_ref[side, span, :] = grad
                    prob_parts.append(prob.astype(jnp.bfloat16))
                    grad_parts.append(grad)
                probs.append(jnp.concatenate(prob_parts, axis=0))
                grad_all = jnp.concatenate(grad_parts, axis=0)
                grads.append(grad_all)
                left = jnp.concatenate([key_t[side * HEAD_DIM : (side + 1) * HEAD_DIM], marks], axis=0)
                grad_q = nn(left, grad_all)
                grad_qs.append(grad_q[:HEAD_DIM])
                sums = grad_q[HEAD_DIM : HEAD_DIM + 8]
                before, after = jnp.zeros((8, TILE), jnp.float32), jnp.zeros((8, TILE), jnp.float32)
                for part in range(query_tiles):
                    query_pos = tile_pos(first + part, tensor_index, tiles)
                    piece = sums[:, part * TILE : (part + 1) * TILE]
                    before = before + jnp.where(key_pos <= query_pos - 2, piece, 0.0)
                    after = after + jnp.where(key_pos >= query_pos + 2, piece, 0.0)
                far_ref[head, 0] = before
                far_ref[head, 1] = after
                for diff in (-1, 0, 1):
                    near = None
                    for part in range(query_tiles):
                        wanted = tile_pos(first + part, tensor_index, tiles) - diff
                        valid = jnp.logical_and(wanted >= 0, wanted < tiles)
                        local = tile_pos(jnp.clip(wanted, 0, tiles - 1), tensor_index, tiles)
                        block = grads_ref[
                            side,
                            pl.ds(pl.multiple_of(local * TILE, TILE), TILE),
                            part * TILE : (part + 1) * TILE,
                        ].astype(jnp.float32)
                        block = block if diff == 0 else jnp.where(valid, block, 0.0)
                        near = block if near is None else near + block
                    near_ref[head, diff + 1] = near
            dv = nn(jnp.concatenate(probs, axis=1), jnp.concatenate(do_halves, axis=0))
            dk = nn(jnp.concatenate(grads, axis=1), jnp.concatenate(query_halves, axis=0)) * scale
            if seeded:
                dv = dv + dv_seed[:, lanes]
                dk = dk + dk_seed[:, lanes]
            dv_ref[:, lanes] = dv.astype(sum_type)
            dk_ref[:, lanes] = dk.astype(sum_type)
            dq_ref[:, lanes] = (jnp.concatenate(grad_qs, axis=0).T * scale).astype(jnp.bfloat16)
            return carry

        lax.fori_loop(0, pairs, one_pair, 0)

    return pl.pallas_call(
        kernel,
        in_specs=[smem()] + [vmem()] * (13 if seeded else 11),
        out_specs=[vmem()] * 5,
        out_shape=[
            jax.ShapeDtypeStruct((count, width), jnp.bfloat16),
            jax.ShapeDtypeStruct((rows, width), sum_type),
            jax.ShapeDtypeStruct((rows, width), sum_type),
            jax.ShapeDtypeStruct((2 * pairs, 3, TILE, TILE), jnp.float32),
            jax.ShapeDtypeStruct((2 * pairs, 2, 8, TILE), jnp.float32),
        ],
        scratch_shapes=[pltpu.VMEM((2, rows, count), jnp.bfloat16)],
        compiler_params=pltpu.CompilerParams(vmem_limit_bytes=14 * MB),
        cost_estimate=cost(18 * 10**9 * count // own_rows, 20 * rows * width),
        name="attend_back",
    )(info, query, grad_out, out, lse, *keys, *values, key_marks, query_marks, strip, *(seeds or ()))


def band_levels(diff):
    delta = diff * TILE + (
        lax.broadcasted_iota(jnp.int32, (TILE, TILE), 1) - lax.broadcasted_iota(jnp.int32, (TILE, TILE), 0)
    )
    distance = jnp.abs(delta) + 1
    level = jnp.zeros_like(delta)
    for exponent in range(1, BUCKETS // 2):
        level = level + (distance >= 2**exponent).astype(jnp.int32)
    return level + (BUCKETS // 2) * (delta < 0).astype(jnp.int32)


def band_sums(nears, fars):
    heads = nears[0].shape[0]
    calls = len(nears)

    def kernel(*refs):
        near_refs, far_refs, o_ref = refs[:calls], refs[calls : 2 * calls], refs[-1]
        rows = [[jnp.zeros((1, TILE), jnp.float32) for _ in range(BUCKETS)] for _ in range(heads)]
        for head in range(heads):
            far = sum(ref[head] for ref in far_refs)
            rows[head][BUCKETS // 2 - 1] += jnp.sum(far[0], axis=0, keepdims=True)
            rows[head][BUCKETS - 1] += jnp.sum(far[1], axis=0, keepdims=True)
        for diff, present in ((0, [*range(8), *range(9, 16)]), (1, range(1, 8)), (-1, range(9, 16))):
            level = band_levels(diff)
            for head in range(heads):
                near = sum(ref[head, diff + 1] for ref in near_refs)
                for bucket in present:
                    rows[head][bucket] += jnp.sum(jnp.where(level == bucket, near, 0.0), axis=0, keepdims=True)
        at = lax.broadcasted_iota(jnp.int32, (BUCKETS, TILE), 0) == lax.broadcasted_iota(
            jnp.int32, (BUCKETS, TILE), 1
        )
        o_ref[...] = jnp.zeros_like(o_ref)
        for head in range(heads):
            sums = jnp.sum(jnp.concatenate(rows[head], axis=0), axis=1, keepdims=True)
            o_ref[head : head + 1, :] = jnp.sum(jnp.where(at, sums, 0.0), axis=0, keepdims=True)

    return pl.pallas_call(
        kernel,
        in_specs=[vmem()] * (2 * calls),
        out_specs=vmem(),
        out_shape=jax.ShapeDtypeStruct((8, TILE), jnp.float32),
        compiler_params=pltpu.CompilerParams(vmem_limit_bytes=8 * MB),
        cost_estimate=cost(heads * 3 * 16 * TILE * TILE, heads * 8 * TILE * TILE),
        name="band_sums",
    )(*nears, *fars)


def pack_small(gain_one_part, gain_two_parts, table, heads):
    model = gain_one_part.shape[1]
    calls = len(gain_two_parts)

    def kernel(*refs):
        one_ref, table_ref, o_ref = refs[0], refs[calls + 1], refs[calls + 2]
        o_ref[...] = jnp.zeros_like(o_ref)
        o_ref[0:1, :] = jnp.sum(one_ref[...], axis=0, keepdims=True)
        two = sum(ref[...] for ref in refs[1 : calls + 1])
        o_ref[1:2, :] = jnp.sum(two, axis=0, keepdims=True)
        o_ref[2 : 2 + heads, :TILE] = table_ref[:heads, :]

    return pl.pallas_call(
        kernel,
        in_specs=[vmem()] * (calls + 2),
        out_specs=vmem(),
        out_shape=jax.ShapeDtypeStruct((8, model), jnp.float32),
        compiler_params=pltpu.CompilerParams(vmem_limit_bytes=2 * MB),
        cost_estimate=cost(1000, 1000),
        name="pack_small",
    )(gain_one_part, *gain_two_parts, table)


def add_small(mine, theirs, rows):
    def kernel(a_ref, b_ref, o_ref):
        line = lax.broadcasted_iota(jnp.int32, a_ref.shape, 0)
        o_ref[...] = a_ref[...] + jnp.where(line < rows, b_ref[...], 0.0)

    return pl.pallas_call(
        kernel,
        in_specs=[vmem()] * 2,
        out_specs=vmem(),
        out_shape=jax.ShapeDtypeStruct(mine.shape, jnp.float32),
        compiler_params=pltpu.CompilerParams(vmem_limit_bytes=2 * MB),
        cost_estimate=cost(1000, 1000),
        name="add_small",
    )(mine, theirs)


def bias_strip(rel_table):
    heads = rel_table.shape[0]

    def kernel(t_ref, o_ref):
        table = t_ref[...].astype(jnp.float32) * LOG2E
        levels = [band_levels(diff) for diff in (-1, 0, 1)]
        masks = [[level == bucket for bucket in range(BUCKETS)] for level in levels]
        for head in range(heads):
            entries = [table[head : head + 1, bucket : bucket + 1] for bucket in range(BUCKETS)]
            for slot, present in enumerate((range(9, 16), [*range(8), *range(9, 16)], range(1, 8))):
                tile = jnp.zeros((TILE, TILE), jnp.float32)
                for bucket in present:
                    tile = jnp.where(masks[slot][bucket], entries[bucket], tile)
                o_ref[head, slot + 1] = tile
            o_ref[head, 0] = jnp.broadcast_to(entries[15], (TILE, TILE))
            o_ref[head, 4] = jnp.broadcast_to(entries[7], (TILE, TILE))

    return pl.pallas_call(
        kernel,
        in_specs=[vmem()],
        out_specs=vmem(),
        out_shape=jax.ShapeDtypeStruct((heads, 5, TILE, TILE), jnp.float32),
        compiler_params=pltpu.CompilerParams(vmem_limit_bytes=8 * MB),
        cost_estimate=cost(10**9, 0, 1),
        name="bias_strip",
    )(rel_table)


def page_marks(lengths, rows, tensor_index):
    slots = lengths.shape[0]

    def kernel(len_ref, t_ref, k_ref, q_ref):
        place = lax.broadcasted_iota(jnp.int32, (rows, 128), 0) + (rows // 2) * t_ref[0]
        place = jnp.where(place >= rows, place - rows, place)
        lanes = lax.broadcasted_iota(jnp.int32, (rows, 128), 1)
        end = jnp.int32(0)
        page = jnp.zeros((rows, 128), jnp.int32)
        for slot in range(slots):
            end = end + len_ref[slot]
            page = page + (place >= end).astype(jnp.int32)
        k_ref[...] = jnp.where(page == lanes, 1.0, 0.0).astype(jnp.bfloat16)
        other = jnp.logical_and(page != lanes, lanes < slots)
        q_ref[...] = jnp.where(other, -1e30, 0.0).astype(jnp.bfloat16)

    return pl.pallas_call(
        kernel,
        in_specs=[smem(), smem()],
        out_specs=[vmem()] * 2,
        out_shape=[jax.ShapeDtypeStruct((rows, 128), jnp.bfloat16)] * 2,
        compiler_params=pltpu.CompilerParams(vmem_limit_bytes=8 * MB),
        cost_estimate=cost(10**9, 0, 1),
        name="page_marks",
    )(lengths, tensor_index)


def tn(left, right):
    return lax.dot_general(left, right, (((0,), (0,)), ((), ())), preferred_element_type=jnp.float32)


def standardize(values):
    centred = values - jnp.mean(values, axis=-1, keepdims=True)
    variance = jnp.mean(centred * centred, axis=-1, keepdims=True)
    inverse = lax.rsqrt(variance + 1e-05)
    return centred * inverse, inverse


def norm_back(grad, standard, inverse, gain):
    scaled = grad * gain
    mean = jnp.mean(scaled, axis=-1, keepdims=True)
    slope = jnp.mean(scaled * standard, axis=-1, keepdims=True)
    return inverse * (scaled - mean - standard * slope)


def fold_rows(values):
    return jnp.sum(values.reshape(-1, 8, values.shape[-1]), axis=0)


def first_norm(inputs, gain):
    rows, model = inputs.shape

    def kernel(x_ref, g_ref, o_ref):
        gain = g_ref[...].astype(jnp.float32)
        for start in range(0, rows, 128):
            standard, _ = standardize(x_ref[start : start + 128, :].astype(jnp.float32))
            o_ref[start : start + 128, :] = (standard * gain).astype(jnp.bfloat16)

    return pl.pallas_call(
        kernel,
        in_specs=[vmem()] * 2,
        out_specs=vmem(),
        out_shape=jax.ShapeDtypeStruct((rows, model), jnp.bfloat16),
        compiler_params=pltpu.CompilerParams(vmem_limit_bytes=6 * MB),
        cost_estimate=cost(rows * model * 8, 4 * rows * model),
        name="first_norm",
    )(inputs, gain)


def project(normed, weights):
    rows, model = normed.shape
    width = weights[0].shape[1]

    def kernel(x_ref, *refs):
        for w_ref, o_ref in zip(refs[:3], refs[3:]):
            o_ref[...] = nn(x_ref[...], w_ref[...]).astype(jnp.bfloat16)

    return pl.pallas_call(
        kernel,
        in_specs=[vmem()] * 4,
        out_specs=[vmem()] * 3,
        out_shape=[jax.ShapeDtypeStruct((rows, width), jnp.bfloat16)] * 3,
        compiler_params=pltpu.CompilerParams(vmem_limit_bytes=4 * MB),
        cost_estimate=cost(6 * rows * model * width, 0, 1),
        name="project",
    )(normed, *weights)


def second_norm(start, inputs, own_part, peer_part, gain):
    rows, model = peer_part.shape

    def kernel(x_ref, a_ref, b_ref, g_ref, m_ref, o_ref):
        gain = g_ref[...].astype(jnp.float32)
        for offset in range(0, rows, 128):
            span = slice(offset, offset + 128)
            wide = slice(start + offset, start + offset + 128)
            middle = x_ref[wide, :].astype(jnp.float32) + a_ref[wide, :] + b_ref[span, :].astype(jnp.float32)
            m_ref[span, :] = middle
            standard, _ = standardize(middle)
            o_ref[span, :] = (standard * gain).astype(jnp.bfloat16)

    return pl.pallas_call(
        kernel,
        in_specs=[vmem()] * 4,
        out_specs=[vmem()] * 2,
        out_shape=[
            jax.ShapeDtypeStruct((rows, model), jnp.float32),
            jax.ShapeDtypeStruct((rows, model), jnp.bfloat16),
        ],
        compiler_params=pltpu.CompilerParams(vmem_limit_bytes=8 * MB),
        cost_estimate=cost(rows * model * 8, 14 * rows * model),
        name="second_norm",
    )(inputs, own_part, peer_part, gain)


FF_CHUNK = 512


def feed(normeds, start, grads, w_up, w_down, sum_type):
    rows = sum(n.shape[0] for n in normeds)
    model, ff = w_up.shape
    calls = len(normeds)

    def kernel(*refs):
        g_ref, u_ref, d_ref, h_ref, p_ref, gn_ref, bt_ref = refs[calls:]
        normed = rows_of(refs[:calls])
        for begin in range(0, ff, FF_CHUNK):
            span = slice(begin, begin + FF_CHUNK)
            pre = nn(normed, u_ref[:, span])
            grad_hidden = nt(g_ref[start : start + rows, :], d_ref[span, :])
            square = pre * pre
            bent = jnp.tanh(pre * (0.7978845608 + (0.7978845608 * 0.044715) * square))
            gate = 0.5 + 0.5 * bent
            h_ref[:, span] = (pre * gate).astype(jnp.bfloat16)
            slope = gate + pre * (0.5 - 0.5 * bent * bent) * (
                0.7978845608 + (3 * 0.7978845608 * 0.044715) * square
            )
            p_ref[:, span] = (grad_hidden * slope).astype(jnp.bfloat16)
        gn_ref[...] = nt(p_ref[...], u_ref[...]).astype(sum_type)
        bt_ref[...] = nn(h_ref[...], d_ref[...]).astype(sum_type)

    return pl.pallas_call(
        kernel,
        in_specs=[vmem()] * (calls + 3),
        out_specs=[vmem()] * 4,
        out_shape=[jax.ShapeDtypeStruct((rows, ff), jnp.bfloat16)] * 2
        + [jax.ShapeDtypeStruct((rows, model), sum_type)] * 2,
        compiler_params=pltpu.CompilerParams(vmem_limit_bytes=8 * MB),
        cost_estimate=cost(8 * rows * model * ff, 4 * model * ff + 8 * rows * ff),
        name="feed",
    )(*normeds, grads, w_up, w_down)


def grouped_call(kernel, groups, **options):
    sizes = [len(g) for g in groups]

    def body(place_ref, *refs):
        lists, at = [], 0
        for size in sizes:
            lists.append(refs[at : at + size])
            at += size
        kernel(place_ref, *lists, *refs[at:])

    return pl.pallas_call(body, in_specs=[smem()] + [vmem()] * sum(sizes), **options)


def turned(refs, span=slice(None)):
    return jnp.concatenate([ref[:, span].T for ref in refs], axis=1)


def feed_grads(places, pieces, hiddens, grad_pres, normeds, grads):
    rows = sum(h.shape[0] for h in hiddens)
    ff = hiddens[0].shape[1]
    model = normeds[0].shape[1]
    size = ff // pieces
    fine = model // size

    def kernel(place_ref, h_refs, p_refs, n_refs, g_refs, *rest):
        down_ref, up_ref = rest[4:]
        grad = rows_of(g_refs)
        normed_t = turned(n_refs)
        for part in range(ff // model):
            span = slice(part * model, (part + 1) * model)
            down = nn(turned(h_refs, span), grad).astype(jnp.bfloat16)
            for k in range(fine):
                store_piece(down_ref, place_ref[0], pieces, part * fine + k, size, down[k * size : (k + 1) * size])
        for part in range(ff // model):
            span = slice(part * model, (part + 1) * model)
            pre = jnp.concatenate([ref[:, span] for ref in p_refs], axis=0)
            up = nn(normed_t, pre).astype(jnp.bfloat16)
            for k in range(fine):
                store_piece(up_ref, place_ref[1], pieces, part * fine + k, size, up[k * size : (k + 1) * size])
        for number, out_ref in enumerate(rest[:4]):
            out_ref[...] = (down_ref, up_ref)[number // 2][number % 2]

    groups = (hiddens, grad_pres, normeds, grads)
    return grouped_call(
        kernel,
        groups,
        out_specs=[vmem()] * 4,
        out_shape=[jax.ShapeDtypeStruct((ff // 2, model), jnp.bfloat16)] * 4,
        scratch_shapes=[pltpu.VMEM((2, ff // 2, model), jnp.bfloat16)] * 2,
        compiler_params=pltpu.CompilerParams(vmem_limit_bytes=16 * MB),
        cost_estimate=cost(4 * rows * model * ff, 4 * rows * ff + 4 * ff * model),
        name="feed_grads",
    )(places, *[a for g in groups for a in g])


def second_norm_back(start, own_part, peer_part, middle, grad_out, gain, w_out):
    rows, model = middle.shape
    width = w_out.shape[0]

    def kernel(a_ref, b_ref, m_ref, g_ref, gain_ref, w_ref, gm_ref, gb_ref, ga_ref, gain_out):
        gain = gain_ref[...].astype(jnp.float32)
        part = jnp.zeros((8, model), jnp.float32)
        for offset in range(0, rows, 128):
            span = slice(offset, offset + 128)
            wide = slice(start + offset, start + offset + 128)
            grad = a_ref[wide, :] + b_ref[span, :].astype(jnp.float32)
            standard, inverse = standardize(m_ref[span, :])
            result = g_ref[wide, :].astype(jnp.float32) + norm_back(grad, standard, inverse, gain)
            gm_ref[span, :] = result
            gb_ref[span, :] = result.astype(jnp.bfloat16)
            part = part + fold_rows(grad * standard)
        gain_out[...] = part
        ga_ref[...] = nt(gb_ref[...], w_ref[...]).astype(jnp.bfloat16)

    return pl.pallas_call(
        kernel,
        in_specs=[vmem()] * 6,
        out_specs=[vmem()] * 4,
        out_shape=[
            jax.ShapeDtypeStruct((rows, model), jnp.float32),
            jax.ShapeDtypeStruct((rows, model), jnp.bfloat16),
            jax.ShapeDtypeStruct((rows, width), jnp.bfloat16),
            jax.ShapeDtypeStruct((8, model), jnp.float32),
        ],
        compiler_params=pltpu.CompilerParams(vmem_limit_bytes=10 * MB),
        cost_estimate=cost(10**11, 0, 1 if start else 0.0),
        name="second_norm_back",
    )(own_part, peer_part, middle, grad_out, gain, w_out)


def normed_grad(grad_qs, grad_k, grad_v, offset, weights):
    rows = sum(q.shape[0] for q in grad_qs)
    model, width = weights[0].shape
    calls = len(grad_qs)

    def kernel(*refs):
        k_ref, v_ref, wq_ref, wk_ref, wv_ref, o_ref = refs[calls:]
        span = slice(offset, offset + rows)
        total = nt(rows_of(refs[:calls]), wq_ref[...])
        total = total + nt(k_ref[span, :], wk_ref[...]) + nt(v_ref[span, :], wv_ref[...])
        o_ref[...] = total.astype(jnp.bfloat16)

    return pl.pallas_call(
        kernel,
        in_specs=[vmem()] * (calls + 5),
        out_specs=vmem(),
        out_shape=jax.ShapeDtypeStruct((rows, model), jnp.bfloat16),
        compiler_params=pltpu.CompilerParams(vmem_limit_bytes=6 * MB),
        cost_estimate=cost(10**11, 0, 1),
        name="normed_grad",
    )(*grad_qs, grad_k, grad_v, *weights)


def first_norm_back(grad_qs, grad_k, grad_v, weights, peer_part, inputs, middles, gain):
    rows, model = inputs.shape
    width = weights[0].shape[1]
    calls = len(grad_qs)
    size = rows // calls

    def kernel(*refs):
        q_refs, m_refs = refs[:calls], refs[calls : 2 * calls]
        k_ref, v_ref, wq_ref, wk_ref, wv_ref, b_ref, x_ref, gain_ref, o_ref, gain_out = refs[2 * calls :]
        gain = gain_ref[...].astype(jnp.float32)
        part = jnp.zeros((8, model), jnp.float32)
        for call in range(calls):
            span = slice(call * size, (call + 1) * size)
            grad = nt(q_refs[call][...], wq_ref[...])
            grad = grad + nt(k_ref[span, :], wk_ref[...]) + nt(v_ref[span, :], wv_ref[...])
            grad = grad + b_ref[span, :].astype(jnp.float32)
            standard, inverse = standardize(x_ref[span, :].astype(jnp.float32))
            result = m_refs[call][...] + norm_back(grad, standard, inverse, gain)
            o_ref[span, :] = result.astype(jnp.bfloat16)
            part = part + fold_rows(grad * standard)
        gain_out[...] = part

    return pl.pallas_call(
        kernel,
        in_specs=[vmem()] * (2 * calls + 8),
        out_specs=[vmem()] * 2,
        out_shape=[
            jax.ShapeDtypeStruct((rows, model), jnp.bfloat16),
            jax.ShapeDtypeStruct((8, model), jnp.float32),
        ],
        compiler_params=pltpu.CompilerParams(vmem_limit_bytes=10 * MB),
        cost_estimate=cost(6 * rows * model * width, 12 * rows * model),
        name="first_norm_back",
    )(*grad_qs, *middles, grad_k, grad_v, *weights, peer_part, inputs, gain)


def store_piece(ref, place, pieces, block, size, values):
    half = pieces // 2
    spot = jnp.bitwise_xor(place, block)
    ref[spot // half, pl.ds(pl.multiple_of(lax.rem(spot, half) * size, size), size), :] = values


def attention_grads(places, pieces, normeds, grad_qs, grad_k, grad_v, outs, branches):
    rows, width = grad_k.shape
    model = normeds[0].shape[1]
    size = 2 * model // pieces
    fine = model // size

    def kernel(place_ref, n_refs, q_refs, k_refs, v_refs, o_refs, b_refs, *rest):
        first_ref, second_ref = rest[4:]
        normed_t = turned(n_refs)
        for ref, which, base, right in (
            (first_ref, 2, 0, rows_of(q_refs)),
            (first_ref, 2, fine, rows_of(k_refs)),
            (second_ref, 3, 0, rows_of(v_refs)),
        ):
            result = nn(normed_t, right).astype(jnp.bfloat16)
            for k in range(fine):
                store_piece(ref, place_ref[which], pieces, base + k, size, result[k * size : (k + 1) * size])
        result = nn(turned(o_refs), rows_of(b_refs)).astype(jnp.bfloat16)
        for side in range(2):
            for k in range(fine // 2):
                store_piece(
                    second_ref,
                    place_ref[3],
                    pieces,
                    fine + side * (fine // 2) + k,
                    size,
                    result[k * size : (k + 1) * size, side * width : (side + 1) * width],
                )
        for number, out_ref in enumerate(rest[:4]):
            out_ref[...] = (first_ref, second_ref)[number // 2][number % 2]

    groups = (normeds, grad_qs, (grad_k,), (grad_v,), outs, branches)
    return grouped_call(
        kernel,
        groups,
        out_specs=[vmem()] * 4,
        out_shape=[jax.ShapeDtypeStruct((model, width), jnp.bfloat16)] * 4,
        scratch_shapes=[pltpu.VMEM((2, model, width), jnp.bfloat16)] * 2,
        compiler_params=pltpu.CompilerParams(vmem_limit_bytes=12 * MB),
        cost_estimate=cost(8 * rows * model * width, 6 * rows * model),
        name="attention_grads",
    )(places, *[a for g in groups for a in g])


def swap(values):
    return lax.ppermute(values, "tensor", [(0, 1), (1, 0)])


def dp_swap(values, bit, count):
    return lax.ppermute(values, "dp", [(i, i ^ bit) for i in range(count)])


def place_of(bits):
    index = lax.axis_index("dp")
    place = jnp.int32(0)
    for bit in bits:
        place = place * 2 + lax.rem(index // bit, 2)
    return place


def owner_place(block, bits, gather):
    place = 0
    for bit in reversed(gather):
        place = place * 2 + (block // 2 ** (len(bits) - 1 - bits.index(bit))) % 2
    return place


def add_rows(mine, theirs, split, weight):
    rows, width = mine.shape
    size = rows // 2 if split else rows

    def kernel(a_ref, b_ref, *out_refs):
        for part, out_ref in enumerate(out_refs):
            span = slice(part * size, (part + 1) * size)
            total = a_ref[span, :].astype(jnp.float32) + b_ref[span, :].astype(jnp.float32)
            out_ref[...] = total.astype(jnp.bfloat16)

    count = 2 if split else 1
    return pl.pallas_call(
        kernel,
        in_specs=[vmem()] * 2,
        out_specs=[vmem()] * count,
        out_shape=[jax.ShapeDtypeStruct((size, width), jnp.bfloat16)] * count,
        compiler_params=pltpu.CompilerParams(vmem_limit_bytes=4 * MB),
        cost_estimate=cost(weight, 0, 1),
        name="add_rows",
    )(mine, theirs)


def join_rows(upper, lower, weight):
    rows, width = upper.shape

    def kernel(a_ref, b_ref, o_ref):
        o_ref[:rows, :] = a_ref[...]
        o_ref[rows:, :] = b_ref[...]

    return pl.pallas_call(
        kernel,
        in_specs=[vmem()] * 2,
        out_specs=vmem(),
        out_shape=jax.ShapeDtypeStruct((2 * rows, width), jnp.bfloat16),
        compiler_params=pltpu.CompilerParams(vmem_limit_bytes=2 * MB),
        cost_estimate=cost(weight, 0, 1),
        name="join_rows",
    )(upper, lower)


class Reduction:
    def __init__(self, halves, bits, last, gather, count):
        self.keep, self.bits, self.last, self.gather, self.count = halves[0], bits, last, gather, count
        self.level = 0
        self.coming = dp_swap(halves[1], bits[0], count)
        self.part = None

    @property
    def steps(self):
        return len(self.bits) + len(self.last) + len(self.gather) - 1

    def after(self, token):
        if self.level < len(self.bits) + len(self.last):
            self.keep, _ = tie(self.keep, token)
        else:
            self.part, _ = tie(self.part, token)

    def advance(self, weight):
        sums = len(self.bits) + len(self.last)
        if self.level < sums:
            split = self.level + 1 < len(self.bits)
            self.part, *sent = add_rows(self.keep, self.coming, split, weight)
        else:
            self.part = join_rows(self.part, self.coming, weight)
        self.level += 1
        if self.level == sums:
            done = 2**sums
            if done < self.count:
                groups = [[j * done + i for j in range(self.count // done)] for i in range(done)]
                self.part = lax.psum(self.part, "dp", axis_index_groups=groups)
        if self.level < len(self.bits):
            self.keep = self.part
            self.coming = dp_swap(sent[0], self.bits[self.level], self.count)
        elif self.level < sums:
            self.keep = self.part
            self.coming = dp_swap(self.part, self.last[0], self.count)
        else:
            self.coming = dp_swap(self.part, self.gather[self.level - sums], self.count)
        return self.part


def tie(*values):
    return lax.optimization_barrier(values)


def place_feed(halves, place, bits, gather, shape, along):
    pieces = 2 ** len(bits)
    rows, width = halves[0].shape
    size = 2 * rows // pieces

    def kernel(place_ref, a_ref, b_ref, out_ref, wide_ref, sems):
        copies = []
        for k in range(pieces):
            spot = jnp.bitwise_xor(place_ref[0], owner_place(k, bits, gather))
            span = pl.ds(pl.multiple_of(lax.rem(spot, pieces // 2) * size, size), size)
            values = jnp.where(spot < pieces // 2, a_ref[span, :], b_ref[span, :])
            wide_ref[k] = values.astype(jnp.float32)
            row, column = k % along, k // along
            target = out_ref.at[pl.ds(row * size, size), pl.ds(column * width, width)]
            copies.append(pltpu.make_async_copy(wide_ref.at[k], target, sems.at[k]))
            copies[-1].start()
        for copy in copies:
            copy.wait()

    return pl.pallas_call(
        kernel,
        in_specs=[smem(), vmem(), vmem()],
        out_specs=pl.BlockSpec(memory_space=pltpu.HBM),
        out_shape=jax.ShapeDtypeStruct(shape, jnp.float32),
        scratch_shapes=[pltpu.VMEM((pieces, size, width), jnp.float32), pltpu.SemaphoreType.DMA((pieces,))],
        compiler_params=pltpu.CompilerParams(vmem_limit_bytes=8 * MB),
        cost_estimate=cost(rows * width, 12 * rows * width),
        name="place_feed",
    )(place.reshape(1), *halves)


def place_attention(first, second, places, orders):
    pieces = 2 ** len(orders[0][0])
    model, width = first[0].shape
    size = 2 * model // pieces
    fine = model // size

    def kernel(place_ref, fa_ref, fb_ref, sa_ref, sb_ref, q_ref, k_ref, v_ref, o_ref, wide_ref, sems):
        copies = []
        for out_ref, a_ref, b_ref, which, base in (
            (q_ref, fa_ref, fb_ref, 0, 0),
            (k_ref, fa_ref, fb_ref, 0, fine),
            (v_ref, sa_ref, sb_ref, 1, 0),
            (o_ref, sa_ref, sb_ref, 1, fine),
        ):
            for k in range(fine):
                spot = jnp.bitwise_xor(place_ref[which], owner_place(base + k, orders[which][0], orders[which][2]))
                rows = pl.ds(pl.multiple_of(lax.rem(spot, pieces // 2) * size, size), size)
                number = len(copies)
                values = jnp.where(spot < pieces // 2, a_ref[rows, :], b_ref[rows, :])
                wide_ref[number] = values.astype(jnp.float32)
                row, column = (k % (fine // 2), k // (fine // 2)) if out_ref is o_ref else (k, 0)
                target = out_ref.at[pl.ds(row * size, size), pl.ds(column * width, width)]
                copies.append(pltpu.make_async_copy(wide_ref.at[number], target, sems.at[number]))
                copies[-1].start()
        for copy in copies:
            copy.wait()

    return pl.pallas_call(
        kernel,
        in_specs=[smem()] + [vmem()] * 4,
        out_specs=[pl.BlockSpec(memory_space=pltpu.HBM)] * 4,
        out_shape=[jax.ShapeDtypeStruct((model, width), jnp.float32)] * 3
        + [jax.ShapeDtypeStruct((width, model), jnp.float32)],
        scratch_shapes=[pltpu.VMEM((4 * fine, size, width), jnp.float32), pltpu.SemaphoreType.DMA((4 * fine,))],
        compiler_params=pltpu.CompilerParams(vmem_limit_bytes=8 * MB),
        cost_estimate=cost(4 * model * width, 24 * model * width),
        name="place_attention",
    )(places, *first, *second)


def finish(middles, own_branch, arrived):
    rows, model = own_branch.shape
    calls = len(middles)
    size = rows // calls

    def kernel(*refs):
        b_ref, own_ref, o_ref = refs[calls:]
        for call in range(calls):
            span = slice(call * size, (call + 1) * size)
            total = refs[call][...] + own_ref[span, :] + b_ref[span, :].astype(jnp.float32)
            o_ref[span, :] = total.astype(jnp.bfloat16)

    return pl.pallas_call(
        kernel,
        in_specs=[vmem()] * (calls + 2),
        out_specs=vmem(),
        out_shape=jax.ShapeDtypeStruct((rows, model), jnp.bfloat16),
        compiler_params=pltpu.CompilerParams(vmem_limit_bytes=4 * MB),
        cost_estimate=cost(3 * rows * model, 14 * rows * model),
        name="finish",
    )(*middles, arrived, own_branch)


ORDER = (
    "LNa", "FG", "D0", "LNb", "U0", "D1", "U1", "B1a", "B1b", "B2a", "D2", "B2b", "AG", "D3", "NG",
    "V0", "bands", "P0", "U2", "V1", "P1", "D4", "U3", "P2", "LN1", "E5", "D5", "V2", "P3", "U4",
    "V3", "P4", "D6", "U5", "out", "s0", "V4", "P5", "s1", "plD", "s2", "V5", "U6", "s3", "P6",
    "s4", "V6", "plU", "plP", "fin",
)
BITS = {
    "D": ((1, 4, 2), (8,), (4, 2, 1)),
    "U": ((1, 4, 2), (8,), (4, 2, 1)),
    "P": ((1, 4, 2), (8,), (2, 4, 1)),
    "V": ((1, 2, 4), (8,), (4, 2, 1)),
}


def body(
    inputs, grad_out, page_lengths, gain_one, gain_two, w_query, w_key, w_value, w_out, w_up, w_down, rel_table
):
    count = lax.axis_size("dp")
    tensor_index = lax.axis_index("tensor")
    own_rows, model = inputs.shape
    rows = 2 * own_rows
    half = own_rows // 2
    ff = w_up.shape[1]
    weights = (w_query, w_key, w_value)
    orders = {name: [[bit for bit in bits if bit < count] for bits in lists] for name, lists in BITS.items()}
    pieces = 2 ** len(orders["D"][0])
    pay_places = jnp.stack([place_of(orders[name][0]) for name in "DUPV"])
    got_places = jnp.stack([place_of(orders[name][2][::-1]) for name in "DUPV"])

    info = tensor_index.reshape(1)
    gain_one, gain_two = gain_one.reshape(1, model), gain_two.reshape(1, model)
    inputs, pay_places, got_places, info, gain_one, rel_table = tie(
        inputs, pay_places, got_places, info, gain_one, rel_table
    )
    normed_own = first_norm(inputs, gain_one)
    normed_peer = swap(normed_own)
    query_own, key_own, value_own = project(normed_own, weights)
    key_marks, query_marks = page_marks(page_lengths[0], rows, info)
    strip = bias_strip(rel_table)
    sent_grad, _ = tie(grad_out, query_own)
    grad_peer = swap(sent_grad)
    query_peer, key_peer, value_peer = project(normed_peer, weights)
    keys, values = (key_own, key_peer), (value_own, value_peer)
    marks = (key_marks, query_marks, strip)

    peer_outs, peer_lses, parts_from_peer = [], [], []
    query = query_peer
    for start in (0, half):
        out, lse, part = attention_forward(
            info, start, half, True, query, keys, values, *marks, w_out, jnp.bfloat16
        )
        peer_outs.append(out)
        peer_lses.append(lse)
        parts_from_peer.append(swap(part))
        query, _ = tie(query_peer, part)
    query, _, grad_peer = tie(query_own, part, grad_peer)
    own_out, own_lse, own_part = attention_forward(
        info, 0, own_rows, False, query, keys, values, *marks, w_out, jnp.float32
    )
    middles, normed_twos, normed_twos_peer = [], [], []
    for side, start in enumerate((0, half)):
        arrived = parts_from_peer[side]
        if side > 0:
            arrived, _ = tie(arrived, normed_two)
        middle, normed_two = second_norm(start, inputs, own_part, arrived, gain_two)
        middles.append(middle)
        normed_twos.append(normed_two)
        normed_twos_peer.append(swap(normed_two))
    own_hidden, own_pre, own_two, own_branch = feed(normed_twos, 0, grad_out, w_up, w_down, jnp.float32)
    last = own_two
    peer_hiddens, peer_pres, peer_branches, twos_from_peer = [], [], [], []
    for side, start in enumerate((0, half)):
        normed_two, _ = tie(normed_twos_peer[side], last)
        hidden, pre, two, branch = feed([normed_two], start, grad_peer, w_up, w_down, jnp.bfloat16)
        peer_hiddens.append(hidden)
        peer_pres.append(pre)
        peer_branches.append(branch)
        twos_from_peer.append(swap(two))
        last = two
    chains = {}
    token = peer_branches[1]
    seeds = None
    backs, branches_peer, grad_qs_own, grad_qs_peer, nears, fars = [], [], [], [], [], []
    heads = rel_table.shape[0]
    got = {}

    def late(value):
        return tie(value, token)[0]

    def halves(name):
        return chains[name].part, chains[name].coming

    for event in ORDER:
        side = 1 if event.endswith("b") else 0
        start = side * half
        if event in ("D0", "U0", "P0", "V0"):
            continue
        if event == "FG":
            payloads = feed_grads(
                pay_places,
                pieces,
                (own_hidden, *peer_hiddens),
                (own_pre, *peer_pres),
                (*normed_twos, *normed_twos_peer),
                (late(grad_out), grad_peer),
            )
            for number, name in enumerate("DU"):
                chains[name] = Reduction(payloads[2 * number : 2 * number + 2], *orders[name], count)
            token = payloads[0]
        elif event[0] in chains and event[1].isdigit():
            chain = chains[event[0]]
            if chain.level < chain.steps:
                chain.after(token)
                token = chain.advance(3450000000 if "P" in chains else 0)
        elif event in ("LNa", "LNb"):
            back = second_norm_back(
                start, own_two, late(twos_from_peer[side]), middles[side], grad_out, gain_two, w_out
            )
            backs.append(back)
            branches_peer.append(swap(back[1]))
            token = back[2]
        elif event in ("B1a", "B1b"):
            result = attention_backward(
                info,
                start,
                False,
                query_own,
                late(backs[side][2]),
                own_out,
                own_lse,
                keys,
                values,
                *marks,
                seeds,
                jnp.float32,
            )
            grad_qs_own.append(result[0])
        elif event in ("B2a", "B2b"):
            result = attention_backward(
                info,
                start,
                True,
                query_peer,
                nt(late(branches_peer[side]), w_out).astype(jnp.bfloat16),
                peer_outs[side],
                peer_lses[side],
                keys,
                values,
                *marks,
                seeds,
                jnp.bfloat16 if side else jnp.float32,
            )
            grad_qs_peer.append(result[0])
        elif event == "AG":
            payloads = attention_grads(
                pay_places,
                pieces,
                (normed_own, normed_peer),
                (*grad_qs_own, grad_qs_peer[0], late(grad_qs_peer[1])),
                *seeds,
                (own_out, *peer_outs),
                (backs[0][1], backs[1][1], *branches_peer),
            )
            for number, name in enumerate("PV"):
                chains[name] = Reduction(payloads[2 * number : 2 * number + 2], *orders[name], count)
            token = payloads[0]
        elif event == "NG":
            token = normed_grad((grad_qs_peer[0], late(grad_qs_peer[1])), *seeds, own_rows, weights)
            one_from_peer = swap(token)
        elif event == "E5":
            arrived = swap(jnp.concatenate([late(peer_branches[0]), peer_branches[1]], axis=0))
        elif event == "bands":
            token = bands = band_sums([late(nears[0]), *nears[1:]], fars)
        elif event == "LN1":
            input_grad, token = first_norm_back(
                grad_qs_own,
                *seeds,
                weights,
                late(one_from_peer),
                inputs,
                (backs[0][0], backs[1][0]),
                gain_one,
            )
            gain_one_part = token
        elif event == "s0":
            token = small = pack_small(late(gain_one_part), [backs[0][3], backs[1][3]], bands, heads)
            other, reach = swap(small), 2
        elif event in ("s1", "s2", "s3", "s4", "fin"):
            token = small = add_small(small, late(other), reach)
            reach = 8
            bit = {"s1": 1, "s2": 2, "s3": 4, "s4": 8, "fin": 0}[event]
            other = dp_swap(small, bit, count) if 0 < bit < count else jnp.zeros_like(small)
        elif event == "out":
            token = out = finish(middles, own_branch, late(arrived))
        elif event == "plD":
            part, coming = halves("D")
            token = down_total = place_feed(
                (part, late(coming)), got_places[0], orders["D"][0], orders["D"][2], (ff, model), pieces
            )
        elif event == "plU":
            part, coming = halves("U")
            token = up_total = place_feed(
                (part, late(coming)), got_places[1], orders["U"][0], orders["U"][2], (model, ff), pieces // 2
            )
        elif event == "plP":
            part, coming = halves("V")
            totals = place_attention(halves("P"), (part, late(coming)), got_places[2:], (orders["P"], orders["V"]))
            token = totals[0]
        if event[0] == "B" and event[1].isdigit():
            token, seeds = result[0], result[1:3]
            nears.append(result[3])
            fars.append(result[4])

    if count > 16:
        groups = [[j * 16 + i for j in range(count // 16)] for i in range(16)]
        small = lax.psum(small, "dp", axis_index_groups=groups)
    table_total = small[2 : 2 + heads, : rel_table.shape[1]]
    return (
        out,
        input_grad,
        small[0],
        small[1],
        *totals,
        up_total,
        down_total,
        table_total,
    )


def solution(mesh):
    in_specs = (
        P(("dp", "tensor"), None),
        P(("dp", "tensor"), None),
        P("dp", None),
        P(),
        P(),
        P(None, "tensor"),
        P(None, "tensor"),
        P(None, "tensor"),
        P("tensor", None),
        P(None, "tensor"),
        P("tensor", None),
        P("tensor", None),
    )
    out_specs = (
        P(("dp", "tensor"), None),
        P(("dp", "tensor"), None),
        P(),
        P(),
        P(None, "tensor"),
        P(None, "tensor"),
        P(None, "tensor"),
        P("tensor", None),
        P(None, "tensor"),
        P("tensor", None),
        P("tensor", None),
    )
    return jax.shard_map(body, mesh=mesh, in_specs=in_specs, out_specs=out_specs, check_vma=False)
```

```python
import functools
import jax
import jax.numpy as jnp
from jax import lax
from jax.experimental import pallas as pl
from jax.experimental.pallas import tpu as pltpu
from jax.sharding import PartitionSpec as P

HEAD_DIM = 64
BUCKETS = 16
LOG2E = 1.4426950408889634
TILE = 128
QB = 256
MB = 1 << 20


def cost(flops, traffic, share=0.01):
    return pl.CostEstimate(flops=int(share * flops), transcendentals=0, bytes_accessed=int(share * traffic))


def nt(left, right):
    return lax.dot_general(left, right, (((1,), (1,)), ((), ())), preferred_element_type=jnp.float32)


def nn(left, right):
    return jnp.dot(left, right, preferred_element_type=jnp.float32)


def half_of(block, side):
    lanes = lax.broadcasted_iota(jnp.int32, block.shape, 1)
    keep = (lanes < HEAD_DIM) if side == 0 else (lanes >= HEAD_DIM)
    return jnp.where(keep, block, jnp.zeros_like(block))


def tile_pos(local_tile, tensor_index, tiles):
    return lax.rem(local_tile + (tiles // 2) * tensor_index, tiles)


def bias_rows(strip_ref, head, key_tile, query_tile, query_tiles, tensor_index, tiles):
    pieces = []
    key_pos = tile_pos(key_tile, tensor_index, tiles)
    for step in range(query_tiles):
        diff = tile_pos(query_tile + step, tensor_index, tiles) - key_pos
        pieces.append(strip_ref[head, jnp.clip(diff, -2, 2) + 2])
    return jnp.concatenate(pieces, axis=1)


def ones_rows(rows):
    return (lax.broadcasted_iota(jnp.int32, (16, rows), 0) == 0).astype(jnp.bfloat16)


def vmem():
    return pl.BlockSpec(memory_space=pltpu.VMEM)


def smem():
    return pl.BlockSpec(memory_space=pltpu.SMEM)


def rows_of(refs):
    return jnp.concatenate([ref[...] for ref in refs], axis=0) if len(refs) > 1 else refs[0][...]


def attention_forward(info, start, count, peer, query, keys, values, key_marks, query_marks, strip, w_out, part_type):
    own_rows, width = query.shape
    rows = key_marks.shape[0]
    model = w_out.shape[1]
    pairs = width // 128
    tiles = rows // TILE
    query_tiles = count // TILE
    base = (own_rows if peer else 0) + start
    first = base // TILE

    def kernel(info_ref, q_ref, ko_ref, kp_ref, vo_ref, vp_ref, kf_ref, qf_ref, strip_ref, w_ref, o_ref, lse_ref, part_ref):
        tensor_index = info_ref[0]
        marks = qf_ref[base : base + count, :]
        def one_pair(pair, carry):
            lanes = pl.ds(pl.multiple_of(pair * 128, 128), 128)
            keys = jnp.concatenate(
                [jnp.concatenate([ko_ref[:, lanes], kp_ref[:, lanes]], axis=0), kf_ref[...]], axis=1
            )
            value_t = jnp.concatenate([vo_ref[:, lanes].T, vp_ref[:, lanes].T], axis=1)
            outs = []
            for side in range(2):
                query_half = half_of(q_ref[start : start + count, lanes], side)
                raw = nt(keys, jnp.concatenate([query_half, marks], axis=1))
                parts = []
                top = None
                for j in range(tiles):
                    part = raw[j * TILE : (j + 1) * TILE] * (LOG2E * HEAD_DIM**-0.5) + bias_rows(
                        strip_ref, 2 * pair + side, j, first, query_tiles, tensor_index, tiles
                    )
                    parts.append(part)
                    top = part if top is None else jnp.maximum(top, part)
                peak = jnp.max(top, axis=0, keepdims=True)
                weights = jnp.concatenate([jnp.exp2(part - peak).astype(jnp.bfloat16) for part in parts], axis=0)
                left = jnp.concatenate([value_t[side * HEAD_DIM : (side + 1) * HEAD_DIM], ones_rows(rows)], axis=0)
                out_t = nn(left, weights)
                total = out_t[HEAD_DIM : HEAD_DIM + 1]
                outs.append(out_t[:HEAD_DIM] * (1.0 / total))
                lse_ref[pair, side : side + 1, :] = peak + jnp.log2(total)
            o_ref[:, lanes] = jnp.concatenate(outs, axis=0).T.astype(jnp.bfloat16)
            return carry

        lax.fori_loop(0, pairs, one_pair, 0)
        part_ref[...] = nn(o_ref[...], w_ref[...]).astype(part_type)

    return pl.pallas_call(
        kernel,
        in_specs=[smem()] + [vmem()] * 9,
        out_specs=[vmem()] * 3,
        out_shape=[
            jax.ShapeDtypeStruct((count, width), jnp.bfloat16),
            jax.ShapeDtypeStruct((pairs, 2, count), jnp.float32),
            jax.ShapeDtypeStruct((count, model), part_type),
        ],
        compiler_params=pltpu.CompilerParams(vmem_limit_bytes=8 * MB),
        cost_estimate=cost(9 * 10**9 * count // own_rows, 8 * rows * width),
        name="attend",
    )(info, query, *keys, *values, key_marks, query_marks, strip, w_out)


def attention_backward(
    info, start, peer, query, grad_out, out, lse, keys, values, key_marks, query_marks, strip, seeds, sum_type
):
    own_rows, width = query.shape
    count = grad_out.shape[0]
    rows = key_marks.shape[0]
    pairs = width // 128
    tiles = rows // TILE
    query_tiles = count // TILE
    base = (own_rows if peer else 0) + start
    first = base // TILE
    shift = start if out.shape[0] > count else 0
    seeded = seeds is not None
    scale = HEAD_DIM**-0.5

    def kernel(info_ref, q_ref, do_ref, o_ref, lse_ref, ko_ref, kp_ref, vo_ref, vp_ref, kf_ref, qf_ref, strip_ref, *rest):
        if seeded:
            dk_seed, dv_seed, *rest = rest
        dq_ref, dk_ref, dv_ref, near_ref, far_ref, grads_ref = rest
        tensor_index = info_ref[0]
        query_marks = qf_ref[base : base + count, :]
        marks = (
            lax.broadcasted_iota(jnp.int32, (16, rows), 1) // TILE
            == lax.broadcasted_iota(jnp.int32, (16, rows), 0)
        ).astype(jnp.bfloat16)
        key_pos = tile_pos(lax.broadcasted_iota(jnp.int32, (8, TILE), 0), tensor_index, tiles)
        def one_pair(pair, carry):
            lanes = pl.ds(pl.multiple_of(pair * 128, 128), 128)
            key_pair = jnp.concatenate([ko_ref[:, lanes], kp_ref[:, lanes]], axis=0)
            keys = jnp.concatenate([key_pair, kf_ref[...]], axis=1)
            key_t = key_pair.T
            values = jnp.concatenate([vo_ref[:, lanes], vp_ref[:, lanes]], axis=0)
            inner = do_ref[:, lanes].astype(jnp.float32) * o_ref[shift : shift + count, lanes].astype(jnp.float32)
            inner = inner.T
            probs, grads, grad_qs, query_halves, do_halves = [], [], [], [], []
            for side in range(2):
                head = 2 * pair + side
                query_half = half_of(q_ref[start : start + count, lanes], side)
                do_half = half_of(do_ref[:, lanes], side)
                query_halves.append(query_half)
                do_halves.append(do_half)
                raw = nt(keys, jnp.concatenate([query_half, query_marks], axis=1))
                grad_prob = nt(values, do_half)
                lse = lse_ref[pair, side : side + 1, shift : shift + count]
                delta = jnp.sum(inner[side * HEAD_DIM : (side + 1) * HEAD_DIM], axis=0, keepdims=True)
                prob_parts, grad_parts = [], []
                for j in range(tiles):
                    span = slice(j * TILE, (j + 1) * TILE)
                    bias = bias_rows(strip_ref, head, j, first, query_tiles, tensor_index, tiles)
                    prob = jnp.exp2(raw[span] * (LOG2E * scale) + (bias - lse))
                    grad = (prob * (grad_prob[span] - delta)).astype(jnp.bfloat16)
                    grads_ref[side, span, :] = grad
                    prob_parts.append(prob.astype(jnp.bfloat16))
                    grad_parts.append(grad)
                probs.append(jnp.concatenate(prob_parts, axis=0))
                grad_all = jnp.concatenate(grad_parts, axis=0)
                grads.append(grad_all)
                left = jnp.concatenate([key_t[side * HEAD_DIM : (side + 1) * HEAD_DIM], marks], axis=0)
                grad_q = nn(left, grad_all)
                grad_qs.append(grad_q[:HEAD_DIM])
                sums = grad_q[HEAD_DIM : HEAD_DIM + 8]
                before, after = jnp.zeros((8, TILE), jnp.float32), jnp.zeros((8, TILE), jnp.float32)
                for part in range(query_tiles):
                    query_pos = tile_pos(first + part, tensor_index, tiles)
                    piece = sums[:, part * TILE : (part + 1) * TILE]
                    before = before + jnp.where(key_pos <= query_pos - 2, piece, 0.0)
                    after = after + jnp.where(key_pos >= query_pos + 2, piece, 0.0)
                far_ref[head, 0] = before
                far_ref[head, 1] = after
                for diff in (-1, 0, 1):
                    near = None
                    for part in range(query_tiles):
                        wanted = tile_pos(first + part, tensor_index, tiles) - diff
                        valid = jnp.logical_and(wanted >= 0, wanted < tiles)
                        local = tile_pos(jnp.clip(wanted, 0, tiles - 1), tensor_index, tiles)
                        block = grads_ref[
                            side,
                            pl.ds(pl.multiple_of(local * TILE, TILE), TILE),
                            part * TILE : (part + 1) * TILE,
                        ].astype(jnp.float32)
                        block = block if diff == 0 else jnp.where(valid, block, 0.0)
                        near = block if near is None else near + block
                    near_ref[head, diff + 1] = near
            dv = nn(jnp.concatenate(probs, axis=1), jnp.concatenate(do_halves, axis=0))
            dk = nn(jnp.concatenate(grads, axis=1), jnp.concatenate(query_halves, axis=0)) * scale
            if seeded:
                dv = dv + dv_seed[:, lanes]
                dk = dk + dk_seed[:, lanes]
            dv_ref[:, lanes] = dv.astype(sum_type)
            dk_ref[:, lanes] = dk.astype(sum_type)
            dq_ref[:, lanes] = (jnp.concatenate(grad_qs, axis=0).T * scale).astype(jnp.bfloat16)
            return carry

        lax.fori_loop(0, pairs, one_pair, 0)

    return pl.pallas_call(
        kernel,
        in_specs=[smem()] + [vmem()] * (13 if seeded else 11),
        out_specs=[vmem()] * 5,
        out_shape=[
            jax.ShapeDtypeStruct((count, width), jnp.bfloat16),
            jax.ShapeDtypeStruct((rows, width), sum_type),
            jax.ShapeDtypeStruct((rows, width), sum_type),
            jax.ShapeDtypeStruct((2 * pairs, 3, TILE, TILE), jnp.float32),
            jax.ShapeDtypeStruct((2 * pairs, 2, 8, TILE), jnp.float32),
        ],
        scratch_shapes=[pltpu.VMEM((2, rows, count), jnp.bfloat16)],
        compiler_params=pltpu.CompilerParams(vmem_limit_bytes=14 * MB),
        cost_estimate=cost(18 * 10**9 * count // own_rows, 20 * rows * width),
        name="attend_back",
    )(info, query, grad_out, out, lse, *keys, *values, key_marks, query_marks, strip, *(seeds or ()))


def band_levels(diff):
    delta = diff * TILE + (
        lax.broadcasted_iota(jnp.int32, (TILE, TILE), 1) - lax.broadcasted_iota(jnp.int32, (TILE, TILE), 0)
    )
    distance = jnp.abs(delta) + 1
    level = jnp.zeros_like(delta)
    for exponent in range(1, BUCKETS // 2):
        level = level + (distance >= 2**exponent).astype(jnp.int32)
    return level + (BUCKETS // 2) * (delta < 0).astype(jnp.int32)


def band_sums(nears, fars):
    heads = nears[0].shape[0]
    calls = len(nears)

    def kernel(*refs):
        near_refs, far_refs, o_ref = refs[:calls], refs[calls : 2 * calls], refs[-1]
        rows = [[jnp.zeros((1, TILE), jnp.float32) for _ in range(BUCKETS)] for _ in range(heads)]
        for head in range(heads):
            far = sum(ref[head] for ref in far_refs)
            rows[head][BUCKETS // 2 - 1] += jnp.sum(far[0], axis=0, keepdims=True)
            rows[head][BUCKETS - 1] += jnp.sum(far[1], axis=0, keepdims=True)
        for diff, present in ((0, [*range(8), *range(9, 16)]), (1, range(1, 8)), (-1, range(9, 16))):
            level = band_levels(diff)
            for head in range(heads):
                near = sum(ref[head, diff + 1] for ref in near_refs)
                for bucket in present:
                    rows[head][bucket] += jnp.sum(jnp.where(level == bucket, near, 0.0), axis=0, keepdims=True)
        at = lax.broadcasted_iota(jnp.int32, (BUCKETS, TILE), 0) == lax.broadcasted_iota(
            jnp.int32, (BUCKETS, TILE), 1
        )
        o_ref[...] = jnp.zeros_like(o_ref)
        for head in range(heads):
            sums = jnp.sum(jnp.concatenate(rows[head], axis=0), axis=1, keepdims=True)
            o_ref[head : head + 1, :] = jnp.sum(jnp.where(at, sums, 0.0), axis=0, keepdims=True)

    return pl.pallas_call(
        kernel,
        in_specs=[vmem()] * (2 * calls),
        out_specs=vmem(),
        out_shape=jax.ShapeDtypeStruct((8, TILE), jnp.float32),
        compiler_params=pltpu.CompilerParams(vmem_limit_bytes=8 * MB),
        cost_estimate=cost(heads * 3 * 16 * TILE * TILE, heads * 8 * TILE * TILE),
        name="band_sums",
    )(*nears, *fars)


def pack_small(gain_one_part, gain_two_parts, table, heads):
    model = gain_one_part.shape[1]
    calls = len(gain_two_parts)

    def kernel(*refs):
        one_ref, table_ref, o_ref = refs[0], refs[calls + 1], refs[calls + 2]
        o_ref[...] = jnp.zeros_like(o_ref)
        o_ref[0:1, :] = jnp.sum(one_ref[...], axis=0, keepdims=True)
        two = sum(ref[...] for ref in refs[1 : calls + 1])
        o_ref[1:2, :] = jnp.sum(two, axis=0, keepdims=True)
        o_ref[2 : 2 + heads, :TILE] = table_ref[:heads, :]

    return pl.pallas_call(
        kernel,
        in_specs=[vmem()] * (calls + 2),
        out_specs=vmem(),
        out_shape=jax.ShapeDtypeStruct((8, model), jnp.float32),
        compiler_params=pltpu.CompilerParams(vmem_limit_bytes=2 * MB),
        cost_estimate=cost(1000, 1000),
        name="pack_small",
    )(gain_one_part, *gain_two_parts, table)


def add_small(mine, theirs, rows):
    def kernel(a_ref, b_ref, o_ref):
        line = lax.broadcasted_iota(jnp.int32, a_ref.shape, 0)
        o_ref[...] = a_ref[...] + jnp.where(line < rows, b_ref[...], 0.0)

    return pl.pallas_call(
        kernel,
        in_specs=[vmem()] * 2,
        out_specs=vmem(),
        out_shape=jax.ShapeDtypeStruct(mine.shape, jnp.float32),
        compiler_params=pltpu.CompilerParams(vmem_limit_bytes=2 * MB),
        cost_estimate=cost(1000, 1000),
        name="add_small",
    )(mine, theirs)


def bias_strip(rel_table):
    heads = rel_table.shape[0]

    def kernel(t_ref, o_ref):
        table = t_ref[...].astype(jnp.float32) * LOG2E
        levels = [band_levels(diff) for diff in (-1, 0, 1)]
        masks = [[level == bucket for bucket in range(BUCKETS)] for level in levels]
        for head in range(heads):
            entries = [table[head : head + 1, bucket : bucket + 1] for bucket in range(BUCKETS)]
            for slot, present in enumerate((range(9, 16), [*range(8), *range(9, 16)], range(1, 8))):
                tile = jnp.zeros((TILE, TILE), jnp.float32)
                for bucket in present:
                    tile = jnp.where(masks[slot][bucket], entries[bucket], tile)
                o_ref[head, slot + 1] = tile
            o_ref[head, 0] = jnp.broadcast_to(entries[15], (TILE, TILE))
            o_ref[head, 4] = jnp.broadcast_to(entries[7], (TILE, TILE))

    return pl.pallas_call(
        kernel,
        in_specs=[vmem()],
        out_specs=vmem(),
        out_shape=jax.ShapeDtypeStruct((heads, 5, TILE, TILE), jnp.float32),
        compiler_params=pltpu.CompilerParams(vmem_limit_bytes=8 * MB),
        cost_estimate=cost(10**9, 0, 1),
        name="bias_strip",
    )(rel_table)


def page_marks(lengths, rows, tensor_index):
    slots = lengths.shape[0]

    def kernel(len_ref, t_ref, k_ref, q_ref):
        place = lax.broadcasted_iota(jnp.int32, (rows, 128), 0) + (rows // 2) * t_ref[0]
        place = jnp.where(place >= rows, place - rows, place)
        lanes = lax.broadcasted_iota(jnp.int32, (rows, 128), 1)
        end = jnp.int32(0)
        page = jnp.zeros((rows, 128), jnp.int32)
        for slot in range(slots):
            end = end + len_ref[slot]
            page = page + (place >= end).astype(jnp.int32)
        k_ref[...] = jnp.where(page == lanes, 1.0, 0.0).astype(jnp.bfloat16)
        other = jnp.logical_and(page != lanes, lanes < slots)
        q_ref[...] = jnp.where(other, -1e30, 0.0).astype(jnp.bfloat16)

    return pl.pallas_call(
        kernel,
        in_specs=[smem(), smem()],
        out_specs=[vmem()] * 2,
        out_shape=[jax.ShapeDtypeStruct((rows, 128), jnp.bfloat16)] * 2,
        compiler_params=pltpu.CompilerParams(vmem_limit_bytes=8 * MB),
        cost_estimate=cost(10**9, 0, 1),
        name="page_marks",
    )(lengths, tensor_index)


def tn(left, right):
    return lax.dot_general(left, right, (((0,), (0,)), ((), ())), preferred_element_type=jnp.float32)


def standardize(values):
    centred = values - jnp.mean(values, axis=-1, keepdims=True)
    variance = jnp.mean(centred * centred, axis=-1, keepdims=True)
    inverse = lax.rsqrt(variance + 1e-05)
    return centred * inverse, inverse


def norm_back(grad, standard, inverse, gain):
    scaled = grad * gain
    mean = jnp.mean(scaled, axis=-1, keepdims=True)
    slope = jnp.mean(scaled * standard, axis=-1, keepdims=True)
    return inverse * (scaled - mean - standard * slope)


def fold_rows(values):
    return jnp.sum(values.reshape(-1, 8, values.shape[-1]), axis=0)


def first_norm(inputs, gain):
    rows, model = inputs.shape

    def kernel(x_ref, g_ref, o_ref):
        gain = g_ref[...].astype(jnp.float32)
        for start in range(0, rows, 128):
            standard, _ = standardize(x_ref[start : start + 128, :].astype(jnp.float32))
            o_ref[start : start + 128, :] = (standard * gain).astype(jnp.bfloat16)

    return pl.pallas_call(
        kernel,
        in_specs=[vmem()] * 2,
        out_specs=vmem(),
        out_shape=jax.ShapeDtypeStruct((rows, model), jnp.bfloat16),
        compiler_params=pltpu.CompilerParams(vmem_limit_bytes=6 * MB),
        cost_estimate=cost(rows * model * 8, 4 * rows * model),
        name="first_norm",
    )(inputs, gain)


def project(normed, weights):
    rows, model = normed.shape
    width = weights[0].shape[1]

    def kernel(x_ref, *refs):
        for w_ref, o_ref in zip(refs[:3], refs[3:]):
            o_ref[...] = nn(x_ref[...], w_ref[...]).astype(jnp.bfloat16)

    return pl.pallas_call(
        kernel,
        in_specs=[vmem()] * 4,
        out_specs=[vmem()] * 3,
        out_shape=[jax.ShapeDtypeStruct((rows, width), jnp.bfloat16)] * 3,
        compiler_params=pltpu.CompilerParams(vmem_limit_bytes=4 * MB),
        cost_estimate=cost(6 * rows * model * width, 0, 1),
        name="project",
    )(normed, *weights)


def second_norm(start, inputs, own_part, peer_part, gain):
    rows, model = peer_part.shape

    def kernel(x_ref, a_ref, b_ref, g_ref, m_ref, o_ref):
        gain = g_ref[...].astype(jnp.float32)
        for offset in range(0, rows, 128):
            span = slice(offset, offset + 128)
            wide = slice(start + offset, start + offset + 128)
            middle = x_ref[wide, :].astype(jnp.float32) + a_ref[wide, :] + b_ref[span, :].astype(jnp.float32)
            m_ref[span, :] = middle
            standard, _ = standardize(middle)
            o_ref[span, :] = (standard * gain).astype(jnp.bfloat16)

    return pl.pallas_call(
        kernel,
        in_specs=[vmem()] * 4,
        out_specs=[vmem()] * 2,
        out_shape=[
            jax.ShapeDtypeStruct((rows, model), jnp.float32),
            jax.ShapeDtypeStruct((rows, model), jnp.bfloat16),
        ],
        compiler_params=pltpu.CompilerParams(vmem_limit_bytes=8 * MB),
        cost_estimate=cost(rows * model * 8, 14 * rows * model),
        name="second_norm",
    )(inputs, own_part, peer_part, gain)


FF_CHUNK = 512


def feed(normeds, start, grads, w_up, w_down, sum_type):
    rows = sum(n.shape[0] for n in normeds)
    model, ff = w_up.shape
    calls = len(normeds)

    def kernel(*refs):
        g_ref, u_ref, d_ref, h_ref, p_ref, gn_ref, bt_ref = refs[calls:]
        normed = rows_of(refs[:calls])
        def one_chunk(step, carry):
            span = pl.ds(pl.multiple_of(step * FF_CHUNK, FF_CHUNK), FF_CHUNK)
            pre = nn(normed, u_ref[:, span])
            grad_hidden = nt(g_ref[start : start + rows, :], d_ref[span, :])
            square = pre * pre
            bent = jnp.tanh(pre * (0.7978845608 + (0.7978845608 * 0.044715) * square))
            gate = 0.5 + 0.5 * bent
            h_ref[:, span] = (pre * gate).astype(jnp.bfloat16)
            slope = gate + pre * (0.5 - 0.5 * bent * bent) * (
                0.7978845608 + (3 * 0.7978845608 * 0.044715) * square
            )
            p_ref[:, span] = (grad_hidden * slope).astype(jnp.bfloat16)
            return carry

        lax.fori_loop(0, ff // FF_CHUNK, one_chunk, 0)
        gn_ref[...] = nt(p_ref[...], u_ref[...]).astype(sum_type)
        bt_ref[...] = nn(h_ref[...], d_ref[...]).astype(sum_type)

    return pl.pallas_call(
        kernel,
        in_specs=[vmem()] * (calls + 3),
        out_specs=[vmem()] * 4,
        out_shape=[jax.ShapeDtypeStruct((rows, ff), jnp.bfloat16)] * 2
        + [jax.ShapeDtypeStruct((rows, model), sum_type)] * 2,
        compiler_params=pltpu.CompilerParams(vmem_limit_bytes=8 * MB),
        cost_estimate=cost(8 * rows * model * ff, 4 * model * ff + 8 * rows * ff),
        name="feed",
    )(*normeds, grads, w_up, w_down)


def grouped_call(kernel, groups, **options):
    sizes = [len(g) for g in groups]

    def body(place_ref, *refs):
        lists, at = [], 0
        for size in sizes:
            lists.append(refs[at : at + size])
            at += size
        kernel(place_ref, *lists, *refs[at:])

    return pl.pallas_call(body, in_specs=[smem()] + [vmem()] * sum(sizes), **options)


def turned(refs, span=slice(None)):
    return jnp.concatenate([ref[:, span].T for ref in refs], axis=1)


def feed_grads(places, pieces, hiddens, grad_pres, normeds, grads):
    rows = sum(h.shape[0] for h in hiddens)
    ff = hiddens[0].shape[1]
    model = normeds[0].shape[1]
    size = ff // pieces
    fine = model // size

    def kernel(place_ref, h_refs, p_refs, n_refs, g_refs, *rest):
        down_ref, up_ref = rest[4:]
        grad = rows_of(g_refs)
        normed_t = turned(n_refs)
        for part in range(ff // model):
            span = slice(part * model, (part + 1) * model)
            down = nn(turned(h_refs, span), grad).astype(jnp.bfloat16)
            for k in range(fine):
                store_piece(down_ref, place_ref[0], pieces, part * fine + k, size, down[k * size : (k + 1) * size])
        for part in range(ff // model):
            span = slice(part * model, (part + 1) * model)
            pre = jnp.concatenate([ref[:, span] for ref in p_refs], axis=0)
            up = nn(normed_t, pre).astype(jnp.bfloat16)
            for k in range(fine):
                store_piece(up_ref, place_ref[1], pieces, part * fine + k, size, up[k * size : (k + 1) * size])
        for number, out_ref in enumerate(rest[:4]):
            out_ref[...] = (down_ref, up_ref)[number // 2][number % 2]

    groups = (hiddens, grad_pres, normeds, grads)
    return grouped_call(
        kernel,
        groups,
        out_specs=[vmem()] * 4,
        out_shape=[jax.ShapeDtypeStruct((ff // 2, model), jnp.bfloat16)] * 4,
        scratch_shapes=[pltpu.VMEM((2, ff // 2, model), jnp.bfloat16)] * 2,
        compiler_params=pltpu.CompilerParams(vmem_limit_bytes=16 * MB),
        cost_estimate=cost(4 * rows * model * ff, 4 * rows * ff + 4 * ff * model),
        name="feed_grads",
    )(places, *[a for g in groups for a in g])


def second_norm_back(start, own_part, peer_part, middle, grad_out, gain, w_out):
    rows, model = middle.shape
    width = w_out.shape[0]

    def kernel(a_ref, b_ref, m_ref, g_ref, gain_ref, w_ref, gm_ref, gb_ref, ga_ref, gain_out):
        gain = gain_ref[...].astype(jnp.float32)
        part = jnp.zeros((8, model), jnp.float32)
        for offset in range(0, rows, 128):
            span = slice(offset, offset + 128)
            wide = slice(start + offset, start + offset + 128)
            grad = a_ref[wide, :] + b_ref[span, :].astype(jnp.float32)
            standard, inverse = standardize(m_ref[span, :])
            result = g_ref[wide, :].astype(jnp.float32) + norm_back(grad, standard, inverse, gain)
            gm_ref[span, :] = result
            gb_ref[span, :] = result.astype(jnp.bfloat16)
            part = part + fold_rows(grad * standard)
        gain_out[...] = part
        ga_ref[...] = nt(gb_ref[...], w_ref[...]).astype(jnp.bfloat16)

    return pl.pallas_call(
        kernel,
        in_specs=[vmem()] * 6,
        out_specs=[vmem()] * 4,
        out_shape=[
            jax.ShapeDtypeStruct((rows, model), jnp.float32),
            jax.ShapeDtypeStruct((rows, model), jnp.bfloat16),
            jax.ShapeDtypeStruct((rows, width), jnp.bfloat16),
            jax.ShapeDtypeStruct((8, model), jnp.float32),
        ],
        compiler_params=pltpu.CompilerParams(vmem_limit_bytes=10 * MB),
        cost_estimate=cost(10**11, 0, 1 if start else 0.0),
        name="second_norm_back",
    )(own_part, peer_part, middle, grad_out, gain, w_out)


def normed_grad(grad_qs, grad_k, grad_v, offset, weights):
    rows = sum(q.shape[0] for q in grad_qs)
    model, width = weights[0].shape
    calls = len(grad_qs)

    def kernel(*refs):
        k_ref, v_ref, wq_ref, wk_ref, wv_ref, o_ref = refs[calls:]
        span = slice(offset, offset + rows)
        total = nt(rows_of(refs[:calls]), wq_ref[...])
        total = total + nt(k_ref[span, :], wk_ref[...]) + nt(v_ref[span, :], wv_ref[...])
        o_ref[...] = total.astype(jnp.bfloat16)

    return pl.pallas_call(
        kernel,
        in_specs=[vmem()] * (calls + 5),
        out_specs=vmem(),
        out_shape=jax.ShapeDtypeStruct((rows, model), jnp.bfloat16),
        compiler_params=pltpu.CompilerParams(vmem_limit_bytes=6 * MB),
        cost_estimate=cost(10**11, 0, 1),
        name="normed_grad",
    )(*grad_qs, grad_k, grad_v, *weights)


def first_norm_back(grad_qs, grad_k, grad_v, weights, peer_part, inputs, middles, gain):
    rows, model = inputs.shape
    width = weights[0].shape[1]
    calls = len(grad_qs)
    size = rows // calls

    def kernel(*refs):
        q_refs, m_refs = refs[:calls], refs[calls : 2 * calls]
        k_ref, v_ref, wq_ref, wk_ref, wv_ref, b_ref, x_ref, gain_ref, o_ref, gain_out = refs[2 * calls :]
        gain = gain_ref[...].astype(jnp.float32)
        part = jnp.zeros((8, model), jnp.float32)
        for call in range(calls):
            span = slice(call * size, (call + 1) * size)
            grad = nt(q_refs[call][...], wq_ref[...])
            grad = grad + nt(k_ref[span, :], wk_ref[...]) + nt(v_ref[span, :], wv_ref[...])
            grad = grad + b_ref[span, :].astype(jnp.float32)
            standard, inverse = standardize(x_ref[span, :].astype(jnp.float32))
            result = m_refs[call][...] + norm_back(grad, standard, inverse, gain)
            o_ref[span, :] = result.astype(jnp.bfloat16)
            part = part + fold_rows(grad * standard)
        gain_out[...] = part

    return pl.pallas_call(
        kernel,
        in_specs=[vmem()] * (2 * calls + 8),
        out_specs=[vmem()] * 2,
        out_shape=[
            jax.ShapeDtypeStruct((rows, model), jnp.bfloat16),
            jax.ShapeDtypeStruct((8, model), jnp.float32),
        ],
        compiler_params=pltpu.CompilerParams(vmem_limit_bytes=10 * MB),
        cost_estimate=cost(6 * rows * model * width, 12 * rows * model),
        name="first_norm_back",
    )(*grad_qs, *middles, grad_k, grad_v, *weights, peer_part, inputs, gain)


def store_piece(ref, place, pieces, block, size, values):
    half = pieces // 2
    spot = jnp.bitwise_xor(place, block)
    ref[spot // half, pl.ds(pl.multiple_of(lax.rem(spot, half) * size, size), size), :] = values


def attention_grads(places, pieces, normeds, grad_qs, grad_k, grad_v, outs, branches):
    rows, width = grad_k.shape
    model = normeds[0].shape[1]
    size = 2 * model // pieces
    fine = model // size

    def kernel(place_ref, n_refs, q_refs, k_refs, v_refs, o_refs, b_refs, *rest):
        first_ref, second_ref = rest[4:]
        normed_t = turned(n_refs)
        for ref, which, base, right in (
            (first_ref, 2, 0, rows_of(q_refs)),
            (first_ref, 2, fine, rows_of(k_refs)),
            (second_ref, 3, 0, rows_of(v_refs)),
        ):
            result = nn(normed_t, right).astype(jnp.bfloat16)
            for k in range(fine):
                store_piece(ref, place_ref[which], pieces, base + k, size, result[k * size : (k + 1) * size])
        result = nn(turned(o_refs), rows_of(b_refs)).astype(jnp.bfloat16)
        for side in range(2):
            for k in range(fine // 2):
                store_piece(
                    second_ref,
                    place_ref[3],
                    pieces,
                    fine + side * (fine // 2) + k,
                    size,
                    result[k * size : (k + 1) * size, side * width : (side + 1) * width],
                )
        for number, out_ref in enumerate(rest[:4]):
            out_ref[...] = (first_ref, second_ref)[number // 2][number % 2]

    groups = (normeds, grad_qs, (grad_k,), (grad_v,), outs, branches)
    return grouped_call(
        kernel,
        groups,
        out_specs=[vmem()] * 4,
        out_shape=[jax.ShapeDtypeStruct((model, width), jnp.bfloat16)] * 4,
        scratch_shapes=[pltpu.VMEM((2, model, width), jnp.bfloat16)] * 2,
        compiler_params=pltpu.CompilerParams(vmem_limit_bytes=12 * MB),
        cost_estimate=cost(8 * rows * model * width, 6 * rows * model),
        name="attention_grads",
    )(places, *[a for g in groups for a in g])


def swap(values):
    return lax.ppermute(values, "tensor", [(0, 1), (1, 0)])


def dp_swap(values, bit, count):
    return lax.ppermute(values, "dp", [(i, i ^ bit) for i in range(count)])


def place_of(bits):
    index = lax.axis_index("dp")
    place = jnp.int32(0)
    for bit in bits:
        place = place * 2 + lax.rem(index // bit, 2)
    return place


def owner_place(block, bits, gather):
    place = 0
    for bit in reversed(gather):
        place = place * 2 + (block // 2 ** (len(bits) - 1 - bits.index(bit))) % 2
    return place


def add_rows(mine, theirs, split, weight):
    rows, width = mine.shape
    size = rows // 2 if split else rows

    def kernel(a_ref, b_ref, *out_refs):
        for part, out_ref in enumerate(out_refs):
            span = slice(part * size, (part + 1) * size)
            total = a_ref[span, :].astype(jnp.float32) + b_ref[span, :].astype(jnp.float32)
            out_ref[...] = total.astype(jnp.bfloat16)

    count = 2 if split else 1
    return pl.pallas_call(
        kernel,
        in_specs=[vmem()] * 2,
        out_specs=[vmem()] * count,
        out_shape=[jax.ShapeDtypeStruct((size, width), jnp.bfloat16)] * count,
        compiler_params=pltpu.CompilerParams(vmem_limit_bytes=4 * MB),
        cost_estimate=cost(weight, 0, 1),
        name="add_rows",
    )(mine, theirs)


def join_rows(upper, lower, weight):
    rows, width = upper.shape

    def kernel(a_ref, b_ref, o_ref):
        o_ref[:rows, :] = a_ref[...]
        o_ref[rows:, :] = b_ref[...]

    return pl.pallas_call(
        kernel,
        in_specs=[vmem()] * 2,
        out_specs=vmem(),
        out_shape=jax.ShapeDtypeStruct((2 * rows, width), jnp.bfloat16),
        compiler_params=pltpu.CompilerParams(vmem_limit_bytes=2 * MB),
        cost_estimate=cost(weight, 0, 1),
        name="join_rows",
    )(upper, lower)


class Reduction:
    def __init__(self, halves, bits, last, gather, count):
        self.keep, self.bits, self.last, self.gather, self.count = halves[0], bits, last, gather, count
        self.level = 0
        self.coming = dp_swap(halves[1], bits[0], count)
        self.part = None

    @property
    def steps(self):
        return len(self.bits) + len(self.last) + len(self.gather) - 1

    def after(self, token):
        if self.level < len(self.bits) + len(self.last):
            self.keep, _ = tie(self.keep, token)
        else:
            self.part, _ = tie(self.part, token)

    def advance(self, weight):
        sums = len(self.bits) + len(self.last)
        if self.level < sums:
            split = self.level + 1 < len(self.bits)
            self.part, *sent = add_rows(self.keep, self.coming, split, weight)
        else:
            self.part = join_rows(self.part, self.coming, weight)
        self.level += 1
        if self.level == sums:
            done = 2**sums
            if done < self.count:
                groups = [[j * done + i for j in range(self.count // done)] for i in range(done)]
                self.part = lax.psum(self.part, "dp", axis_index_groups=groups)
        if self.level < len(self.bits):
            self.keep = self.part
            self.coming = dp_swap(sent[0], self.bits[self.level], self.count)
        elif self.level < sums:
            self.keep = self.part
            self.coming = dp_swap(self.part, self.last[0], self.count)
        else:
            self.coming = dp_swap(self.part, self.gather[self.level - sums], self.count)
        return self.part


def tie(*values):
    return lax.optimization_barrier(values)


def place_feed(halves, place, bits, gather, shape, along):
    pieces = 2 ** len(bits)
    rows, width = halves[0].shape
    size = 2 * rows // pieces

    def kernel(place_ref, a_ref, b_ref, out_ref, wide_ref, sems):
        copies = []
        for k in range(pieces):
            spot = jnp.bitwise_xor(place_ref[0], owner_place(k, bits, gather))
            span = pl.ds(pl.multiple_of(lax.rem(spot, pieces // 2) * size, size), size)
            values = jnp.where(spot < pieces // 2, a_ref[span, :], b_ref[span, :])
            wide_ref[k] = values.astype(jnp.float32)
            row, column = k % along, k // along
            target = out_ref.at[pl.ds(row * size, size), pl.ds(column * width, width)]
            copies.append(pltpu.make_async_copy(wide_ref.at[k], target, sems.at[k]))
            copies[-1].start()
        for copy in copies:
            copy.wait()

    return pl.pallas_call(
        kernel,
        in_specs=[smem(), vmem(), vmem()],
        out_specs=pl.BlockSpec(memory_space=pltpu.HBM),
        out_shape=jax.ShapeDtypeStruct(shape, jnp.float32),
        scratch_shapes=[pltpu.VMEM((pieces, size, width), jnp.float32), pltpu.SemaphoreType.DMA((pieces,))],
        compiler_params=pltpu.CompilerParams(vmem_limit_bytes=8 * MB),
        cost_estimate=cost(rows * width, 12 * rows * width),
        name="place_feed",
    )(place.reshape(1), *halves)


def place_attention(first, second, places, orders):
    pieces = 2 ** len(orders[0][0])
    model, width = first[0].shape
    size = 2 * model // pieces
    fine = model // size

    def kernel(place_ref, fa_ref, fb_ref, sa_ref, sb_ref, q_ref, k_ref, v_ref, o_ref, wide_ref, sems):
        copies = []
        for out_ref, a_ref, b_ref, which, base in (
            (q_ref, fa_ref, fb_ref, 0, 0),
            (k_ref, fa_ref, fb_ref, 0, fine),
            (v_ref, sa_ref, sb_ref, 1, 0),
            (o_ref, sa_ref, sb_ref, 1, fine),
        ):
            for k in range(fine):
                spot = jnp.bitwise_xor(place_ref[which], owner_place(base + k, orders[which][0], orders[which][2]))
                rows = pl.ds(pl.multiple_of(lax.rem(spot, pieces // 2) * size, size), size)
                number = len(copies)
                values = jnp.where(spot < pieces // 2, a_ref[rows, :], b_ref[rows, :])
                wide_ref[number] = values.astype(jnp.float32)
                row, column = (k % (fine // 2), k // (fine // 2)) if out_ref is o_ref else (k, 0)
                target = out_ref.at[pl.ds(row * size, size), pl.ds(column * width, width)]
                copies.append(pltpu.make_async_copy(wide_ref.at[number], target, sems.at[number]))
                copies[-1].start()
        for copy in copies:
            copy.wait()

    return pl.pallas_call(
        kernel,
        in_specs=[smem()] + [vmem()] * 4,
        out_specs=[pl.BlockSpec(memory_space=pltpu.HBM)] * 4,
        out_shape=[jax.ShapeDtypeStruct((model, width), jnp.float32)] * 3
        + [jax.ShapeDtypeStruct((width, model), jnp.float32)],
        scratch_shapes=[pltpu.VMEM((4 * fine, size, width), jnp.float32), pltpu.SemaphoreType.DMA((4 * fine,))],
        compiler_params=pltpu.CompilerParams(vmem_limit_bytes=8 * MB),
        cost_estimate=cost(4 * model * width, 24 * model * width),
        name="place_attention",
    )(places, *first, *second)


def finish(middles, own_branch, arrived):
    rows, model = own_branch.shape
    calls = len(middles)
    size = rows // calls

    def kernel(*refs):
        b_ref, own_ref, o_ref = refs[calls:]
        for call in range(calls):
            span = slice(call * size, (call + 1) * size)
            total = refs[call][...] + own_ref[span, :] + b_ref[span, :].astype(jnp.float32)
            o_ref[span, :] = total.astype(jnp.bfloat16)

    return pl.pallas_call(
        kernel,
        in_specs=[vmem()] * (calls + 2),
        out_specs=vmem(),
        out_shape=jax.ShapeDtypeStruct((rows, model), jnp.bfloat16),
        compiler_params=pltpu.CompilerParams(vmem_limit_bytes=4 * MB),
        cost_estimate=cost(3 * rows * model, 14 * rows * model),
        name="finish",
    )(*middles, arrived, own_branch)


ORDER = (
    "LNa", "FG", "D0", "LNb", "U0", "D1", "U1", "B1a", "B1b", "B2a", "D2", "B2b", "AG", "D3", "NG",
    "V0", "bands", "P0", "U2", "V1", "P1", "D4", "U3", "P2", "LN1", "E5", "D5", "V2", "P3", "U4",
    "V3", "P4", "D6", "U5", "out", "s0", "V4", "P5", "s1", "plD", "s2", "V5", "U6", "s3", "P6",
    "s4", "V6", "plU", "plP", "fin",
)
BITS = {
    "D": ((1, 4, 2), (8,), (4, 2, 1)),
    "U": ((1, 4, 2), (8,), (4, 2, 1)),
    "P": ((1, 4, 2), (8,), (2, 4, 1)),
    "V": ((1, 2, 4), (8,), (4, 2, 1)),
}


def body(
    inputs, grad_out, page_lengths, gain_one, gain_two, w_query, w_key, w_value, w_out, w_up, w_down, rel_table
):
    count = lax.axis_size("dp")
    tensor_index = lax.axis_index("tensor")
    own_rows, model = inputs.shape
    rows = 2 * own_rows
    half = own_rows // 2
    ff = w_up.shape[1]
    weights = (w_query, w_key, w_value)
    orders = {name: [[bit for bit in bits if bit < count] for bits in lists] for name, lists in BITS.items()}
    pieces = 2 ** len(orders["D"][0])
    pay_places = jnp.stack([place_of(orders[name][0]) for name in "DUPV"])
    got_places = jnp.stack([place_of(orders[name][2][::-1]) for name in "DUPV"])

    info = tensor_index.reshape(1)
    gain_one, gain_two = gain_one.reshape(1, model), gain_two.reshape(1, model)
    inputs, pay_places, got_places, info, gain_one, rel_table = tie(
        inputs, pay_places, got_places, info, gain_one, rel_table
    )
    normed_own = first_norm(inputs, gain_one)
    normed_peer = swap(normed_own)
    query_own, key_own, value_own = project(normed_own, weights)
    key_marks, query_marks = page_marks(page_lengths[0], rows, info)
    strip = bias_strip(rel_table)
    sent_grad, _ = tie(grad_out, query_own)
    grad_peer = swap(sent_grad)
    query_peer, key_peer, value_peer = project(normed_peer, weights)
    keys, values = (key_own, key_peer), (value_own, value_peer)
    marks = (key_marks, query_marks, strip)

    peer_outs, peer_lses, parts_from_peer = [], [], []
    query = query_peer
    for start in (0, half):
        out, lse, part = attention_forward(
            info, start, half, True, query, keys, values, *marks, w_out, jnp.bfloat16
        )
        peer_outs.append(out)
        peer_lses.append(lse)
        parts_from_peer.append(swap(part))
        query, _ = tie(query_peer, part)
    query, _, grad_peer = tie(query_own, part, grad_peer)
    own_out, own_lse, own_part = attention_forward(
        info, 0, own_rows, False, query, keys, values, *marks, w_out, jnp.float32
    )
    middles, normed_twos, normed_twos_peer = [], [], []
    for side, start in enumerate((0, half)):
        arrived = parts_from_peer[side]
        if side > 0:
            arrived, _ = tie(arrived, normed_two)
        middle, normed_two = second_norm(start, inputs, own_part, arrived, gain_two)
        middles.append(middle)
        normed_twos.append(normed_two)
        normed_twos_peer.append(swap(normed_two))
    own_hidden, own_pre, own_two, own_branch = feed(normed_twos, 0, grad_out, w_up, w_down, jnp.float32)
    last = own_two
    peer_hiddens, peer_pres, peer_branches, twos_from_peer = [], [], [], []
    for side, start in enumerate((0, half)):
        normed_two, _ = tie(normed_twos_peer[side], last)
        hidden, pre, two, branch = feed([normed_two], start, grad_peer, w_up, w_down, jnp.bfloat16)
        peer_hiddens.append(hidden)
        peer_pres.append(pre)
        peer_branches.append(branch)
        twos_from_peer.append(swap(two))
        last = two
    chains = {}
    token = peer_branches[1]
    seeds = None
    backs, branches_peer, grad_qs_own, grad_qs_peer, nears, fars = [], [], [], [], [], []
    heads = rel_table.shape[0]
    got = {}

    def late(value):
        return tie(value, token)[0]

    def halves(name):
        return chains[name].part, chains[name].coming

    for event in ORDER:
        side = 1 if event.endswith("b") else 0
        start = side * half
        if event in ("D0", "U0", "P0", "V0"):
            continue
        if event == "FG":
            payloads = feed_grads(
                pay_places,
                pieces,
                (own_hidden, *peer_hiddens),
                (own_pre, *peer_pres),
                (*normed_twos, *normed_twos_peer),
                (late(grad_out), grad_peer),
            )
            for number, name in enumerate("DU"):
                chains[name] = Reduction(payloads[2 * number : 2 * number + 2], *orders[name], count)
            token = payloads[0]
        elif event[0] in chains and event[1].isdigit():
            chain = chains[event[0]]
            if chain.level < chain.steps:
                chain.after(token)
                token = chain.advance(3450000000 if "P" in chains else 0)
        elif event in ("LNa", "LNb"):
            back = second_norm_back(
                start, own_two, late(twos_from_peer[side]), middles[side], grad_out, gain_two, w_out
            )
            backs.append(back)
            branches_peer.append(swap(back[1]))
            token = back[2]
        elif event in ("B1a", "B1b"):
            result = attention_backward(
                info,
                start,
                False,
                query_own,
                late(backs[side][2]),
                own_out,
                own_lse,
                keys,
                values,
                *marks,
                seeds,
                jnp.float32,
            )
            grad_qs_own.append(result[0])
        elif event in ("B2a", "B2b"):
            result = attention_backward(
                info,
                start,
                True,
                query_peer,
                nt(late(branches_peer[side]), w_out).astype(jnp.bfloat16),
                peer_outs[side],
                peer_lses[side],
                keys,
                values,
                *marks,
                seeds,
                jnp.bfloat16 if side else jnp.float32,
            )
            grad_qs_peer.append(result[0])
        elif event == "AG":
            payloads = attention_grads(
                pay_places,
                pieces,
                (normed_own, normed_peer),
                (*grad_qs_own, grad_qs_peer[0], late(grad_qs_peer[1])),
                *seeds,
                (own_out, *peer_outs),
                (backs[0][1], backs[1][1], *branches_peer),
            )
            for number, name in enumerate("PV"):
                chains[name] = Reduction(payloads[2 * number : 2 * number + 2], *orders[name], count)
            token = payloads[0]
        elif event == "NG":
            token = normed_grad((grad_qs_peer[0], late(grad_qs_peer[1])), *seeds, own_rows, weights)
            one_from_peer = swap(token)
        elif event == "E5":
            arrived = swap(jnp.concatenate([late(peer_branches[0]), peer_branches[1]], axis=0))
        elif event == "bands":
            token = bands = band_sums([late(nears[0]), *nears[1:]], fars)
        elif event == "LN1":
            input_grad, token = first_norm_back(
                grad_qs_own,
                *seeds,
                weights,
                late(one_from_peer),
                inputs,
                (backs[0][0], backs[1][0]),
                gain_one,
            )
            gain_one_part = token
        elif event == "s0":
            token = small = pack_small(late(gain_one_part), [backs[0][3], backs[1][3]], bands, heads)
            other, reach = swap(small), 2
        elif event in ("s1", "s2", "s3", "s4", "fin"):
            token = small = add_small(small, late(other), reach)
            reach = 8
            bit = {"s1": 1, "s2": 2, "s3": 4, "s4": 8, "fin": 0}[event]
            other = dp_swap(small, bit, count) if 0 < bit < count else jnp.zeros_like(small)
        elif event == "out":
            token = out = finish(middles, own_branch, late(arrived))
        elif event == "plD":
            part, coming = halves("D")
            token = down_total = place_feed(
                (part, late(coming)), got_places[0], orders["D"][0], orders["D"][2], (ff, model), pieces
            )
        elif event == "plU":
            part, coming = halves("U")
            token = up_total = place_feed(
                (part, late(coming)), got_places[1], orders["U"][0], orders["U"][2], (model, ff), pieces // 2
            )
        elif event == "plP":
            part, coming = halves("V")
            totals = place_attention(halves("P"), (part, late(coming)), got_places[2:], (orders["P"], orders["V"]))
            token = totals[0]
        if event[0] == "B" and event[1].isdigit():
            token, seeds = result[0], result[1:3]
            nears.append(result[3])
            fars.append(result[4])

    if count > 16:
        groups = [[j * 16 + i for j in range(count // 16)] for i in range(16)]
        small = lax.psum(small, "dp", axis_index_groups=groups)
    table_total = small[2 : 2 + heads, : rel_table.shape[1]]
    return (
        out,
        input_grad,
        small[0],
        small[1],
        *totals,
        up_total,
        down_total,
        table_total,
    )


def solution(mesh):
    in_specs = (
        P(("dp", "tensor"), None),
        P(("dp", "tensor"), None),
        P("dp", None),
        P(),
        P(),
        P(None, "tensor"),
        P(None, "tensor"),
        P(None, "tensor"),
        P("tensor", None),
        P(None, "tensor"),
        P("tensor", None),
        P("tensor", None),
    )
    out_specs = (
        P(("dp", "tensor"), None),
        P(("dp", "tensor"), None),
        P(),
        P(),
        P(None, "tensor"),
        P(None, "tensor"),
        P(None, "tensor"),
        P("tensor", None),
        P(None, "tensor"),
        P("tensor", None),
        P("tensor", None),
    )
    return jax.shard_map(body, mesh=mesh, in_specs=in_specs, out_specs=out_specs, check_vma=False)
```
